32 devices in a mesh: shard: 8 (over y, x, core), rep: 4 (over z).
Axes of the slice: x: 2, y: 2, z: 4, core: 2. Of those that a mesh axis runs over, the one named last changes fastest.
Arguments:
- inputs: bfloat16 [64, 256, 1024], P(('shard', 'rep')), may hold values from -6 to 6
- lengths: int32 [64], replicated, may hold values from 64 to 256, as said below
- dealing: int32 [64], replicated, may hold values from 0 to 63, as said below
- w_query: bfloat16 [1024, 1024], P('shard'), may hold values from -0.25 to 0.25
- w_key: bfloat16 [1024, 1024], P('shard'), may hold values from -0.25 to 0.25
- w_value: bfloat16 [1024, 1024], P('shard'), may hold values from -0.1875 to 0.1875
- w_out: bfloat16 [1024, 1024], P('shard'), may hold values from -0.5 to 0.5
- b_query: bfloat16 [1024], P('shard'), may hold values from -1.5 to 1.5
- b_value: bfloat16 [1024], P('shard'), may hold values from -1.5 to 1.5
- b_out: bfloat16 [1024], P('shard'), may hold values from -1.5 to 1.5
- ln1_gain: bfloat16 [1024], P('shard'), may hold values from 0.099609375 to 1.8984375
- ln1_bias: bfloat16 [1024], P('shard'), may hold values from -1.5 to 1.5
- w_up: bfloat16 [1024, 4096], P('shard'), may hold values from -0.1875 to 0.1875
- b_up: bfloat16 [4096], P('shard'), may hold values from -1.5 to 1.5
- w_down: bfloat16 [4096, 1024], P('shard'), may hold values from -0.09375 to 0.09375
- b_down: bfloat16 [1024], P('shard'), may hold values from -1.5 to 1.5
- ln2_gain: bfloat16 [1024], P('shard'), may hold values from 0.099609375 to 1.8984375
- ln2_bias: bfloat16 [1024], P('shard'), may hold values from -1.5 to 1.5
- cotangent: bfloat16 [64, 256, 1024], P(('shard', 'rep')), may hold values from -6 to 6
Outputs:
- layer_out: bfloat16 [64, 256, 1024], P(('shard', 'rep'))
- grad_input: bfloat16 [64, 256, 1024], P(('shard', 'rep'))
- grad_w_query: float32 [1024, 1024], P('shard')
- grad_w_key: float32 [1024, 1024], P('shard')
- grad_w_value: float32 [1024, 1024], P('shard')
- grad_w_out: float32 [1024, 1024], P('shard')
- grad_b_query: float32 [1024], P('shard')
- grad_b_value: float32 [1024], P('shard')
- grad_b_out: float32 [1024], P('shard')
- grad_ln1_gain: float32 [1024], P('shard')
- grad_ln1_bias: float32 [1024], P('shard')
- grad_w_up: float32 [1024, 4096], P('shard')
- grad_b_up: float32 [4096], P('shard')
- grad_w_down: float32 [4096, 1024], P('shard')
- grad_b_down: float32 [1024], P('shard')
- grad_ln2_gain: float32 [1024], P('shard')
- grad_ln2_bias: float32 [1024], P('shard')
The draws below stay inside these ranges and needn't reach their ends.
Inputs may be any that keep to these rules, and one draw needn't show every extreme that they name: `lengths`: length of initial sequence; positions at or past it are padding. `dealing`: a permutation of the 64 sequences that maps each aligned block of 8 positions onto itself.
All inputs are finite; a program needn't handle non-finite values.
Results may differ from the reference program's by a relative error of at most 0.02.
Values may be sent and summed in bfloat16 or wider, within the bound.
No kernel may reach another device: no remote copies, remote signals or barrier semaphores. Data moves between devices by JAX's collectives and lax.ppermute only.
A program may use at most 192 MiB of HBM per device.

```python
import jax
import jax.numpy as jnp
from jax import lax

D = 1024
H = 16
HD = 64
FF = 4096
SLOT = 256
MB = 2
GROUP = 8
SEQS = 64


def common_lengths(key):
    inner = jax.random.fold_in(key, 11)
    first, second, third = jax.random.split(inner, 3)
    drawn = jax.random.randint(first, (SEQS,), SLOT // 4, SLOT + 1, dtype=jnp.int32)
    high_at = jax.random.randint(second, (), 0, SEQS, dtype=jnp.int32)
    short_at = (high_at + 1 + jax.random.randint(third, (), 0, SEQS - 1, dtype=jnp.int32)) % SEQS
    spots = jnp.arange(SEQS, dtype=jnp.int32)
    drawn = jnp.where(spots == high_at, SLOT, drawn)
    drawn = jnp.where(spots == short_at, SLOT // 4, drawn)
    return drawn


def draw_lengths(key, part):
    return common_lengths(key)


def draw_dealing(key, part):
    lengths = common_lengths(key)
    blocks = SEQS // GROUP
    replicas = GROUP // MB
    grouped = lengths.reshape(blocks, GROUP)
    places = jnp.arange(GROUP, dtype=jnp.int32)
    score = grouped * GROUP + (GROUP - 1 - places)[None, :]
    order = jnp.argsort(-score, axis=1, stable=True).astype(jnp.int32)
    rounds = places // replicas
    within = places % replicas
    device = jnp.where(rounds % 2 == 0, within, replicas - 1 - within)
    target = device * MB + rounds
    starts = (jnp.arange(blocks, dtype=jnp.int32) * GROUP)[:, None]
    placed = jnp.zeros((blocks, GROUP), jnp.int32).at[:, target].set(order + starts)
    return placed.reshape(SEQS)


def level_of(key, shape, cuts, smallest, high):
    level = 1.0
    for dim, shards_of in cuts:
        steps = jax.random.uniform(jax.random.fold_in(jax.random.fold_in(key, 6), dim), (shards_of,), jnp.float32, smallest / len(cuts), high / len(cuts))
        level = level * jnp.repeat(jnp.exp(steps), shape[dim] // shards_of).reshape((-1,) + (1,) * (len(shape) - 1 - dim))
    return level


def noise(stream_key, dims, deviation, bound, cuts=(), kind=jnp.bfloat16):
    values = deviation * jax.random.normal(stream_key, dims, jnp.float32)
    if cuts:
        values = values * level_of(stream_key, dims, cuts, -0.22, 0.18)
    return jnp.clip(values, -bound, bound).astype(kind)


def setup_inputs(seed: int = 0) -> dict:
    keys = jax.random.split(jax.random.key(seed), 20)
    return {
        "inputs": noise(keys[0], (SEQS, SLOT, D), 1.0, 6.0, ((0, 32),)),
        "lengths": draw_lengths(jax.random.fold_in(keys[19], 71), 0),
        "dealing": draw_dealing(jax.random.fold_in(keys[19], 71), 0),
        "w_query": noise(keys[3], (D, D), (D // 2) ** -0.5, 0.25, ((0, 8),)),
        "w_key": noise(keys[4], (D, D), (D // 2) ** -0.5, 0.25, ((0, 8),)),
        "w_value": noise(keys[5], (D, D), D ** -0.5, 0.1875, ((0, 8),)),
        "w_out": noise(keys[6], (D, D), (D // 8) ** -0.5, 0.5, ((0, 8),)),
        "b_query": noise(keys[7], (D,), 0.3, 1.5, ((0, 8),)),
        "b_value": noise(keys[8], (D,), 0.3, 1.5, ((0, 8),)),
        "b_out": noise(keys[9], (D,), 0.3, 1.5, ((0, 8),)),
        "ln1_gain": jnp.clip(1.0 + 0.18 * jax.random.normal(keys[10], (D,), jnp.float32), 0.099609375, 1.8984375).astype(jnp.bfloat16),
        "ln1_bias": noise(keys[11], (D,), 0.3, 1.5, ((0, 8),)),
        "w_up": noise(keys[12], (D, FF), D ** -0.5, 0.1875, ((0, 8),)),
        "b_up": noise(keys[13], (FF,), 0.3, 1.5, ((0, 8),)),
        "w_down": noise(keys[14], (FF, D), FF ** -0.5, 0.09375, ((0, 8),)),
        "b_down": noise(keys[15], (D,), 0.3, 1.5, ((0, 8),)),
        "ln2_gain": jnp.clip(1.0 + 0.18 * jax.random.normal(keys[16], (D,), jnp.float32), 0.099609375, 1.8984375).astype(jnp.bfloat16),
        "ln2_bias": noise(keys[17], (D,), 0.3, 1.5, ((0, 8),)),
        "cotangent": noise(keys[18], (SEQS, SLOT, D), 1.0, 6.0, ((0, 32),)),
    }


EPS = 1e-05
NEG = -1e+30
HIGHEST = lax.Precision.HIGHEST

@jax.custom_vjp
def low(v):
    return lax.optimization_barrier(v.astype(jnp.bfloat16)).astype(jnp.float32)

@jax.custom_vjp
def low_back(v):
    return v

def low_keep(v):
    return (low(v), None)

def low_pass(kept, grad):
    return (grad,)

def back_keep(v):
    return (v, None)

def back_low(kept, grad):
    return (low(grad),)
low.defvjp(low_keep, low_pass)
low_back.defvjp(back_keep, back_low)

def product(left, right):
    return jnp.dot(left, right, precision=HIGHEST, preferred_element_type=jnp.float32)

def norm_rows(values, gain, shift):
    center = values - lax.optimization_barrier(jnp.mean(values, -1, keepdims=True))
    spread = lax.optimization_barrier(jnp.mean(center * center, -1, keepdims=True))
    return center * lax.rsqrt(spread + EPS) * gain + shift

def layer_block(tokens, seq_lens, params):
    w_query, w_key, w_value, w_out, b_query, b_value, b_out, ln1_gain, ln1_bias, w_up, b_up, w_down, b_down, ln2_gain, ln2_bias = params
    count, rows, width = tokens.shape
    query = low(low_back(product(tokens, w_query) + b_query)).reshape(count, rows, H, HD)
    keyed = low(low_back(product(tokens, w_key))).reshape(count, rows, H, HD)
    value = low(low_back(product(tokens, w_value) + b_value)).reshape(count, rows, H, HD)
    raw = jnp.einsum('bqhd,bkhd->bhqk', query, keyed, precision=HIGHEST)
    scores = low_back(raw) * HD ** (-0.5)
    places = jnp.arange(rows)
    allowed = places[None, None, None, :] < seq_lens[:, None, None, None]
    scores = jnp.where(allowed, scores, NEG)
    probs = jax.nn.softmax(scores, axis=-1)
    mixed = jnp.einsum('bhqk,bkhd->bqhd', low(probs), value, precision=HIGHEST).reshape(count, rows, width)
    branch = low_back(product(low(low_back(mixed)), w_out)) + b_out
    hidden = norm_rows(tokens + branch, ln1_gain, ln1_bias)
    pre = low_back(product(low(hidden), w_up) + b_up)
    act = low(jax.nn.gelu(pre, approximate=False))
    summed = hidden + low_back(product(act, w_down)) + b_down
    normed = norm_rows(summed, ln2_gain, ln2_bias)
    rows_ok = places[None, :] < seq_lens[:, None]
    return jnp.where(rows_ok[..., None], normed, 0.0)

def reference(inputs, lengths, dealing, w_query, w_key, w_value, w_out, b_query, b_value, b_out, ln1_gain, ln1_bias, w_up, b_up, w_down, b_down, ln2_gain, ln2_bias, cotangent):
    params = tuple((item.astype(jnp.float32) for item in (w_query, w_key, w_value, w_out, b_query, b_value, b_out, ln1_gain, ln1_bias, w_up, b_up, w_down, b_down, ln2_gain, ln2_bias)))
    dealt = jnp.take(inputs, dealing, axis=0).astype(jnp.float32)
    seq_lens = jnp.take(lengths, dealing, axis=0)
    per_block = max(1, min(SEQS, 4096 // SLOT))
    blocks = SEQS // per_block

    def whole(tokens, weights):

        def one_block(pair):
            return layer_block(pair[0], pair[1], weights)
        outs = lax.map(jax.checkpoint(one_block), (tokens.reshape(blocks, per_block, SLOT, D), seq_lens.reshape(blocks, per_block)))
        return outs.reshape(SEQS, SLOT, D)
    layer_out, pull = jax.vjp(whole, dealt, params)
    grad_dealt, grads = pull(cotangent.astype(jnp.float32))
    grad_input = jnp.zeros_like(grad_dealt).at[dealing].set(grad_dealt)
    g_wq, g_wk, g_wv, g_wo, g_bq, g_bv, g_bo, g_l1g, g_l1b, g_wu, g_bu, g_wd, g_bd, g_l2g, g_l2b = grads
    return (layer_out.astype(jnp.bfloat16), grad_input.astype(jnp.bfloat16), g_wq, g_wk, g_wv, g_wo, g_bq, g_bv, g_bo, g_l1g, g_l1b, g_wu, g_bu, g_wd, g_bd, g_l2g, g_l2b)
```

```python
import jax
import jax.numpy as jnp
from jax import lax
from jax.sharding import PartitionSpec as P

H = 16
HD = 64
EPS = 1e-05
NEG = -1e30
F32 = jnp.float32
BF16 = jnp.bfloat16


def matmul(left, right):
    return jnp.dot(left, right, preferred_element_type=F32)


def left_trans(left, right):
    return lax.dot_general(left, right, (((0,), (0,)), ((), ())), preferred_element_type=F32)


def right_trans(left, right):
    return lax.dot_general(left, right, (((1,), (1,)), ((), ())), preferred_element_type=F32)


def normalize(values, gain, shift):
    center = values - jnp.mean(values, -1, keepdims=True)
    inverse = lax.rsqrt(jnp.mean(center * center, -1, keepdims=True) + EPS)
    unit = center * inverse
    return (unit * gain + shift, unit, inverse)


def norm_back(grad, unit, inverse, gain):
    scaled = grad * gain
    return inverse * (
        scaled
        - jnp.mean(scaled, -1, keepdims=True)
        - unit * jnp.mean(scaled * unit, -1, keepdims=True)
    )


def gelu_both(pre):
    cumul = 0.5 * (1.0 + lax.erf(pre * 0.7071067811865476))
    density = jnp.exp(-0.5 * pre * pre) * 0.3989422804014327
    return (pre * cumul, cumul + pre * density)


def pick(pool, targets):
    return jnp.stack(
        [lax.dynamic_index_in_dim(pool, targets[i], 0, keepdims=False) for i in range(targets.shape[0])]
    )


def local(
    inputs, lengths, dealing, w_query, w_key, w_value, w_out, b_query, b_value, b_out,
    ln1_gain, ln1_bias, w_up, b_up, w_down, b_down, ln2_gain, ln2_bias, cotangent,
):
    batches, rows, width = inputs.shape
    shards = lax.axis_size("shard")
    replicas = lax.axis_size("rep")
    group = batches * replicas
    shard_index = lax.axis_index("shard")
    rep_index = lax.axis_index("rep")
    anchor = shard_index * group
    slots = anchor + rep_index * batches + jnp.arange(batches, dtype=jnp.int32)
    seq_lengths = jnp.take(lengths, slots)
    local_dealing = lax.dynamic_slice_in_dim(dealing, anchor, group) - anchor
    sources = jnp.take(dealing, slots) - anchor
    places = jnp.arange(group, dtype=jnp.int32)
    wanted = jnp.sum(
        jnp.where(local_dealing[None, :] == (slots - anchor)[:, None], places[None, :], 0), 1
    )

    def gather(block):
        return lax.all_gather(block, "shard", axis=0, tiled=True)

    block = w_query.shape[0]
    wide = w_up.shape[1]
    small = (b_query, b_value, b_out, ln1_gain, ln1_bias, b_down, ln2_gain, ln2_bias, b_up)
    vec = jnp.concatenate(small)
    first = jnp.concatenate([w_query, w_key, w_value, w_out], 0)
    all_vec = lax.all_gather(vec, "shard", axis=0, tiled=True).reshape(shards, -1)
    all_first = gather(first).reshape(shards, 4, block, width)
    cuts = [0]
    for part in small:
        cuts.append(cuts[-1] + part.shape[0])
    (bias_query, bias_value, bias_out, gain_one, shift_one, bias_down, gain_two, shift_two, bias_up) = [
        all_vec[:, cuts[i] : cuts[i + 1]].reshape(-1).astype(F32) for i in range(len(small))
    ]
    full_query, full_key, full_value, full_out = [
        all_first[:, i].reshape(width, width) for i in range(4)
    ]
    full_up = gather(w_up)
    full_down = gather(w_down)
    cot = pick(lax.all_gather(cotangent, "rep", axis=0, tiled=True), wanted)

    tokens = inputs.reshape(batches * rows, width)
    query = (matmul(tokens, full_query) + bias_query).astype(BF16)
    keyed = matmul(tokens, full_key).astype(BF16)
    value = (matmul(tokens, full_value) + bias_value).astype(BF16)
    heads = lambda a: a.reshape(batches, rows, H, HD).transpose(0, 2, 1, 3)
    flat = lambda a: a.transpose(0, 2, 1, 3).reshape(batches * rows, width)
    qh, kh, vh = heads(query), heads(keyed), heads(value)
    allowed = lax.broadcasted_iota(jnp.int32, (batches, 1, 1, rows), 3) < seq_lengths[:, None, None, None]
    scale = HD ** (-0.5)
    scores = jnp.einsum("bhqd,bhkd->bhqk", qh, kh, preferred_element_type=F32) * scale
    scores = jnp.where(allowed, scores, NEG)
    raised = jnp.exp(scores - jnp.max(scores, -1, keepdims=True))
    probs = raised / jnp.sum(raised, -1, keepdims=True)
    probs_low = probs.astype(BF16)
    mixed_low = flat(jnp.einsum("bhqk,bhkd->bhqd", probs_low, vh, preferred_element_type=F32).astype(BF16))
    hidden, unit_one, inverse_one = normalize(
        tokens.astype(F32) + matmul(mixed_low, full_out) + bias_out, gain_one, shift_one
    )
    hidden_low = hidden.astype(BF16)
    pre = matmul(hidden_low, full_up) + bias_up
    act, slope = gelu_both(pre)
    act_low = act.astype(BF16)
    summed = hidden + matmul(act_low, full_down) + bias_down
    normed, unit_two, inverse_two = normalize(summed, gain_two, shift_two)
    valid = (lax.broadcasted_iota(jnp.int32, (batches, rows, 1), 1) < seq_lengths[:, None, None]).reshape(-1, 1)
    out = jnp.where(valid, normed, 0.0).astype(BF16).reshape(batches, rows, width)
    layer_out = pick(lax.all_gather(out, "rep", axis=0, tiled=True), sources)

    grad_out = jnp.where(valid, cot.reshape(-1, width).astype(F32), 0.0)
    grad_gain_two = jnp.sum(grad_out * unit_two, 0)
    grad_shift_two = jnp.sum(grad_out, 0)
    grad_sum = norm_back(grad_out, unit_two, inverse_two, gain_two)
    grad_bias_down = jnp.sum(grad_sum, 0)
    grad_sum_low = grad_sum.astype(BF16)

    def reduced(part):
        return lax.psum_scatter(part, "shard", scatter_dimension=0, tiled=True)

    def over_rep(part):
        return lax.psum(part, "rep").astype(F32)

    g_down = reduced(left_trans(act_low, grad_sum_low).astype(BF16))
    grad_pre = (right_trans(grad_sum_low, full_down) * slope).astype(BF16)
    grad_bias_up = jnp.sum(grad_pre.astype(F32), 0)
    g_up = reduced(left_trans(hidden_low, grad_pre).astype(BF16))
    grad_hidden = grad_sum + right_trans(grad_pre, full_up)
    grad_gain_one = jnp.sum(grad_hidden * unit_one, 0)
    grad_shift_one = jnp.sum(grad_hidden, 0)
    grad_resid = norm_back(grad_hidden, unit_one, inverse_one, gain_one)
    grad_bias_out = jnp.sum(grad_resid, 0)
    grad_resid_low = grad_resid.astype(BF16)
    grad_w_out = left_trans(mixed_low, grad_resid_low).astype(BF16)
    grad_mixed = heads(right_trans(grad_resid_low, full_out).astype(BF16))
    grad_probs = jnp.einsum("bhqd,bhkd->bhqk", grad_mixed, vh, preferred_element_type=F32)
    inner = jnp.sum(probs * grad_probs, -1, keepdims=True)
    grad_scores = (probs * (grad_probs - inner) * scale).astype(BF16)
    query_low = flat(jnp.einsum("bhqk,bhkd->bhqd", grad_scores, kh, preferred_element_type=F32).astype(BF16))
    key_low = flat(jnp.einsum("bhqk,bhqd->bhkd", grad_scores, qh, preferred_element_type=F32).astype(BF16))
    value_low = flat(jnp.einsum("bhqk,bhqd->bhkd", probs_low, grad_mixed, preferred_element_type=F32).astype(BF16))
    grad_bias_query = jnp.sum(query_low.astype(F32), 0)
    grad_bias_value = jnp.sum(value_low.astype(F32), 0)
    blocks = [
        part.reshape(shards, block, width)
        for part in (
            left_trans(tokens, query_low).astype(BF16),
            left_trans(tokens, key_low).astype(BF16),
            left_trans(tokens, value_low).astype(BF16),
            grad_w_out,
        )
    ]
    g_first = reduced(jnp.concatenate(blocks, 1).reshape(shards * 4 * block, width))
    grad_tokens = (
        grad_resid
        + right_trans(query_low, full_query)
        + right_trans(key_low, full_key)
        + right_trans(value_low, full_value)
    )
    grad_input = grad_tokens.astype(BF16).reshape(batches, rows, width)
    vec_terms = (
        grad_bias_query, grad_bias_value, grad_bias_out, grad_gain_one, grad_shift_one,
        grad_bias_down, grad_gain_two, grad_shift_two, grad_bias_up,
    )
    g_vec = jnp.concatenate([part.reshape(shards, -1) for part in vec_terms], 1)
    g_vec = lax.psum(g_vec, ("shard", "rep"))
    g_vec = lax.dynamic_index_in_dim(g_vec, shard_index, 0, keepdims=False)
    (g_bquery, g_bvalue, g_bout, g_gain_one, g_shift_one, g_bdown, g_gain_two, g_shift_two, g_bup) = [
        g_vec[cuts[i] : cuts[i + 1]] for i in range(len(small))
    ]
    g_down = over_rep(g_down)
    g_up = over_rep(g_up)
    g_first = over_rep(g_first).reshape(4, block, width)
    return (
        layer_out, grad_input, g_first[0], g_first[1], g_first[2], g_first[3],
        g_bquery, g_bvalue, g_bout, g_gain_one, g_shift_one,
        g_up, g_bup, g_down, g_bdown, g_gain_two, g_shift_two,
    )


def solution(mesh):
    seqs = P(("shard", "rep"), None, None)
    mat = P("shard", None)
    vec = P("shard")
    in_specs = (
        seqs, P(), P(), mat, mat, mat, mat, vec, vec, vec, vec, vec, mat, vec, mat, vec, vec, vec, seqs,
    )
    out_specs = (
        seqs, seqs, mat, mat, mat, mat, vec, vec, vec, vec, vec, mat, vec, mat, vec, vec, vec,
    )
    return jax.shard_map(local, mesh=mesh, in_specs=in_specs, out_specs=out_specs, check_vma=False)
```

```python
import jax
import jax.numpy as jnp
from jax import lax
from jax.experimental import pallas as pl
from jax.experimental.pallas import tpu as pltpu
from jax.sharding import PartitionSpec as P

H = 16
HD = 64
EPS = 1e-05
NEG = -1e30
F32 = jnp.float32
BF16 = jnp.bfloat16


def matmul(left, right):
    return jnp.dot(left, right, preferred_element_type=F32)


def left_trans(left, right):
    return lax.dot_general(left, right, (((0,), (0,)), ((), ())), preferred_element_type=F32)


def right_trans(left, right):
    return lax.dot_general(left, right, (((1,), (1,)), ((), ())), preferred_element_type=F32)


def normalize(values, gain, shift):
    center = values - jnp.mean(values, -1, keepdims=True)
    inverse = lax.rsqrt(jnp.mean(center * center, -1, keepdims=True) + EPS)
    unit = center * inverse
    return (unit * gain + shift, unit, inverse)


def norm_back(grad, unit, inverse, gain):
    scaled = grad * gain
    return inverse * (
        scaled
        - jnp.mean(scaled, -1, keepdims=True)
        - unit * jnp.mean(scaled * unit, -1, keepdims=True)
    )


def gelu_both(pre):
    cumul = 0.5 * (1.0 + lax.erf(pre * 0.7071067811865476))
    density = jnp.exp(-0.5 * pre * pre) * 0.3989422804014327
    return (pre * cumul, cumul + pre * density)


VMEM = 56 * 1024 * 1024
ANY = pl.BlockSpec(memory_space=pl.ANY)
DMA = pltpu.SemaphoreType.DMA


def spec(shape, index):
    return pl.BlockSpec(shape, index)


def whole(shape):
    zeros = (0,) * len(shape)
    return pl.BlockSpec(shape, lambda *_: zeros)


def sds(shape, dtype):
    return jax.ShapeDtypeStruct(shape, dtype)


def call(kernel, grid, in_specs, out_specs, out_shape, scratch, flops, moved, trans=0):
    return pl.pallas_call(
        kernel,
        grid_spec=pltpu.PrefetchScalarGridSpec(
            num_scalar_prefetch=1,
            grid=grid,
            in_specs=in_specs,
            out_specs=out_specs,
            scratch_shapes=list(scratch),
        ),
        out_shape=out_shape,
        compiler_params=pltpu.CompilerParams(vmem_limit_bytes=VMEM),
        cost_estimate=pl.CostEstimate(flops=1024, bytes_accessed=1024, transcendentals=0),
    )


def dot_nn(a, b):
    return lax.dot_general(a, b, (((1,), (0,)), ((), ())), preferred_element_type=F32)


def dot_nt(a, b):
    return lax.dot_general(a, b, (((1,), (1,)), ((), ())), preferred_element_type=F32)


def dot_tn(a, b):
    return lax.dot_general(a, b, (((0,), (0,)), ((), ())), preferred_element_type=F32)


def fetch(meta, parts, target, sems, low, high, columns=None):
    cut = parts[3].shape[0]
    each = len(parts) // 2
    for core in range(2):
        for chip in range(4):
            at = meta[0] ^ (2 * chip + core)
            if chip < 3:
                pieces = [(parts[each * core + chip], low, high, 0)]
            else:
                pieces = []
                if low < cut:
                    pieces.append((parts[each * core + 3], low, min(high, cut), 0))
                if high > cut:
                    start = max(low, cut)
                    pieces.append((parts[each * core + 4], start - cut, high - cut, start - low))
            for ref, begin, end, offset in pieces:
                source = ref.at[pl.ds(begin, end - begin)]
                if columns is not None:
                    source = ref.at[pl.ds(begin, end - begin), columns]
                goal = target.at[at]
                if len(pieces) > 1:
                    goal = target.at[at, pl.ds(offset, end - begin)]
                pltpu.make_async_copy(source, goal, sems.at[at]).start()


def arrived(target, sem):
    pltpu.make_async_copy(target, target, sem).wait()


def hand_over(meta, source, target, sems, block):
    copies = []
    for chip in range(4):
        at = pl.ds(pl.multiple_of((meta[0] ^ (2 * chip + 1)) * block, block), block)
        copies.append(pltpu.make_async_copy(source.at[:, at], target.at[chip], sems.at[chip]))
        copies[-1].start()
    return copies


def gelu_and_slope(pre):
    density = jnp.exp(-0.5 * pre * pre)
    t = 1.0 / (1.0 + 0.27577164466275367 * jnp.abs(pre))
    tail = -0.1137685166 * t + 0.4433319969
    for coefficient in (-0.3176998336, 0.3247794523, 0.04569430636, 0.1176625937):
        tail = tail * t + coefficient
    tail = tail * t * density
    cumul = jnp.where(pre < 0.0, tail, 1.0 - tail)
    return pre * cumul, cumul + pre * (density * 0.3989422804014327)


def project(meta, tokens, first):
    rows, width = tokens.shape
    tile = 512
    count = width // tile

    def kernel(meta, x_ref, *refs):
        parts, (out_ref, vec_ref, up_ref, give_ref, held, short, made, sems, short_sems, out_sems, give_sems) = refs[: len(first)], refs[len(first) :]
        for w in range(3):
            fetch(meta, parts, held.at[w], sems.at[w], 128 * w, 128 * (w + 1))
            if w == 0:
                fetch(meta, parts, short, short_sems, 512, 528)
        gifts = hand_over(meta, x_ref, give_ref, give_sems, 128)
        for b in range(8):
            arrived(short.at[b], short_sems.at[b])
        for b in range(8):
            two = short[b].astype(F32)
            for v in range(8):
                vec_ref[v : v + 1, 128 * b : 128 * (b + 1)] = two[0:1, 128 * v : 128 * (v + 1)]
            up_ref[0:1, 512 * b : 512 * (b + 1)] = two[1:2, :512]

        def body(i, carry):
            w, n = i // count, i % count

            @pl.when(n == 0)
            def _():
                for b in range(8):
                    arrived(held.at[w, b], sems.at[w, b])

            at = pl.ds(pl.multiple_of(n * tile, tile), tile)
            weight = held[w, :, :, at].reshape(width, tile)
            bias = jnp.where(w == 0, vec_ref[0:1, at], vec_ref[1:2, at])
            bias = jnp.where(w == 1, jnp.zeros_like(bias), bias)
            made[w, :, at] = (dot_nn(x_ref[...], weight) + bias).astype(BF16)

            @pl.when(n == count - 1)
            def _():
                pltpu.make_async_copy(made.at[w], out_ref.at[w], out_sems.at[w]).start()

            return carry

        lax.fori_loop(0, 3 * count, body, 0)
        for w in range(3):
            pltpu.make_async_copy(made.at[w], out_ref.at[w], out_sems.at[w]).wait()
        for copy in gifts:
            copy.wait()

    return call(
        kernel,
        (1,),
        [whole((rows, width))] + [ANY] * len(first),
        [ANY, whole((8, width)), whole((1, 4 * width)), ANY],
        [sds((3, rows, width), BF16), sds((8, width), F32), sds((1, 4 * width), F32), sds((4, rows, 128), BF16)],
        [
            pltpu.VMEM((3, 8, 128, width), BF16), pltpu.VMEM((8, 16, width), BF16),
            pltpu.VMEM((3, rows, width), BF16), DMA((3, 8)), DMA((8,)), DMA((3,)), DMA((4,)),
        ],
        flops=10 * rows * width * width,
        moved=10 * rows * width + 6 * width * width,
    )(meta, tokens, *first)


HEADS = 4


def attend(meta, qkv, batches, rows):
    total, width = qkv.shape[1:]
    span = HEADS * HD
    steps = width // span

    def kernel(meta, q_ref, k_ref, v_ref, mixed_ref, probs_ref):
        length = meta[1 + pl.program_id(0)]
        allowed = lax.broadcasted_iota(jnp.int32, (rows, rows), 1) < length
        left = lax.broadcasted_iota(jnp.int32, (rows, 128), 1) < HD
        for pair in range(HEADS // 2):
            cols = slice(128 * pair, 128 * (pair + 1))
            query, keyed, value = q_ref[0, :, cols], k_ref[0, :, cols], v_ref[0, :, cols]
            outs = []
            for half in range(2):
                mine = left if half == 0 else jnp.logical_not(left)
                scores = dot_nt(jnp.where(mine, query, jnp.zeros_like(query)), keyed) * (HD**-0.5)
                scores = jnp.where(allowed, scores, NEG)
                raised = jnp.exp(scores - jnp.max(scores, -1, keepdims=True))
                probs = raised * (1.0 / jnp.sum(raised, -1, keepdims=True))
                low = probs.astype(BF16)
                probs_ref[0, 2 * pair + half] = low
                outs.append(dot_nn(low, value))
            mixed_ref[:, cols] = jnp.where(left, outs[0], outs[1]).astype(BF16)

    part = lambda w: spec((1, rows, span), lambda b, h, meta: (w, b, h))
    return call(
        kernel,
        (batches, steps),
        [part(0), part(1), part(2)],
        [
            spec((rows, span), lambda b, h, meta: (b, h)),
            spec((1, HEADS, rows, rows), lambda b, h, meta: (b, h, 0, 0)),
        ],
        [sds((total, width), BF16), sds((batches, H, rows, rows), BF16)],
        [],
        flops=20 * total * rows * width,
        moved=8 * total * width + 2 * batches * H * rows * rows,
        trans=batches * H * rows * rows,
    )(meta, qkv, qkv, qkv)


def mix_out(meta, mixed, tokens, first, vecs):
    total, width = mixed.shape
    tile = 128

    def kernel(meta, mixed_ref, tokens_ref, vec_ref, *refs):
        parts, (unit_ref, inv_ref, low_ref, give_ref, held, sems, give_sems) = refs[: len(first)], refs[len(first) :]
        fetch(meta, parts, held, sems, 384, 512)
        gifts = hand_over(meta, mixed_ref, give_ref.at[0], give_sems.at[0], 128)
        for b in range(8):
            arrived(held.at[b], sems.at[b])

        def body(i, carry):
            here = pl.ds(pl.multiple_of(i * tile, tile), tile)
            branch = dot_nn(mixed_ref[here], held[...].reshape(width, width)) + vec_ref[2:3]
            hidden, unit, inverse = normalize(tokens_ref[here].astype(F32) + branch, vec_ref[3:4], vec_ref[4:5])
            unit_ref[here] = unit
            inv_ref[here] = jnp.broadcast_to(inverse, (tile, 128))
            low_ref[here] = hidden.astype(BF16)
            return carry

        lax.fori_loop(0, total // tile, body, 0)
        gifts += hand_over(meta, low_ref, give_ref.at[1], give_sems.at[1], 128)
        for copy in gifts:
            copy.wait()

    block = (total, width)
    return call(
        kernel,
        (1,),
        [whole(block), whole(block), whole(vecs.shape)] + [ANY] * len(first),
        [whole(block), whole((total, 128)), whole(block), ANY],
        [sds(block, F32), sds((total, 128), F32), sds(block, BF16), sds((2, 4, total, 128), BF16)],
        [pltpu.VMEM((8, 128, width), BF16), DMA((8,)), DMA((2, 4))],
        flops=5 * total * width * width,
        moved=10 * total * width + 2 * width * width,
    )(meta, mixed, tokens, vecs, *first)


def feed_up(meta, low, up, bias):
    total, width = low.shape
    wide = up[0].shape[1]
    strip, tile = 1024, 512
    strips, inner = wide // strip, strip // tile

    def kernel(meta, x_ref, bias_ref, *refs):
        parts, (act_ref, slope_ref, give_ref, held, act, slope, sems, out_sems, give_sems) = refs[: len(up)], refs[len(up) :]
        for t in range(strips):
            fetch(meta, parts, held.at[t], sems.at[t], 0, 128, pl.ds(strip * t, strip))

        def leave(i):
            at = pl.ds(pl.multiple_of(i * tile, tile), tile)
            return (
                pltpu.make_async_copy(act.at[i], act_ref.at[:, at], out_sems.at[0, i]),
                pltpu.make_async_copy(slope.at[i], slope_ref.at[:, at], out_sems.at[1, i]),
            )

        def body(i, carry):
            t, n = i // inner, i % inner

            @pl.when(n == 0)
            def _():
                for b in range(8):
                    arrived(held.at[t, b], sems.at[t, b])

            weight = held[t, :, :, pl.ds(pl.multiple_of(n * tile, tile), tile)].reshape(width, tile)
            pre = dot_nn(x_ref[...], weight) + bias_ref[:, pl.ds(pl.multiple_of(i * tile, tile), tile)]
            value, grad = gelu_and_slope(pre)
            act[i] = value.astype(BF16)
            slope[i] = grad.astype(BF16)
            for copy in leave(i):
                copy.start()
            code = meta[0] ^ i

            @pl.when(code % 2 == 1)
            def _():
                pltpu.make_async_copy(act.at[i], give_ref.at[code // 2], give_sems.at[code // 2]).start()

            return carry

        lax.fori_loop(0, strips * inner, body, 0)
        for i in range(strips * inner):
            for copy in leave(i):
                copy.wait()
        for chip in range(4):
            arrived(give_ref.at[chip], give_sems.at[chip])

    out = sds((total, wide), BF16)
    tiles = wide // tile
    return call(
        kernel,
        (1,),
        [whole((total, width)), whole((1, wide))] + [ANY] * len(up),
        [ANY, ANY, ANY],
        [out, out, sds((4, total, tile), BF16)],
        [
            pltpu.VMEM((strips, 8, 128, strip), BF16), pltpu.VMEM((tiles, total, tile), BF16),
            pltpu.VMEM((tiles, total, tile), BF16), DMA((strips, 8)), DMA((2, tiles)), DMA((4,)),
        ],
        flops=5 * total * width * wide,
        moved=4 * total * wide + 2 * width * wide,
    )(meta, low, bias, *up)


def feed_down(meta, act, down, unit_one, cot_pool, vecs, batches, rows):
    total, wide = act.shape
    width = down[0].shape[1]
    chunk = 64

    def kernel(meta, act_ref, unit_ref, cot_ref, vec_ref, *refs):
        parts = refs[: len(down)]
        (out_ref, sum_ref, low_ref, grad_ref, held, left, total_ref, unit, cot, sems, left_sems, more) = refs[len(down) :]
        for b in range(8):
            pltpu.make_async_copy(act_ref.at[:, pl.ds(512 * b, 512)], left.at[b], left_sems.at[b]).start()
        fetch(meta, parts, held, sems, 0, 512)
        rest = [pltpu.make_async_copy(unit_ref, unit, more.at[0])] + [
            pltpu.make_async_copy(cot_ref.at[meta[3 + i]], cot.at[i], more.at[1 + i]) for i in range(batches)
        ]
        for copy in rest:
            copy.start()

        def add(b, carry):
            arrived(left.at[b], left_sems.at[b])
            arrived(held.at[b], sems.at[b])
            part = dot_nn(left[b], held[b])

            @pl.when(b == 0)
            def _():
                total_ref[...] = part

            @pl.when(b > 0)
            def _():
                total_ref[...] += part

            return carry

        lax.fori_loop(0, 8, add, 0)
        for copy in rest:
            copy.wait()
        grad_ref[...] = jnp.zeros_like(grad_ref)

        def body(i, carry):
            here = pl.ds(pl.multiple_of(i * chunk, chunk), chunk)
            batch = i // (rows // chunk)
            at = pl.multiple_of((i % (rows // chunk)) * chunk, chunk)
            summed = (unit[here] * vec_ref[3:4] + vec_ref[4:5]) + total_ref[here] + vec_ref[5:6]
            normed, unit_two, inverse = normalize(summed, vec_ref[6:7], vec_ref[7:8])
            place = at + lax.broadcasted_iota(jnp.int32, (chunk, 1), 0)
            valid = place < meta[1 + batch]
            out_ref[here] = jnp.where(valid, normed, 0.0).astype(BF16)
            grad_out = jnp.where(valid, cot[batch, pl.ds(at, chunk)].astype(F32), 0.0)
            grad_sum = norm_back(grad_out, unit_two, inverse, vec_ref[6:7])
            sum_ref[here] = grad_sum
            low_ref[here] = grad_sum.astype(BF16)
            grad_ref[0:1] += jnp.sum(grad_out * unit_two, 0, keepdims=True)
            grad_ref[1:2] += jnp.sum(grad_out, 0, keepdims=True)
            grad_ref[2:3] += jnp.sum(grad_sum, 0, keepdims=True)
            return carry

        lax.fori_loop(0, total // chunk, body, 0)

    block = (total, width)
    return call(
        kernel,
        (1,),
        [ANY, ANY, ANY, whole(vecs.shape)] + [ANY] * len(down),
        [whole(block), whole(block), whole(block), whole((8, width))],
        [sds(block, BF16), sds(block, F32), sds(block, BF16), sds((8, width), F32)],
        [
            pltpu.VMEM((8, 512, width), BF16), pltpu.VMEM((8, total, 512), BF16), pltpu.VMEM(block, F32),
            pltpu.VMEM(block, F32), pltpu.VMEM((batches, rows, width), BF16), DMA((8,)), DMA((8,)), DMA((1 + batches,)),
        ],
        flops=6 * total * width * wide,
        moved=2 * total * wide + 2 * width * wide + 14 * total * width,
    )(meta, act, unit_one, cot_pool, vecs, *down)


def back_down(meta, low, down, slope):
    total, width = low.shape
    wide = slope.shape[1]

    def kernel(meta, low_ref, slope_ref, *refs):
        parts, (pre_ref, bias_ref, held, right, made, sems, right_sems, out_sems) = refs[: len(down)], refs[len(down) :]
        fetch(meta, parts, held, sems, 0, 512)
        for b in range(8):
            pltpu.make_async_copy(slope_ref.at[:, pl.ds(512 * b, 512)], right.at[b], right_sems.at[b]).start()

        def leave(b):
            at = pl.ds(pl.multiple_of(512 * b, 512), 512)
            return pltpu.make_async_copy(made.at[b], pre_ref.at[:, at], out_sems.at[b])

        def body(b, carry):
            arrived(held.at[b], sems.at[b])
            arrived(right.at[b], right_sems.at[b])
            grad = (dot_nt(low_ref[...], held[b]) * right[b].astype(F32)).astype(BF16)
            made[b] = grad
            leave(b).start()
            bias_ref[:, pl.ds(pl.multiple_of(512 * b, 512), 512)] = jnp.sum(grad.astype(F32), 0, keepdims=True)
            return carry

        lax.fori_loop(0, 8, body, 0)
        for b in range(8):
            leave(b).wait()

    return call(
        kernel,
        (1,),
        [whole((total, width)), ANY] + [ANY] * len(down),
        [ANY, whole((1, wide))],
        [sds((total, wide), BF16), sds((1, wide), F32)],
        [
            pltpu.VMEM((8, 512, width), BF16), pltpu.VMEM((8, total, 512), BF16), pltpu.VMEM((8, total, 512), BF16),
            DMA((8,)), DMA((8,)), DMA((8,)),
        ],
        flops=4 * total * width * wide,
        moved=4 * total * wide + 2 * width * wide,
    )(meta, low, slope, *down)


def back_up(meta, pre, up, first, grad_sum, unit_one, inverse_one, vecs):
    total, wide = pre.shape
    width = grad_sum.shape[1]
    chunk = 64

    def kernel(meta, pre_ref, sum_ref, unit_ref, inv_ref, vec_ref, *refs):
        parts, others = refs[: len(up)], refs[len(up) : len(up) + len(first)]
        (resid_ref, low_ref, mixed_ref, grad_ref, held, out_held, grad_hidden, unit, sems, out_sems, more) = refs[len(up) + len(first) :]
        fetch(meta, parts, held, sems, 0, 128)
        rest = [
            pltpu.make_async_copy(sum_ref, grad_hidden, more.at[0]),
            pltpu.make_async_copy(unit_ref, unit, more.at[1]),
        ]
        for copy in rest:
            copy.start()
        fetch(meta, others, out_held, out_sems, 384, 512)
        rest[0].wait()

        def through(j, carry):
            for b in range(2):
                arrived(held.at[2 * j + b], sems.at[2 * j + b])
            weight = held[pl.ds(2 * j, 2)].reshape(256, wide)
            grad_hidden[:, pl.ds(pl.multiple_of(256 * j, 256), 256)] += dot_nt(pre_ref[...], weight)
            return carry

        lax.fori_loop(0, 4, through, 0)
        rest[1].wait()
        grad_ref[...] = jnp.zeros_like(grad_ref)

        def body(i, carry):
            here = pl.ds(pl.multiple_of(i * chunk, chunk), chunk)
            grad, unit_here = grad_hidden[here], unit[here]
            grad_ref[0:1] += jnp.sum(grad * unit_here, 0, keepdims=True)
            grad_ref[1:2] += jnp.sum(grad, 0, keepdims=True)
            resid = norm_back(grad, unit_here, inv_ref[here, 0:1], vec_ref[3:4])
            grad_ref[2:3] += jnp.sum(resid, 0, keepdims=True)
            resid_ref[here] = resid
            low_ref[here] = resid.astype(BF16)
            return carry

        lax.fori_loop(0, total // chunk, body, 0)
        for b in range(8):
            arrived(out_held.at[b], out_sems.at[b])

        def out(j, carry):
            weight = out_held[pl.ds(4 * j, 4)].reshape(512, width)
            mixed_ref[:, pl.ds(pl.multiple_of(512 * j, 512), 512)] = dot_nt(low_ref[...], weight).astype(BF16)
            return carry

        lax.fori_loop(0, 2, out, 0)

    block = (total, width)
    return call(
        kernel,
        (1,),
        [whole((total, wide)), ANY, ANY, whole((total, 128)), whole(vecs.shape)] + [ANY] * (len(up) + len(first)),
        [whole(block), whole(block), whole(block), whole((8, width))],
        [sds(block, F32), sds(block, BF16), sds(block, BF16), sds((8, width), F32)],
        [
            pltpu.VMEM((8, 128, wide), BF16), pltpu.VMEM((8, 128, width), BF16), pltpu.VMEM(block, F32),
            pltpu.VMEM(block, F32), DMA((8,)), DMA((8,)), DMA((2,)),
        ],
        flops=5 * total * width * wide,
        moved=2 * total * wide + 2 * width * wide + 18 * total * width,
    )(meta, pre, grad_sum, unit_one, inverse_one, vecs, *up, *first)


def attend_back(meta, qkv, probs, grad_mixed, batches, rows):
    total, width = grad_mixed.shape
    span = HEADS * HD

    def kernel(meta, q_ref, k_ref, v_ref, g_ref, probs_ref, out_ref, bias_ref):
        left = lax.broadcasted_iota(jnp.int32, (rows, 128), 1) < HD
        for pair in range(HEADS // 2):
            cols = slice(128 * pair, 128 * (pair + 1))
            query, keyed, value, grad = q_ref[0, :, cols], k_ref[0, :, cols], v_ref[0, :, cols], g_ref[:, cols]
            got = ([], [], [])
            for half in range(2):
                mine = left if half == 0 else jnp.logical_not(left)
                low = probs_ref[0, 2 * pair + half]
                probs = low.astype(F32)
                grad_probs = dot_nt(jnp.where(mine, grad, jnp.zeros_like(grad)), value)
                inner = jnp.sum(probs * grad_probs, -1, keepdims=True)
                scores = (probs * (grad_probs - inner) * (HD**-0.5)).astype(BF16)
                got[0].append(dot_nn(scores, keyed))
                got[1].append(dot_tn(scores, query))
                got[2].append(dot_tn(low, grad))
            for i in range(3):
                part = jnp.where(left, got[i][0], got[i][1]).astype(BF16)
                out_ref[i, :, cols] = part
                bias_ref[0, i : i + 1, cols] = jnp.sum(part.astype(F32), 0, keepdims=True)

    part = lambda w: spec((1, rows, span), lambda b, h, meta: (w, b, h))
    return call(
        kernel,
        (batches, width // span),
        [
            part(0), part(1), part(2),
            spec((rows, span), lambda b, h, meta: (b, h)),
            spec((1, HEADS, rows, rows), lambda b, h, meta: (b, h, 0, 0)),
        ],
        [
            spec((3, rows, span), lambda b, h, meta: (0, b, h)),
            spec((1, 8, span), lambda b, h, meta: (b, 0, h)),
        ],
        [sds((3, total, width), BF16), sds((batches, 8, width), F32)],
        [],
        flops=30 * total * rows * width,
        moved=14 * total * width + 2 * batches * H * rows * rows,
    )(meta, qkv, qkv, qkv, grad_mixed, probs)


def back_project(meta, grads, first, grad_resid):
    total, width = grad_resid.shape

    def kernel(meta, g_ref, resid_ref, *refs):
        parts, (out_ref, held, resid, made, sems, more, out_sems) = refs[: len(first)], refs[len(first) :]
        fetch(meta, parts, held, sems, 0, 384)
        incoming = pltpu.make_async_copy(resid_ref, resid, more)
        incoming.start()
        incoming.wait()

        def leave(j):
            at = pl.ds(pl.multiple_of(256 * j, 256), 256)
            return pltpu.make_async_copy(made.at[:, at], out_ref.at[:, at], out_sems.at[j])

        def body(j, carry):
            for b in range(2):
                arrived(held.at[2 * j + b], sems.at[2 * j + b])
            at = pl.ds(pl.multiple_of(256 * j, 256), 256)
            part = resid[:, at]
            for w in range(3):
                weight = held[pl.ds(2 * j, 2), 128 * w : 128 * (w + 1)].reshape(256, width)
                part = part + dot_nt(g_ref[w], weight)
            made[:, at] = part.astype(BF16)
            leave(j).start()
            return carry

        lax.fori_loop(0, 4, body, 0)
        for j in range(4):
            leave(j).wait()

    block = (total, width)
    return call(
        kernel,
        (1,),
        [whole((3, total, width)), ANY] + [ANY] * len(first),
        ANY,
        sds(block, BF16),
        [
            pltpu.VMEM((8, 384, width), BF16), pltpu.VMEM(block, F32), pltpu.VMEM(block, BF16), DMA((8,)), DMA(()),
            DMA((4,)),
        ],
        flops=10 * total * width * width,
        moved=12 * total * width + 6 * width * width,
    )(meta, grads, grad_resid, *first)


def weight_grad(meta, left, left_got, right, right_got, codes, block):
    total, cols = right.shape
    share = cols // 2
    tile = min(share, 1024)
    tiles = share // tile
    count = len(codes[0])

    def kernel(meta, left_ref, left_got_ref, right_ref, right_got_ref, *refs):
        outs = refs[:2]
        lefts, rights, made, left_sems, right_sems, out_sems = refs[2:]
        own, got = pl.ds(0, total), pl.ds(total, total)
        for half in range(2):
            for t in range(tiles):
                at = pl.ds(share * half + tile * t, tile)
                slot = half * tiles + t
                pltpu.make_async_copy(right_ref.at[:, at], rights.at[slot, own], right_sems.at[slot]).start()
                pltpu.make_async_copy(right_got_ref.at[:, at], rights.at[slot, got], right_sems.at[slot]).start()
                if t == 0:
                    for i, code in enumerate(codes[half]):
                        at = pl.ds(pl.multiple_of((meta[0] ^ code) * block, block), block)
                        sem = left_sems.at[half, i]
                        pltpu.make_async_copy(left_ref.at[:, at], lefts.at[half, i, own], sem).start()
                        pltpu.make_async_copy(left_got_ref.at[code // 2], lefts.at[half, i, got], sem).start()

        def leave(half, n):
            t, i = n // count, n % count
            at = pl.ds(pl.multiple_of(t * tile, tile), tile)
            return pltpu.make_async_copy(made.at[half, i, :, at], outs[half].at[i, :, at], out_sems.at[half, n])

        for half in range(2):

            def body(n, carry):
                t, i = n // count, n % count

                @pl.when(i == 0)
                def _():
                    arrived(rights.at[half * tiles + t], right_sems.at[half * tiles + t])

                @pl.when(t == 0)
                def _():
                    arrived(lefts.at[half, i], left_sems.at[half, i])

                at = pl.ds(pl.multiple_of(t * tile, tile), tile)
                made[half, i, :, at] = dot_tn(lefts[half, i], rights[half * tiles + t]).astype(BF16)
                leave(half, n).start()
                return carry

            lax.fori_loop(0, tiles * count, body, 0)
        for half in range(2):
            for n in range(tiles * count):
                leave(half, n).wait()

    out = (2, count, block, share)
    return call(
        kernel,
        (1,),
        [ANY] * 4,
        [ANY] * 2,
        [sds(out[1:], BF16)] * 2,
        [
            pltpu.VMEM((2, count, 2 * total, block), BF16), pltpu.VMEM((2 * tiles, 2 * total, tile), BF16),
            pltpu.VMEM(out, BF16), DMA((2, count)), DMA((2 * tiles,)), DMA((2, tiles * count)),
        ],
        flops=0,
        moved=0,
    )(meta, left, left_got, right, right_got)


HIGH = 272


def first_grad(meta, tokens, tokens_got, mixed, mixed_got, grads, grads_got, low, low_got, vec, vec_got, codes):
    total, width = tokens.shape
    count = len(codes[0])

    def kernel(meta, x_ref, x_got, mixed_ref, mixed_got, g_ref, g_got, low_ref, low_got, vec_ref, vec_got, *refs):
        outs = refs[:2]
        lefts, rights, made, short, left_sems, right_sems, out_sems, short_sems = refs[2:]
        own, got = pl.ds(0, total), pl.ds(total, total)

        def left_copy(half, kind, i):
            code = codes[half][i]
            at = pl.ds(pl.multiple_of((meta[0] ^ code) * 128, 128), 128)
            slot, sem = half + kind, left_sems.at[half + kind, i]
            source, other = ((x_ref, x_got), (mixed_ref, mixed_got))[kind]
            pltpu.make_async_copy(source.at[:, at], lefts.at[slot, i, own], sem).start()
            pltpu.make_async_copy(other.at[code // 2], lefts.at[slot, i, got], sem).start()

        for half in range(2):
            for w in (2 * half, 2 * half + 1):
                source, other = (g_ref.at[w], g_got.at[w]) if w < 3 else (low_ref, low_got)
                pltpu.make_async_copy(source, rights.at[w, own], right_sems.at[w]).start()
                pltpu.make_async_copy(other, rights.at[w, got], right_sems.at[w]).start()
            for i in range(count):
                left_copy(half, 0, i)
                if half == 1:
                    left_copy(half, 1, i)
                    at = meta[0] ^ codes[1][i]
                    pltpu.make_async_copy(vec_ref.at[at], short.at[i, 0], short_sems.at[i]).start()
                    pltpu.make_async_copy(vec_got.at[at], short.at[i, 1], short_sems.at[i]).start()
        for half in range(2):

            def body(i, carry):
                for k in range(2):
                    w = 2 * half + k
                    kind = 1 if w == 3 else 0
                    if kind == 1 or k == 0:
                        arrived(lefts.at[half + kind, i], left_sems.at[half + kind, i])

                    @pl.when(i == 0)
                    def _():
                        arrived(rights.at[w], right_sems.at[w])

                    part = dot_tn(lefts[half + kind, i], rights[w])
                    made[half, i, 128 * k : 128 * (k + 1)] = part.astype(BF16)
                if half == 0:
                    made[half, i, 256:] = jnp.zeros((16, width), BF16)
                else:
                    arrived(short.at[i], short_sems.at[i])
                    made[half, i, 256:] = (short[i, 0].astype(F32) + short[i, 1].astype(F32)).astype(BF16)
                pltpu.make_async_copy(made.at[half, i], outs[half].at[i], out_sems.at[half, i]).start()
                return carry

            lax.fori_loop(0, count, body, 0)
        for half in range(2):
            for i in range(count):
                pltpu.make_async_copy(made.at[half, i], outs[half].at[i], out_sems.at[half, i]).wait()

    out = (2, count, HIGH, width)
    return call(
        kernel,
        (1,),
        [ANY] * 10,
        [ANY] * 2,
        [sds(out[1:], BF16)] * 2,
        [
            pltpu.VMEM((3, count, 2 * total, 128), BF16), pltpu.VMEM((4, 2 * total, width), BF16),
            pltpu.VMEM(out, BF16), pltpu.VMEM((count, 2, 16, width), BF16),
            DMA((3, count)), DMA((4,)), DMA((2, count)), DMA((count,)),
        ],
        flops=0,
        moved=0,
    )(meta, tokens, tokens_got, mixed, mixed_got, grads, grads_got, low, low_got, vec, vec_got)


def pack(weights, small):
    block, width = weights[0].shape
    high = block * len(weights) + 16

    def kernel(*refs):
        out_ref = refs[-1]
        for i in range(len(weights)):
            out_ref[block * i : block * (i + 1)] = refs[i][...]
        out_ref[block * len(weights) :] = jnp.zeros((16, width), BF16)
        start = 0
        for ref in refs[len(weights) : -1]:
            count = ref.shape[1]
            row, column = block * len(weights) + start // width, start % width
            out_ref[row : row + 1, column : column + count] = ref[...]
            start += count

    return pl.pallas_call(
        kernel,
        out_shape=jax.ShapeDtypeStruct((high, width), BF16),
        compiler_params=pltpu.CompilerParams(vmem_limit_bytes=VMEM),
        cost_estimate=pl.CostEstimate(flops=1024, bytes_accessed=1024, transcendentals=0),
    )(*weights, *[part.reshape(1, -1) for part in small])


CORE, ALONG_X, ALONG_Y = 1, 2, 4


def swap(value, mask):
    return lax.ppermute(value, "shard", [(i, i ^ mask) for i in range(8)])


def plus(*parts):
    total = parts[0].astype(F32)
    for part in parts[1:]:
        total = total + part.astype(F32)
    return total.astype(BF16)


class Order:
    def __init__(self, meta):
        self.meta = meta

    def place(self, *values):
        return lax.optimization_barrier(values + (self.meta,))[:-1]

    def then(self, value):
        self.meta, value = lax.optimization_barrier((self.meta, value))
        return value

    def run(self, function, *values):
        return self.then(function(*self.place(*values)))


def late(value, *before):
    return lax.optimization_barrier((value,) + before)[0]


def both_cores(*mine):
    return mine + tuple(swap(part, CORE) for part in mine)


class Reduction:
    def __init__(self, order):
        self.order = order
        self.odd = lax.axis_index("rep") % 2 == 1

    def send(self, far):
        self.got = swap(far[0], ALONG_Y), swap(far[1], ALONG_X)

    def keep(self, near):
        self.near = near

    def turn(self):
        def add(near_a, near_b, got_a, got_b):
            return plus(near_a[1], got_a[1]), plus(near_b[1], got_b[1])

        passed = self.order.run(add, *self.near, *self.got)
        self.passed = swap(passed[0], ALONG_X), swap(passed[1], ALONG_Y)

    def pair(self):
        def add(near_a, near_b, got_a, got_b, passed_a, passed_b):
            first, second = plus(near_a[0], got_a[0], passed_a), plus(near_b[0], got_b[0], passed_b)
            return jnp.where(self.odd, second, first), jnp.where(self.odd, first, second)

        self.kept, given = self.order.run(add, *self.near, *self.got, *self.passed)
        self.taken = lax.ppermute(given, "rep", [(i, i ^ 1) for i in range(4)])

    def across(self):
        self.half = self.order.run(plus, self.kept, self.taken)
        self.over = lax.ppermute(self.half, "rep", [(i, i ^ 2) for i in range(4)])

    def back(self):
        self.total = self.order.run(plus, self.half, self.over)
        self.other = lax.ppermute(self.total, "rep", [(i, i ^ 1) for i in range(4)])

    def done(self, axis):
        first = jnp.where(self.odd, self.other, self.total).astype(F32)
        second = jnp.where(self.odd, self.total, self.other).astype(F32)
        return jnp.concatenate([first, second], axis) if axis is not None else (first, second)


def local_eight(
    inputs, lengths, dealing, w_query, w_key, w_value, w_out, b_query, b_value, b_out,
    ln1_gain, ln1_bias, w_up, b_up, w_down, b_down, ln2_gain, ln2_bias, cotangent,
):
    batches, rows, width = inputs.shape
    wide = w_up.shape[1]
    total = batches * rows
    group = batches * 4
    shard_index = lax.axis_index("shard")
    anchor = shard_index * group
    slots = anchor + lax.axis_index("rep") * batches + jnp.arange(batches, dtype=jnp.int32)
    local_dealing = lax.dynamic_slice_in_dim(dealing, anchor, group) - anchor
    sources = jnp.take(dealing, slots) - anchor
    places = jnp.arange(group, dtype=jnp.int32)
    wanted = jnp.sum(
        jnp.where(local_dealing[None, :] == (slots - anchor)[:, None], places[None, :], 0), 1
    )
    meta = jnp.concatenate([shard_index[None].astype(jnp.int32), jnp.take(lengths, slots), wanted])
    order = Order(meta)
    tokens = inputs.reshape(total, width)

    small = (b_query, b_value, b_out, ln1_gain, ln1_bias, b_down, ln2_gain, ln2_bias, b_up)
    own_first = pack((w_query, w_key, w_value, w_out), small)
    first_x, first_y = swap(own_first, ALONG_X), swap(own_first, ALONG_Y)
    first_far = swap(first_x, ALONG_Y)
    up_x = swap(late(w_up, first_x), ALONG_X)
    up_y = swap(late(w_up, first_far), ALONG_Y)
    down_x = swap(late(w_down, up_x), ALONG_X)
    first = both_cores(own_first, first_x, first_y, first_far)
    cot_pool = lax.all_gather(cotangent, "rep", axis=0, tiled=True)

    qkv, vecs, bias_up, tokens_give = order.then(project(order.meta, tokens, first))
    tokens_got = swap(tokens_give, CORE)
    mixed, probs = order.then(attend(order.meta, qkv, batches, rows))
    (up_y,) = order.then(order.place(up_y))
    up_far = swap(up_y, ALONG_X)
    down_y = swap(late(w_down, up_y), ALONG_Y)
    unit_one, inverse_one, hidden_low, both_give = order.then(mix_out(order.meta, mixed, tokens, first, vecs))
    (down_x,) = order.then(order.place(down_x))
    down_top = swap(down_x[:256], ALONG_Y)
    (up_far,) = order.place(up_far)
    up = both_cores(w_up, up_x, up_y, up_far)
    act, slope, act_give = order.then(feed_up(order.meta, hidden_low, up, bias_up))
    (down_y,) = order.then(order.place(down_y))
    down_end = swap(down_y[256:], ALONG_X)
    down = both_cores(w_down, down_x, down_y, down_top, down_end)
    both_got, act_got = swap(both_give, CORE), swap(act_give, CORE)
    tokens_got, both_got, act_got = order.then((tokens_got, both_got, act_got))
    mixed_got, hidden_got = both_got[0], both_got[1]
    out, grad_sum, sum_low, grads_two = order.then(
        feed_down(order.meta, act, down, unit_one, cot_pool, vecs, batches, rows)
    )
    sum_got = order.then(swap(sum_low, CORE))
    out_pool = lax.all_gather(out.reshape(batches, rows, width), "rep", axis=0, tiled=True)
    far, near = [[4, 6], [2, 6]], [[0, 2], [0, 4]]
    of_down, of_up, of_first = Reduction(order), Reduction(order), Reduction(order)

    def down_grad(codes):
        return order.then(weight_grad(order.meta, act, act_got, sum_low, sum_got, codes, 512))

    def up_grad(codes):
        return order.then(weight_grad(order.meta, hidden_low, hidden_got, pre, pre_got, codes, 128))

    def attn_grad(codes):
        return order.then(
            first_grad(
                order.meta, tokens, tokens_got, mixed, mixed_got, grads, grads_got, resid_low, resid_got, vec, vec_got,
                codes,
            )
        )

    of_down.send(down_grad(far))
    pre, grad_bias_up = order.then(back_down(order.meta, sum_low, down, slope))
    pre_got = swap(pre, CORE)
    of_down.keep(down_grad(near))
    of_up.send(up_grad(far))
    grad_resid, resid_low, grad_mixed, grads_one = order.then(
        back_up(order.meta, pre, up, first, grad_sum, unit_one, inverse_one, vecs)
    )
    of_down.turn()
    resid_got = swap(resid_low, CORE)
    of_up.keep(up_grad(near))
    grads, grads_bias = order.then(attend_back(order.meta, qkv, probs, grad_mixed, batches, rows))
    (out_pool,) = order.then(order.place(out_pool))
    of_down.pair()
    of_up.turn()
    grads_got = swap(grads, CORE)
    grads_bias = jnp.sum(grads_bias, 0)
    rows_of = (
        grads_bias[0], grads_bias[2], grads_one[2], grads_one[0], grads_one[1],
        grads_two[2], grads_two[0], grads_two[1],
    )
    vec = jnp.concatenate(
        [jnp.stack(rows_of).reshape(8, 8, 128).transpose(1, 0, 2).reshape(8, width), grad_bias_up.reshape(8, 512)], 1
    )
    vec = jnp.pad(vec, ((0, 0), (0, 16 * width - vec.shape[1]))).reshape(8, 16, width).astype(BF16)
    vec_got = swap(vec, CORE)
    grad_input = order.then(back_project(order.meta, grads, first, grad_resid))
    of_down.across()
    of_first.send(attn_grad(far))
    of_up.pair()
    of_first.keep(attn_grad(near))
    of_down.back()
    of_up.across()
    of_first.turn()
    of_up.back()
    of_first.pair()
    g_down = order.run(lambda *_: of_down.done(1))
    of_first.across()
    g_up = order.run(lambda *_: of_up.done(1))
    of_first.back()
    top, end = of_first.done(None)
    layer_out = pick(out_pool, sources)
    g_vec = end[256:258].reshape(-1)
    line = lambda i: g_vec[128 * i : 128 * (i + 1)]
    return (
        layer_out, grad_input.reshape(batches, rows, width),
        top[0:128], top[128:256], end[0:128], end[128:256],
        line(0), line(1), line(2), line(3), line(4),
        g_up, g_vec[1024:1536], g_down, line(5), line(6), line(7),
    )


def pick(pool, targets):
    return jnp.stack(
        [lax.dynamic_index_in_dim(pool, targets[i], 0, keepdims=False) for i in range(targets.shape[0])]
    )


def local_general(
    inputs, lengths, dealing, w_query, w_key, w_value, w_out, b_query, b_value, b_out,
    ln1_gain, ln1_bias, w_up, b_up, w_down, b_down, ln2_gain, ln2_bias, cotangent,
):
    batches, rows, width = inputs.shape
    shards = lax.axis_size("shard")
    replicas = lax.axis_size("rep")
    group = batches * replicas
    shard_index = lax.axis_index("shard")
    rep_index = lax.axis_index("rep")
    anchor = shard_index * group
    slots = anchor + rep_index * batches + jnp.arange(batches, dtype=jnp.int32)
    seq_lengths = jnp.take(lengths, slots)
    local_dealing = lax.dynamic_slice_in_dim(dealing, anchor, group) - anchor
    sources = jnp.take(dealing, slots) - anchor
    places = jnp.arange(group, dtype=jnp.int32)
    wanted = jnp.sum(
        jnp.where(local_dealing[None, :] == (slots - anchor)[:, None], places[None, :], 0), 1
    )

    def gather(block):
        return lax.all_gather(block, "shard", axis=0, tiled=True)

    block = w_query.shape[0]
    wide = w_up.shape[1]
    small = (b_query, b_value, b_out, ln1_gain, ln1_bias, b_down, ln2_gain, ln2_bias, b_up)
    vec = jnp.concatenate(small)
    first = jnp.concatenate([w_query, w_key, w_value, w_out], 0)
    all_vec = lax.all_gather(vec, "shard", axis=0, tiled=True).reshape(shards, -1)
    all_first = gather(first).reshape(shards, 4, block, width)
    cuts = [0]
    for part in small:
        cuts.append(cuts[-1] + part.shape[0])
    (bias_query, bias_value, bias_out, gain_one, shift_one, bias_down, gain_two, shift_two, bias_up) = [
        all_vec[:, cuts[i] : cuts[i + 1]].reshape(-1).astype(F32) for i in range(len(small))
    ]
    full_query, full_key, full_value, full_out = [
        all_first[:, i].reshape(width, width) for i in range(4)
    ]
    full_up = gather(w_up)
    full_down = gather(w_down)
    cot = pick(lax.all_gather(cotangent, "rep", axis=0, tiled=True), wanted)

    tokens = inputs.reshape(batches * rows, width)
    query = (matmul(tokens, full_query) + bias_query).astype(BF16)
    keyed = matmul(tokens, full_key).astype(BF16)
    value = (matmul(tokens, full_value) + bias_value).astype(BF16)
    heads = lambda a: a.reshape(batches, rows, H, HD).transpose(0, 2, 1, 3)
    flat = lambda a: a.transpose(0, 2, 1, 3).reshape(batches * rows, width)
    qh, kh, vh = heads(query), heads(keyed), heads(value)
    allowed = lax.broadcasted_iota(jnp.int32, (batches, 1, 1, rows), 3) < seq_lengths[:, None, None, None]
    scale = HD ** (-0.5)
    scores = jnp.einsum("bhqd,bhkd->bhqk", qh, kh, preferred_element_type=F32) * scale
    scores = jnp.where(allowed, scores, NEG)
    raised = jnp.exp(scores - jnp.max(scores, -1, keepdims=True))
    probs = raised / jnp.sum(raised, -1, keepdims=True)
    probs_low = probs.astype(BF16)
    mixed_low = flat(jnp.einsum("bhqk,bhkd->bhqd", probs_low, vh, preferred_element_type=F32).astype(BF16))
    hidden, unit_one, inverse_one = normalize(
        tokens.astype(F32) + matmul(mixed_low, full_out) + bias_out, gain_one, shift_one
    )
    hidden_low = hidden.astype(BF16)
    pre = matmul(hidden_low, full_up) + bias_up
    act, slope = gelu_both(pre)
    act_low = act.astype(BF16)
    summed = hidden + matmul(act_low, full_down) + bias_down
    normed, unit_two, inverse_two = normalize(summed, gain_two, shift_two)
    valid = (lax.broadcasted_iota(jnp.int32, (batches, rows, 1), 1) < seq_lengths[:, None, None]).reshape(-1, 1)
    out = jnp.where(valid, normed, 0.0).astype(BF16).reshape(batches, rows, width)
    layer_out = pick(lax.all_gather(out, "rep", axis=0, tiled=True), sources)

    grad_out = jnp.where(valid, cot.reshape(-1, width).astype(F32), 0.0)
    grad_gain_two = jnp.sum(grad_out * unit_two, 0)
    grad_shift_two = jnp.sum(grad_out, 0)
    grad_sum = norm_back(grad_out, unit_two, inverse_two, gain_two)
    grad_bias_down = jnp.sum(grad_sum, 0)
    grad_sum_low = grad_sum.astype(BF16)

    def reduced(part):
        return lax.psum_scatter(part, "shard", scatter_dimension=0, tiled=True)

    def over_rep(part):
        return lax.psum(part, "rep").astype(F32)

    g_down = reduced(left_trans(act_low, grad_sum_low).astype(BF16))
    grad_pre = (right_trans(grad_sum_low, full_down) * slope).astype(BF16)
    grad_bias_up = jnp.sum(grad_pre.astype(F32), 0)
    g_up = reduced(left_trans(hidden_low, grad_pre).astype(BF16))
    grad_hidden = grad_sum + right_trans(grad_pre, full_up)
    grad_gain_one = jnp.sum(grad_hidden * unit_one, 0)
    grad_shift_one = jnp.sum(grad_hidden, 0)
    grad_resid = norm_back(grad_hidden, unit_one, inverse_one, gain_one)
    grad_bias_out = jnp.sum(grad_resid, 0)
    grad_resid_low = grad_resid.astype(BF16)
    grad_w_out = left_trans(mixed_low, grad_resid_low).astype(BF16)
    grad_mixed = heads(right_trans(grad_resid_low, full_out).astype(BF16))
    grad_probs = jnp.einsum("bhqd,bhkd->bhqk", grad_mixed, vh, preferred_element_type=F32)
    inner = jnp.sum(probs * grad_probs, -1, keepdims=True)
    grad_scores = (probs * (grad_probs - inner) * scale).astype(BF16)
    query_low = flat(jnp.einsum("bhqk,bhkd->bhqd", grad_scores, kh, preferred_element_type=F32).astype(BF16))
    key_low = flat(jnp.einsum("bhqk,bhqd->bhkd", grad_scores, qh, preferred_element_type=F32).astype(BF16))
    value_low = flat(jnp.einsum("bhqk,bhqd->bhkd", probs_low, grad_mixed, preferred_element_type=F32).astype(BF16))
    grad_bias_query = jnp.sum(query_low.astype(F32), 0)
    grad_bias_value = jnp.sum(value_low.astype(F32), 0)
    blocks = [
        part.reshape(shards, block, width)
        for part in (
            left_trans(tokens, query_low).astype(BF16),
            left_trans(tokens, key_low).astype(BF16),
            left_trans(tokens, value_low).astype(BF16),
            grad_w_out,
        )
    ]
    g_first = reduced(jnp.concatenate(blocks, 1).reshape(shards * 4 * block, width))
    grad_tokens = (
        grad_resid
        + right_trans(query_low, full_query)
        + right_trans(key_low, full_key)
        + right_trans(value_low, full_value)
    )
    grad_input = grad_tokens.astype(BF16).reshape(batches, rows, width)
    vec_terms = (
        grad_bias_query, grad_bias_value, grad_bias_out, grad_gain_one, grad_shift_one,
        grad_bias_down, grad_gain_two, grad_shift_two, grad_bias_up,
    )
    g_vec = jnp.concatenate([part.reshape(shards, -1) for part in vec_terms], 1)
    g_vec = lax.psum(g_vec, ("shard", "rep"))
    g_vec = lax.dynamic_index_in_dim(g_vec, shard_index, 0, keepdims=False)
    (g_bquery, g_bvalue, g_bout, g_gain_one, g_shift_one, g_bdown, g_gain_two, g_shift_two, g_bup) = [
        g_vec[cuts[i] : cuts[i + 1]] for i in range(len(small))
    ]
    g_down = over_rep(g_down)
    g_up = over_rep(g_up)
    g_first = over_rep(g_first).reshape(4, block, width)
    return (
        layer_out, grad_input, g_first[0], g_first[1], g_first[2], g_first[3],
        g_bquery, g_bvalue, g_bout, g_gain_one, g_shift_one,
        g_up, g_bup, g_down, g_bdown, g_gain_two, g_shift_two,
    )


def solution(mesh):
    seqs = P(("shard", "rep"), None, None)
    mat = P("shard", None)
    vec = P("shard")
    in_specs = (
        seqs, P(), P(), mat, mat, mat, mat, vec, vec, vec, vec, vec, mat, vec, mat, vec, vec, vec, seqs,
    )
    out_specs = (
        seqs, seqs, mat, mat, mat, mat, vec, vec, vec, vec, vec, mat, vec, mat, vec, vec, vec,
    )
    shape = dict(mesh.shape)
    local = local_eight if shape["shard"] == 8 and shape["rep"] == 4 else local_general
    return jax.shard_map(local, mesh=mesh, in_specs=in_specs, out_specs=out_specs, check_vma=False)
```

```python
import math

import jax
import jax.numpy as jnp
from jax import lax
from jax.experimental import pallas as pl
from jax.experimental.pallas import tpu as pltpu
from jax.sharding import PartitionSpec as P

H = 16
HD = 64
EPS = 1e-05
NEG = -1e30
F32 = jnp.float32
BF16 = jnp.bfloat16


def matmul(left, right):
    return jnp.dot(left, right, preferred_element_type=F32)


def left_trans(left, right):
    return lax.dot_general(left, right, (((0,), (0,)), ((), ())), preferred_element_type=F32)


def right_trans(left, right):
    return lax.dot_general(left, right, (((1,), (1,)), ((), ())), preferred_element_type=F32)


def normalize(values, gain, shift):
    center = values - jnp.mean(values, -1, keepdims=True)
    inverse = lax.rsqrt(jnp.mean(center * center, -1, keepdims=True) + EPS)
    unit = center * inverse
    return (unit * gain + shift, unit, inverse)


def norm_back(grad, unit, inverse, gain):
    scaled = grad * gain
    return inverse * (
        scaled
        - jnp.mean(scaled, -1, keepdims=True)
        - unit * jnp.mean(scaled * unit, -1, keepdims=True)
    )


def gelu_both(pre):
    cumul = 0.5 * (1.0 + lax.erf(pre * 0.7071067811865476))
    density = jnp.exp(-0.5 * pre * pre) * 0.3989422804014327
    return (pre * cumul, cumul + pre * density)


VMEM = 56 * 1024 * 1024
TIGHT = ()
ANY = pl.BlockSpec(memory_space=pl.ANY)
DMA = pltpu.SemaphoreType.DMA


def spec(shape, index):
    return pl.BlockSpec(shape, index)


def whole(shape):
    zeros = (0,) * len(shape)
    return pl.BlockSpec(shape, lambda *_: zeros)


def sds(shape, dtype):
    return jax.ShapeDtypeStruct(shape, dtype)


def room(specs, shapes, scratch):
    total = 8 * 1024 * 1024
    for block, shape in zip(specs, shapes):
        if block.block_shape is not None:
            total += 2 * math.prod(block.block_shape) * shape.dtype.itemsize
    for item in scratch:
        if item.memory_space == pltpu.VMEM:
            total += math.prod(item.shape) * jnp.dtype(item.dtype).itemsize
    return total


def call(kernel, grid, in_specs, out_specs, out_shape, scratch):
    def run(*args):
        outs = out_shape if isinstance(out_shape, (list, tuple)) else [out_shape]
        specs = out_specs if isinstance(out_specs, (list, tuple)) else [out_specs]
        limit = VMEM
        if kernel.__qualname__.split(".")[0] in TIGHT:
            limit = room(list(in_specs) + list(specs), list(args[1:]) + list(outs), scratch)
        return pl.pallas_call(
            kernel,
            grid_spec=pltpu.PrefetchScalarGridSpec(
                num_scalar_prefetch=1,
                grid=grid,
                in_specs=in_specs,
                out_specs=out_specs,
                scratch_shapes=list(scratch),
            ),
            out_shape=out_shape,
            compiler_params=pltpu.CompilerParams(vmem_limit_bytes=limit),
            cost_estimate=pl.CostEstimate(flops=1024, bytes_accessed=1024, transcendentals=0),
        )(*args)

    return run


def dot_nn(a, b):
    return lax.dot_general(a, b, (((1,), (0,)), ((), ())), preferred_element_type=F32)


def dot_nt(a, b):
    return lax.dot_general(a, b, (((1,), (1,)), ((), ())), preferred_element_type=F32)


def dot_tn(a, b):
    return lax.dot_general(a, b, (((0,), (0,)), ((), ())), preferred_element_type=F32)


def fetch(meta, parts, target, sems, low, high, columns=None):
    cut = parts[3].shape[0]
    each = len(parts) // 2
    for core in range(2):
        for chip in range(4):
            at = meta[0] ^ (2 * chip + core)
            if chip < 3:
                pieces = [(parts[each * core + chip], low, high, 0)]
            else:
                pieces = []
                if low < cut:
                    pieces.append((parts[each * core + 3], low, min(high, cut), 0))
                if high > cut:
                    start = max(low, cut)
                    pieces.append((parts[each * core + 4], start - cut, high - cut, start - low))
            for ref, begin, end, offset in pieces:
                source = ref.at[pl.ds(begin, end - begin)]
                if columns is not None:
                    source = ref.at[pl.ds(begin, end - begin), columns]
                goal = target.at[at]
                if len(pieces) > 1:
                    goal = target.at[at, pl.ds(offset, end - begin)]
                pltpu.make_async_copy(source, goal, sems.at[at]).start()


def arrived(target, sem):
    pltpu.make_async_copy(target, target, sem).wait()


def hand_over(meta, source, target, sems, block):
    copies = []
    for chip in range(4):
        at = pl.ds(pl.multiple_of((meta[0] ^ (2 * chip + 1)) * block, block), block)
        copies.append(pltpu.make_async_copy(source.at[:, at], target.at[chip], sems.at[chip]))
        copies[-1].start()
    return copies


def project(meta, tokens, first):
    rows, width = tokens.shape
    tile = 512
    count = width // tile

    def kernel(meta, x_ref, *refs):
        parts, (out_ref, vec_ref, up_ref, give_ref, held, short, made, sems, short_sems, out_sems, give_sems) = refs[: len(first)], refs[len(first) :]
        for w in range(3):
            fetch(meta, parts, held.at[w], sems.at[w], 128 * w, 128 * (w + 1))
            if w == 0:
                fetch(meta, parts, short, short_sems, 512, 528)
        gifts = hand_over(meta, x_ref, give_ref, give_sems, 128)
        for b in range(8):
            arrived(short.at[b], short_sems.at[b])
        for b in range(8):
            two = short[b].astype(F32)
            for v in range(8):
                vec_ref[v : v + 1, 128 * b : 128 * (b + 1)] = two[0:1, 128 * v : 128 * (v + 1)]
            up_ref[0:1, 512 * b : 512 * (b + 1)] = two[1:2, :512]

        def body(i, carry):
            w, n = i // count, i % count

            @pl.when(n == 0)
            def _():
                for b in range(8):
                    arrived(held.at[w, b], sems.at[w, b])

            at = pl.ds(pl.multiple_of(n * tile, tile), tile)
            weight = held[w, :, :, at].reshape(width, tile)
            bias = jnp.where(w == 0, vec_ref[0:1, at], vec_ref[1:2, at])
            bias = jnp.where(w == 1, jnp.zeros_like(bias), bias)
            made[w, :, at] = (dot_nn(x_ref[...], weight) + bias).astype(BF16)

            @pl.when(n == count - 1)
            def _():
                pltpu.make_async_copy(made.at[w], out_ref.at[w], out_sems.at[w]).start()

            return carry

        lax.fori_loop(0, 3 * count, body, 0)
        for w in range(3):
            pltpu.make_async_copy(made.at[w], out_ref.at[w], out_sems.at[w]).wait()
        for copy in gifts:
            copy.wait()

    return call(
        kernel,
        (1,),
        [whole((rows, width))] + [ANY] * len(first),
        [ANY, whole((8, width)), whole((1, 4 * width)), ANY],
        [sds((3, rows, width), BF16), sds((8, width), F32), sds((1, 4 * width), F32), sds((4, rows, 128), BF16)],
        [
            pltpu.VMEM((3, 8, 128, width), BF16), pltpu.VMEM((8, 16, width), BF16),
            pltpu.VMEM((3, rows, width), BF16), DMA((3, 8)), DMA((8,)), DMA((3,)), DMA((4,)),
        ],
    )(meta, tokens, *first)


HEADS = 4


def attend(meta, qkv, batches, rows):
    total, width = qkv.shape[1:]
    span = HEADS * HD
    steps = width // span

    def kernel(meta, q_ref, k_ref, v_ref, mixed_ref, raised_ref, inverse_ref):
        length = meta[1 + pl.program_id(0)]
        allowed = lax.broadcasted_iota(jnp.int32, (1, rows), 1) < length
        shift = jnp.where(allowed, 0.0, NEG)
        left = lax.broadcasted_iota(jnp.int32, (rows, 128), 1) < HD
        one = jnp.ones((rows, 128), BF16)
        for pair in range(HEADS // 2):
            cols = slice(128 * pair, 128 * (pair + 1))
            query, keyed, value = q_ref[0, :, cols] * jnp.asarray(HD**-0.5, BF16), k_ref[0, :, cols], v_ref[0, :, cols]
            outs = []
            for half in range(2):
                mine = left if half == 0 else jnp.logical_not(left)
                scores = dot_nt(jnp.where(mine, query, jnp.zeros_like(query)), keyed) + shift
                raised = jnp.exp(scores - jnp.max(scores, -1, keepdims=True)).astype(BF16)
                raised_ref[0, 2 * pair + half] = raised
                outs.append(dot_nn(raised, jnp.where(mine, value, one)))
            inverse = 1.0 / pltpu.roll(jnp.where(left, outs[1], outs[0]), HD, 1)
            inverse_ref[:, cols] = inverse
            mixed_ref[:, cols] = (jnp.where(left, outs[0], outs[1]) * inverse).astype(BF16)

    part = lambda w: spec((1, rows, span), lambda b, h, meta: (w, b, h))
    here = spec((rows, span), lambda b, h, meta: (b, h))
    return call(
        kernel,
        (batches, steps),
        [part(0), part(1), part(2)],
        [here, spec((1, HEADS, rows, rows), lambda b, h, meta: (b, h, 0, 0)), here],
        [sds((total, width), BF16), sds((batches, H, rows, rows), BF16), sds((total, width), F32)],
        [],
    )(meta, qkv, qkv, qkv)


def mix_out(meta, mixed, tokens, first, vecs):
    total, width = mixed.shape
    tile = 128

    def kernel(meta, mixed_ref, tokens_ref, vec_ref, *refs):
        parts, (unit_ref, inv_ref, low_ref, give_ref, held, sems, give_sems) = refs[: len(first)], refs[len(first) :]
        fetch(meta, parts, held, sems, 384, 512)
        gifts = hand_over(meta, mixed_ref, give_ref.at[0], give_sems.at[0], 128)
        for b in range(8):
            arrived(held.at[b], sems.at[b])

        def body(i, carry):
            here = pl.ds(pl.multiple_of(i * tile, tile), tile)
            branch = dot_nn(mixed_ref[here], held[...].reshape(width, width)) + vec_ref[2:3]
            hidden, unit, inverse = normalize(tokens_ref[here].astype(F32) + branch, vec_ref[3:4], vec_ref[4:5])
            unit_ref[here] = unit
            inv_ref[here] = jnp.broadcast_to(inverse, (tile, 128))
            low_ref[here] = hidden.astype(BF16)
            return carry

        lax.fori_loop(0, total // tile, body, 0)
        gifts += hand_over(meta, low_ref, give_ref.at[1], give_sems.at[1], 128)
        for copy in gifts:
            copy.wait()

    block = (total, width)
    return call(
        kernel,
        (1,),
        [whole(block), whole(block), whole(vecs.shape)] + [ANY] * len(first),
        [whole(block), whole((total, 128)), whole(block), ANY],
        [sds(block, F32), sds((total, 128), F32), sds(block, BF16), sds((2, 4, total, 128), BF16)],
        [pltpu.VMEM((8, 128, width), BF16), DMA((8,)), DMA((2, 4))],
    )(meta, mixed, tokens, vecs, *first)


def feed_up(meta, low, up, bias):
    total, width = low.shape
    wide = up[0].shape[1]
    strip, tile = 1024, 512
    strips, inner = wide // strip, strip // tile

    def kernel(meta, x_ref, bias_ref, *refs):
        parts, (act_ref, slope_ref, give_ref, held, act, slope, sems, out_sems, give_sems) = refs[: len(up)], refs[len(up) :]
        for t in range(strips):
            fetch(meta, parts, held.at[t], sems.at[t], 0, 128, pl.ds(strip * t, strip))

        def leave(i):
            at = pl.ds(pl.multiple_of(i * tile, tile), tile)
            return (
                pltpu.make_async_copy(act.at[i], act_ref.at[:, at], out_sems.at[0, i]),
                pltpu.make_async_copy(slope.at[i], slope_ref.at[:, at], out_sems.at[1, i]),
            )

        def body(i, carry):
            t, n = i // inner, i % inner

            @pl.when(n == 0)
            def _():
                for b in range(8):
                    arrived(held.at[t, b], sems.at[t, b])

            weight = held[t, :, :, pl.ds(pl.multiple_of(n * tile, tile), tile)].reshape(width, tile)
            pre = dot_nn(x_ref[...], weight) + bias_ref[:, pl.ds(pl.multiple_of(i * tile, tile), tile)]
            value, grad = gelu_both(pre)
            act[i] = value.astype(BF16)
            slope[i] = grad.astype(BF16)
            for copy in leave(i):
                copy.start()
            code = meta[0] ^ i

            @pl.when(code % 2 == 1)
            def _():
                pltpu.make_async_copy(act.at[i], give_ref.at[code // 2], give_sems.at[code // 2]).start()

            return carry

        lax.fori_loop(0, strips * inner, body, 0)
        for i in range(strips * inner):
            for copy in leave(i):
                copy.wait()
        for chip in range(4):
            arrived(give_ref.at[chip], give_sems.at[chip])

    out = sds((total, wide), BF16)
    tiles = wide // tile
    return call(
        kernel,
        (1,),
        [whole((total, width)), whole((1, wide))] + [ANY] * len(up),
        [ANY, ANY, ANY],
        [out, out, sds((4, total, tile), BF16)],
        [
            pltpu.VMEM((strips, 8, 128, strip), BF16), pltpu.VMEM((tiles, total, tile), BF16),
            pltpu.VMEM((tiles, total, tile), BF16), DMA((strips, 8)), DMA((2, tiles)), DMA((4,)),
        ],
    )(meta, low, bias, *up)


def feed_down(meta, act, slope, down, unit_one, cot_pool, vecs, batches, rows):
    total, wide = act.shape
    width = down[0].shape[1]
    chunk = 128

    def kernel(meta, act_ref, slope_ref, unit_ref, cot_ref, vec_ref, *refs):
        parts = refs[: len(down)]
        (
            out_ref, sum_ref, low_ref, grad_ref, pre_ref, bias_ref, out, grad_sums, low, early,
            held, left, right, total_ref, unit, cot, sems, left_sems, right_sems, out_sems, more,
        ) = refs[len(down) :]
        for b in range(8):
            pltpu.make_async_copy(act_ref.at[:, pl.ds(512 * b, 512)], left.at[b], left_sems.at[b]).start()
        fetch(meta, parts, held, sems, 0, 512)
        rest = [pltpu.make_async_copy(unit_ref, unit, more.at[0])] + [
            pltpu.make_async_copy(cot_ref.at[meta[3 + i]], cot.at[i], more.at[1 + i]) for i in range(batches)
        ]
        for copy in rest:
            copy.start()
        for b in range(8):
            pltpu.make_async_copy(slope_ref.at[:, pl.ds(512 * b, 512)], right.at[b], right_sems.at[b]).start()

        def add(b, carry):
            arrived(left.at[b], left_sems.at[b])
            arrived(held.at[b], sems.at[b])
            part = dot_nn(left[b], held[b])

            @pl.when(b == 0)
            def _():
                total_ref[...] = part

            @pl.when(b > 0)
            def _():
                total_ref[...] += part

            return carry

        lax.fori_loop(0, 8, add, 0)
        for copy in rest:
            copy.wait()
        grad_ref[...] = jnp.zeros_like(grad_ref)

        def body(i, carry):
            here = pl.ds(pl.multiple_of(i * chunk, chunk), chunk)
            batch = i // (rows // chunk)
            at = pl.multiple_of((i % (rows // chunk)) * chunk, chunk)
            summed = (unit[here] * vec_ref[3:4] + vec_ref[4:5]) + total_ref[here] + vec_ref[5:6]
            normed, unit_two, inverse = normalize(summed, vec_ref[6:7], vec_ref[7:8])
            place = at + lax.broadcasted_iota(jnp.int32, (chunk, 1), 0)
            valid = place < meta[1 + batch]
            out[here] = jnp.where(valid, normed, 0.0).astype(BF16)
            grad_out = jnp.where(valid, cot[batch, pl.ds(at, chunk)].astype(F32), 0.0)
            grad_sum = norm_back(grad_out, unit_two, inverse, vec_ref[6:7])
            grad_sums[here] = grad_sum
            low[here] = grad_sum.astype(BF16)
            grad_ref[0:1] += jnp.sum(grad_out * unit_two, 0, keepdims=True)
            grad_ref[1:2] += jnp.sum(grad_out, 0, keepdims=True)
            grad_ref[2:3] += jnp.sum(grad_sum, 0, keepdims=True)
            return carry

        lax.fori_loop(0, total // chunk, body, 0)
        leaving = [
            pltpu.make_async_copy(source, target, early.at[i])
            for i, (source, target) in enumerate(((low, low_ref), (out, out_ref), (grad_sums, sum_ref)))
        ]
        for copy in leaving:
            copy.start()

        def leave(b):
            at = pl.ds(pl.multiple_of(512 * b, 512), 512)
            return pltpu.make_async_copy(left.at[b], pre_ref.at[:, at], out_sems.at[b])

        def through(b, carry):
            arrived(right.at[b], right_sems.at[b])
            grad = (dot_nt(low[...], held[b]) * right[b].astype(F32)).astype(BF16)
            left[b] = grad
            leave(b).start()
            bias_ref[:, pl.ds(pl.multiple_of(512 * b, 512), 512)] = jnp.sum(grad.astype(F32), 0, keepdims=True)
            return carry

        lax.fori_loop(0, 8, through, 0)
        for b in range(8):
            leave(b).wait()
        for copy in leaving:
            copy.wait()

    block = (total, width)
    return call(
        kernel,
        (1,),
        [ANY, ANY, ANY, ANY, whole(vecs.shape)] + [ANY] * len(down),
        [ANY, ANY, ANY, whole((8, width)), ANY, whole((1, wide))],
        [
            sds(block, BF16), sds(block, F32), sds(block, BF16), sds((8, width), F32),
            sds((total, wide), BF16), sds((1, wide), F32),
        ],
        [
            pltpu.VMEM(block, BF16), pltpu.VMEM(block, F32), pltpu.VMEM(block, BF16), DMA((3,)),
            pltpu.VMEM((8, 512, width), BF16), pltpu.VMEM((8, total, 512), BF16), pltpu.VMEM((8, total, 512), BF16),
            pltpu.VMEM(block, F32), pltpu.VMEM(block, F32), pltpu.VMEM((batches, rows, width), BF16),
            DMA((8,)), DMA((8,)), DMA((8,)), DMA((8,)), DMA((1 + batches,)),
        ],
    )(meta, act, slope, unit_one, cot_pool, vecs, *down)


def back_up(meta, pre, up, first, grad_sum, unit_one, inverse_one, vecs):
    total, wide = pre.shape
    width = grad_sum.shape[1]
    chunk, strip = 128, 1024
    strips = wide // strip

    def kernel(meta, pre_ref, sum_ref, unit_ref, inv_ref, vec_ref, *refs):
        parts, others = refs[: len(up)], refs[len(up) : len(up) + len(first)]
        (
            resid_ref, low_ref, mixed_ref, grad_ref,
            held, pres, out_held, hidden, unit, low, mixed, sems, pre_sems, out_sems, more, leave_sems,
        ) = refs[len(up) + len(first) :]
        for t in range(strips):
            at = pl.ds(strip * t, strip)
            pltpu.make_async_copy(pre_ref.at[:, at], pres.at[t], pre_sems.at[t]).start()
            fetch(meta, parts, held.at[t], sems.at[t], 0, 128, at)
            if t == 0:
                incoming = pltpu.make_async_copy(sum_ref, hidden, more.at[0])
                incoming.start()
        other = pltpu.make_async_copy(unit_ref, unit, more.at[1])
        other.start()
        fetch(meta, others, out_held, out_sems, 384, 512)
        incoming.wait()

        def through(t, carry):
            arrived(pres.at[t], pre_sems.at[t])
            for b in range(8):
                arrived(held.at[t, b], sems.at[t, b])
            hidden[...] += dot_nt(pres[t], held[t].reshape(width, strip))
            return carry

        lax.fori_loop(0, strips, through, 0)
        other.wait()
        grad_ref[...] = jnp.zeros_like(grad_ref)

        def body(i, carry):
            here = pl.ds(pl.multiple_of(i * chunk, chunk), chunk)
            grad, unit_here = hidden[here], unit[here]
            grad_ref[0:1] += jnp.sum(grad * unit_here, 0, keepdims=True)
            grad_ref[1:2] += jnp.sum(grad, 0, keepdims=True)
            resid = norm_back(grad, unit_here, inv_ref[here, 0:1], vec_ref[3:4])
            grad_ref[2:3] += jnp.sum(resid, 0, keepdims=True)
            hidden[here] = resid
            low[here] = resid.astype(BF16)
            return carry

        lax.fori_loop(0, total // chunk, body, 0)
        leaving = [
            pltpu.make_async_copy(low, low_ref, leave_sems.at[0]), pltpu.make_async_copy(hidden, resid_ref, leave_sems.at[1])
        ]
        for copy in leaving:
            copy.start()
        for b in range(8):
            arrived(out_held.at[b], out_sems.at[b])

        def leave(j):
            at = pl.ds(pl.multiple_of(512 * j, 512), 512)
            return pltpu.make_async_copy(mixed.at[:, at], mixed_ref.at[:, at], leave_sems.at[2 + j])

        def out(j, carry):
            weight = out_held[pl.ds(4 * j, 4)].reshape(512, width)
            mixed[:, pl.ds(pl.multiple_of(512 * j, 512), 512)] = dot_nt(low[...], weight).astype(BF16)
            leave(j).start()
            return carry

        lax.fori_loop(0, 2, out, 0)
        for copy in leaving + [leave(0), leave(1)]:
            copy.wait()

    block = (total, width)
    return call(
        kernel,
        (1,),
        [ANY, ANY, ANY, whole((total, 128)), whole(vecs.shape)] + [ANY] * (len(up) + len(first)),
        [ANY, ANY, ANY, whole((8, width))],
        [sds(block, F32), sds(block, BF16), sds(block, BF16), sds((8, width), F32)],
        [
            pltpu.VMEM((strips, 8, 128, strip), BF16), pltpu.VMEM((strips, total, strip), BF16),
            pltpu.VMEM((8, 128, width), BF16), pltpu.VMEM(block, F32), pltpu.VMEM(block, F32), pltpu.VMEM(block, BF16),
            pltpu.VMEM(block, BF16), DMA((strips, 8)), DMA((strips,)), DMA((8,)), DMA((2,)), DMA((4,)),
        ],
    )(meta, pre, grad_sum, unit_one, inverse_one, vecs, *up, *first)


def attend_back(meta, qkv, mixed, raised, inverse, grad_mixed, grads_one, grads_two, bias_up, batches, rows):
    total, width = grad_mixed.shape
    span = HEADS * HD
    steps = width // span

    def kernel(meta, q_ref, k_ref, v_ref, mixed_ref, g_ref, raised_ref, inv_ref, one_ref, two_ref, up_ref, out_ref, vec_ref, sums):
        batch, step = pl.program_id(0), pl.program_id(1)
        left = lax.broadcasted_iota(jnp.int32, (rows, 128), 1) < HD
        none = jnp.zeros((rows, 128), BF16)

        @pl.when((batch == 0) & (step == 0))
        def _():
            sums[...] = jnp.zeros_like(sums)

        for pair in range(HEADS // 2):
            cols = slice(128 * pair, 128 * (pair + 1))
            query, keyed, value = q_ref[0, :, cols] * jnp.asarray(HD**-0.5, BF16), k_ref[0, :, cols], v_ref[0, :, cols]
            grad = g_ref[:, cols].astype(F32) * inv_ref[:, cols]
            both = grad * mixed_ref[:, cols].astype(F32)
            grad = grad.astype(BF16)
            got = ([], [], [])
            for half in range(2):
                mine = left if half == 0 else jnp.logical_not(left)
                low = raised_ref[0, 2 * pair + half]
                inner = jnp.sum(jnp.where(mine, both, 0.0), -1, keepdims=True)
                slope = dot_nt(jnp.where(mine, grad, none), value) - inner
                scores = (low.astype(F32) * slope).astype(BF16)
                got[0].append(dot_nn(scores, keyed))
                got[1].append(dot_tn(scores, query))
                got[2].append(dot_tn(low, grad))
            for i in range(3):
                part = jnp.where(left, got[i][0], got[i][1])
                if i == 0:
                    part = part * (HD**-0.5)
                part = part.astype(BF16)
                out_ref[i, :, cols] = part
                if i != 1:
                    at = pl.ds(pl.multiple_of(step * span, span) + 128 * pair, 128)
                    sums[i : i + 1, at] += jnp.sum(part.astype(F32), 0, keepdims=True)

        @pl.when((batch == batches - 1) & (step == steps - 1))
        def _():
            vec_ref[...] = jnp.zeros_like(vec_ref)
            rows_of = (
                sums[0:1], sums[2:3], one_ref[2:3], one_ref[0:1], one_ref[1:2], two_ref[2:3], two_ref[0:1], two_ref[1:2]
            )
            table = jnp.concatenate(rows_of, 0).astype(BF16)
            for b in range(8):
                vec_ref[b, 0:8, 0:128] = table[:, 128 * b : 128 * (b + 1)]
                vec_ref[b, 8:9, 0:512] = up_ref[:, 512 * b : 512 * (b + 1)].astype(BF16)

    part = lambda w: spec((1, rows, span), lambda b, h, meta: (w, b, h))
    here = spec((rows, span), lambda b, h, meta: (b, h))
    return call(
        kernel,
        (batches, steps),
        [
            part(0), part(1), part(2), here, here, spec((1, HEADS, rows, rows), lambda b, h, meta: (b, h, 0, 0)), here,
            whole((8, width)), whole((8, width)), whole((1, 4 * width)),
        ],
        [spec((3, rows, span), lambda b, h, meta: (0, b, h)), whole((8, 16, width))],
        [sds((3, total, width), BF16), sds((8, 16, width), BF16)],
        [pltpu.VMEM((8, width), F32)],
    )(meta, qkv, qkv, qkv, mixed, grad_mixed, raised, inverse, grads_one, grads_two, bias_up)


def back_project(meta, grads, first, grad_resid):
    total, width = grad_resid.shape

    def kernel(meta, g_ref, resid_ref, *refs):
        parts, (out_ref, held, resid, made, sems, more, out_sems) = refs[: len(first)], refs[len(first) :]
        fetch(meta, parts, held, sems, 0, 384)
        incoming = pltpu.make_async_copy(resid_ref, resid, more)
        incoming.start()
        incoming.wait()

        def leave(j):
            at = pl.ds(pl.multiple_of(256 * j, 256), 256)
            return pltpu.make_async_copy(made.at[:, at], out_ref.at[:, at], out_sems.at[j])

        def body(j, carry):
            for b in range(2):
                arrived(held.at[2 * j + b], sems.at[2 * j + b])
            at = pl.ds(pl.multiple_of(256 * j, 256), 256)
            part = resid[:, at]
            for w in range(3):
                weight = held[pl.ds(2 * j, 2), 128 * w : 128 * (w + 1)].reshape(256, width)
                part = part + dot_nt(g_ref[w], weight)
            made[:, at] = part.astype(BF16)
            leave(j).start()
            return carry

        lax.fori_loop(0, 4, body, 0)
        for j in range(4):
            leave(j).wait()

    block = (total, width)
    return call(
        kernel,
        (1,),
        [whole((3, total, width)), ANY] + [ANY] * len(first),
        ANY,
        sds(block, BF16),
        [
            pltpu.VMEM((8, 384, width), BF16), pltpu.VMEM(block, F32), pltpu.VMEM(block, BF16), DMA((8,)), DMA(()),
            DMA((4,)),
        ],
    )(meta, grads, grad_resid, *first)


def ship(made, outs, sems, half, i):
    def copy(target):
        return pltpu.make_async_copy(made.at[half, i], target, sems.at[half, i])

    if isinstance(i, int):
        copy(outs[half].at[i] if i < 2 else outs[2 * i - 2 + half]).start()
        return

    @pl.when(i < 2)
    def _():
        copy(outs[half].at[jnp.minimum(i, 1)]).start()

    @pl.when(i == 2)
    def _():
        copy(outs[2 + half]).start()

    @pl.when(i == 3)
    def _():
        copy(outs[4 + half]).start()


def shipped(made, sems):
    for half in range(2):
        for i in range(4):
            arrived(made.at[half, i], sems.at[half, i])


def chip_of(half, i):
    return (i + 2) % 4 if half == 0 else (2 * i + 1) % 5


def six(rows, cols):
    return [sds((2, rows, cols), BF16)] * 2 + [sds((rows, cols), BF16)] * 4


def load_lefts(meta, own_ref, got_ref, lefts, sems, block, total):
    for chip in (2, 3, 1, 0):
        at = pl.ds(pl.multiple_of((meta[0] ^ (2 * chip)) * block, block), block)
        pltpu.make_async_copy(own_ref.at[:, at], lefts.at[chip, pl.ds(0, total)], sems.at[chip]).start()
        pltpu.make_async_copy(got_ref.at[chip], lefts.at[chip, pl.ds(total, total)], sems.at[chip]).start()


def load_right(own, got, target, sem, total):
    pltpu.make_async_copy(own, target.at[pl.ds(0, total)], sem).start()
    pltpu.make_async_copy(got, target.at[pl.ds(total, total)], sem).start()


def down_grad(meta, act, act_got, low, low_got):
    total, width = low.shape
    block, share = 512, width // 2

    def kernel(meta, left_ref, left_got, right_ref, right_got, *refs):
        outs, (lefts, rights, made, left_sems, right_sems, out_sems) = refs[:6], refs[6:]
        for half in range(2):
            at = pl.ds(share * half, share)
            load_right(right_ref.at[:, at], right_got.at[:, at], rights.at[half], right_sems.at[half], total)
            if half == 0:
                load_lefts(meta, left_ref, left_got, lefts, left_sems, block, total)
        for half in range(2):
            arrived(rights.at[half], right_sems.at[half])

            def body(i, carry):
                chip = chip_of(half, i)
                if half == 0:
                    arrived(lefts.at[chip], left_sems.at[chip])
                made[half, i] = dot_tn(lefts[chip], rights[half]).astype(BF16)
                ship(made, outs, out_sems, half, i)
                return carry

            lax.fori_loop(0, 4, body, 0)
        shipped(made, out_sems)

    outs = call(
        kernel,
        (1,),
        [ANY] * 4,
        [ANY] * 6,
        six(block, share),
        [
            pltpu.VMEM((4, 2 * total, block), BF16), pltpu.VMEM((2, 2 * total, share), BF16),
            pltpu.VMEM((2, 4, block, share), BF16), DMA((4,)), DMA((2,)), DMA((2, 4)),
        ],
    )(meta, act, act_got, low, low_got)
    return outs[:2], outs[2:4], outs[4:]


def load_columns(meta, own_ref, got_ref, target, sem, total):
    for chip in range(4):
        at = pl.ds(pl.multiple_of((meta[0] ^ (2 * chip)) * 128, 128), 128)
        cols = pl.ds(128 * chip, 128)
        pltpu.make_async_copy(own_ref.at[:, at], target.at[pl.ds(0, total), cols], sem).start()
        pltpu.make_async_copy(got_ref.at[chip], target.at[pl.ds(total, total), cols], sem).start()


ORDER = ((2, 3, 0, 1), (1, 3, 0, 2))


def up_grad(meta, hidden, hidden_got, pre, pre_got):
    total, width = hidden.shape
    wide = pre.shape[1]
    tile = 1024
    tiles = wide // tile // 2

    def kernel(meta, x_ref, x_got, pre_ref, pre_got, *refs):
        outs, (lefts, rights, made, left_sem, right_sems, out_sems) = refs[:6], refs[6:]
        for t in range(2 * tiles):
            at = pl.ds(tile * t, tile)
            load_right(pre_ref.at[:, at], pre_got.at[:, at], rights.at[t], right_sems.at[t], total)
            if t == 0:
                load_columns(meta, x_ref, x_got.at[1], lefts, left_sem, total)
        arrived(lefts, left_sem)
        for half in range(2):

            def body(t, carry):
                arrived(rights.at[half * tiles + t], right_sems.at[half * tiles + t])
                part = dot_tn(lefts[...], rights[half * tiles + t]).astype(BF16)
                at = pl.ds(pl.multiple_of(t * tile, tile), tile)
                for i, chip in enumerate(ORDER[half]):
                    made[half, i, :, at] = part[128 * chip : 128 * (chip + 1)]
                return carry

            lax.fori_loop(0, tiles, body, 0)
            for i in range(4):
                ship(made, outs, out_sems, half, i)
        shipped(made, out_sems)

    outs = call(
        kernel,
        (1,),
        [ANY] * 4,
        [ANY] * 6,
        six(128, wide // 2),
        [
            pltpu.VMEM((2 * total, 512), BF16), pltpu.VMEM((2 * tiles, 2 * total, tile), BF16),
            pltpu.VMEM((2, 4, 128, wide // 2), BF16), DMA(()), DMA((2 * tiles,)), DMA((2, 4)),
        ],
    )(meta, hidden, hidden_got, pre, pre_got)
    return outs[:2], outs[2:4], outs[4:]


def first_grad(meta, tokens, tokens_got, mixed, mixed_got, grads, grads_got, low, low_got, vec, vec_got):
    total, width = tokens.shape
    share = width // 2

    def kernel(meta, x_ref, x_got, m_ref, m_got, g_ref, g_got, low_ref, low_got, vec_ref, vec_got, *refs):
        outs = refs[:6], refs[6:12]
        lefts, rights, made_a, made_b, short, left_sems, right_sems, sems_a, sems_b, short_sems = refs[12:]
        for w in range(4):
            own, got = (g_ref.at[w], g_got.at[w]) if w < 3 else (low_ref, low_got)
            load_right(own, got, rights.at[w], right_sems.at[w], total)
            if w == 0:
                load_columns(meta, x_ref, x_got, lefts.at[0], left_sems.at[0], total)
                for chip in range(4):
                    at = meta[0] ^ (2 * chip)
                    pltpu.make_async_copy(vec_ref.at[at], short.at[chip, 0], short_sems.at[chip]).start()
                    pltpu.make_async_copy(vec_got.at[at], short.at[chip, 1], short_sems.at[chip]).start()
            if w == 2:
                load_columns(meta, m_ref, m_got.at[0], lefts.at[1], left_sems.at[1], total)
        arrived(lefts.at[0], left_sems.at[0])
        for group, (made, sems) in enumerate(((made_a, sems_a), (made_b, sems_b))):

            def body(k, carry):
                arrived(rights.at[2 * group + k], right_sems.at[2 * group + k])
                if group == 1:

                    @pl.when(k == 1)
                    def _():
                        arrived(lefts.at[1], left_sems.at[1])

                part = dot_tn(lefts[k * group], rights[2 * group + k]).astype(BF16)
                rows = pl.ds(pl.multiple_of(128 * k, 128), 128)
                for half in range(2):
                    for i, chip in enumerate(ORDER[half]):
                        made[half, i, rows] = part[128 * chip : 128 * (chip + 1), share * half : share * (half + 1)]
                return carry

            lax.fori_loop(0, 2, body, 0)
            if group == 1:
                for i, chip in enumerate(ORDER[0]):
                    arrived(short.at[chip], short_sems.at[chip])
                    both = short[chip, 0].astype(F32) + short[chip, 1].astype(F32)
                    made[0, i, 256:] = both[:, :share].astype(BF16)
                    made[1, i, 256:] = jnp.zeros((16, share), BF16)
            for half in range(2):
                for i in range(4):
                    ship(made, outs[group], sems, half, i)
        shipped(made_a, sems_a)
        shipped(made_b, sems_b)

    outs = call(
        kernel,
        (1,),
        [ANY] * 10,
        [ANY] * 12,
        six(256, share) + six(272, share),
        [
            pltpu.VMEM((2, 2 * total, 512), BF16), pltpu.VMEM((4, 2 * total, width), BF16),
            pltpu.VMEM((2, 4, 256, share), BF16), pltpu.VMEM((2, 4, 272, share), BF16),
            pltpu.VMEM((4, 2, 16, width), BF16), DMA((2,)), DMA((4,)), DMA((2, 4)), DMA((2, 4)), DMA((4,)),
        ],
    )(meta, tokens, tokens_got, mixed, mixed_got, grads, grads_got, low, low_got, vec, vec_got)
    return [(some[:2], some[2:4], some[4:]) for some in (outs[:6], outs[6:])]


def pack(weights, small):
    block, width = weights[0].shape
    high = block * len(weights) + 16

    def kernel(*refs):
        out_ref = refs[-1]
        for i in range(len(weights)):
            out_ref[block * i : block * (i + 1)] = refs[i][...]
        out_ref[block * len(weights) :] = jnp.zeros((16, width), BF16)
        start = 0
        for ref in refs[len(weights) : -1]:
            count = ref.shape[1]
            row, column = block * len(weights) + start // width, start % width
            out_ref[row : row + 1, column : column + count] = ref[...]
            start += count

    return pl.pallas_call(
        kernel,
        out_shape=jax.ShapeDtypeStruct((high, width), BF16),
        compiler_params=pltpu.CompilerParams(vmem_limit_bytes=VMEM),
        cost_estimate=pl.CostEstimate(flops=1024, bytes_accessed=1024, transcendentals=0),
    )(*weights, *[part.reshape(1, -1) for part in small])


CORE, ALONG_X, ALONG_Y = 1, 2, 4


def swap(value, mask):
    return lax.ppermute(value, "shard", [(i, i ^ mask) for i in range(8)])


def plus(*parts):
    total = parts[0].astype(F32)
    for part in parts[1:]:
        total = total + part.astype(F32)
    return total.astype(BF16)


class Order:
    def __init__(self, meta):
        self.meta = meta

    def place(self, *values):
        *values, self.meta = lax.optimization_barrier(values + (self.meta,))
        return values

    def then(self, value):
        self.meta, value = lax.optimization_barrier((self.meta, value))
        return value

    def run(self, function, *values):
        return self.then(function(*self.place(*values)))


def tie(*values):
    return lax.optimization_barrier(values)


def both_cores(*mine):
    return mine + tuple(swap(part, CORE) for part in mine)


def pairs(value, mask):
    return lax.ppermute(value, "rep", [(i, i ^ mask) for i in range(4)])


def turned(rest, got):
    return plus(rest[0], got[0][1]), plus(rest[1], got[1][1])


def passed(values):
    return swap(values[0], ALONG_X), swap(values[1], ALONG_Y)


def sent(values):
    return swap(values[0], ALONG_Y), swap(values[1], ALONG_X)


def summed(own, got, late):
    odd = lax.axis_index("rep") % 2 == 1
    first, second = plus(own[0], got[0][0], late[0]), plus(own[1], got[1][0], late[1])
    return jnp.where(odd, second, first), jnp.where(odd, first, second)


def unfolded(mine, other):
    odd = lax.axis_index("rep") % 2 == 1
    return jnp.where(odd, other, mine).astype(F32), jnp.where(odd, mine, other).astype(F32)


def local_eight(
    inputs, lengths, dealing, w_query, w_key, w_value, w_out, b_query, b_value, b_out,
    ln1_gain, ln1_bias, w_up, b_up, w_down, b_down, ln2_gain, ln2_bias, cotangent,
):
    batches, rows, width = inputs.shape
    wide = w_up.shape[1]
    total = batches * rows
    group = batches * 4
    shard_index = lax.axis_index("shard")
    anchor = shard_index * group
    slots = anchor + lax.axis_index("rep") * batches + jnp.arange(batches, dtype=jnp.int32)
    local_dealing = lax.dynamic_slice_in_dim(dealing, anchor, group) - anchor
    sources = jnp.take(dealing, slots) - anchor
    places = jnp.arange(group, dtype=jnp.int32)
    wanted = jnp.sum(
        jnp.where(local_dealing[None, :] == (slots - anchor)[:, None], places[None, :], 0), 1
    )
    meta = jnp.concatenate([shard_index[None].astype(jnp.int32), jnp.take(lengths, slots), wanted])
    order = Order(meta)
    tokens = inputs.reshape(total, width)

    small = (b_query, b_value, b_out, ln1_gain, ln1_bias, b_down, ln2_gain, ln2_bias, b_up)
    own_first = pack((w_query, w_key, w_value, w_out), small)
    first_x, first_y = swap(own_first, ALONG_X), swap(own_first, ALONG_Y)
    first_x, first_y, to_both = order.then((first_x, first_y, w_up))
    first_far, up_x = swap(first_x, ALONG_Y), swap(to_both, ALONG_X)
    first_c = [swap(part, CORE) for part in (own_first, first_x, first_y)]
    first_far, up_x, to_x, to_y, *first_c = order.then((first_far, up_x, w_down, w_up, *first_c))
    first = (own_first, first_x, first_y, first_far, *first_c, swap(first_far, CORE))
    up_y, down_x = swap(to_y, ALONG_Y), swap(to_x, ALONG_X)
    up_c = [swap(part, CORE) for part in (w_up, up_x)]
    cot_pool = lax.all_gather(cotangent, "rep", axis=0, tiled=True)
    qkv, vecs, bias_up, tokens_give = order.then(project(order.meta, tokens, first))
    mixed, raised, inverse = order.then(attend(order.meta, qkv, batches, rows))
    up_y, down_x, tokens_give, to_y, *up_c = order.then((up_y, down_x, tokens_give, w_down, *up_c))
    up_far, down_y = swap(up_y, ALONG_X), swap(to_y, ALONG_Y)
    up_c.append(swap(up_y, CORE))
    tokens_got = swap(tokens_give, CORE)
    unit_one, inverse_one, hidden_low, both_give = order.then(mix_out(order.meta, mixed, tokens, first, vecs))
    up_far, down_y, tokens_got, both_give, *up_c = order.then((up_far, down_y, tokens_got, both_give, *up_c))
    up = (w_up, up_x, up_y, up_far, *up_c, swap(up_far, CORE))
    down_top, down_end = swap(down_x[:256], ALONG_Y), swap(down_y[256:], ALONG_X)
    up = order.then(up)
    down_c = [swap(part, CORE) for part in (w_down, down_x, down_y)]
    act, slope, act_give = order.then(feed_up(order.meta, hidden_low, up, bias_up))
    down_top, down_end, act_give, both_give, *down_c = order.then((down_top, down_end, act_give, both_give, *down_c))
    down = (w_down, down_x, down_y, down_top, down_end) + tuple(down_c)
    down += tuple(swap(part, CORE) for part in (down_top, down_end))
    *down, act_give, both_give = order.then((*down, act_give, both_give))
    act_got, both_got = swap(act_give, CORE), swap(both_give, CORE)
    out, grad_sum, sum_low, grads_two, pre, grad_bias_up = order.then(
        feed_down(order.meta, act, slope, down, unit_one, cot_pool, vecs, batches, rows)
    )
    sum_got = swap(sum_low, CORE)
    out, act_got, both_got, sum_got, pre = order.then((out, act_got, both_got, sum_got, pre))
    pre_got = swap(pre, CORE)
    out_pool = lax.all_gather(out.reshape(batches, rows, width), "rep", axis=0, tiled=True)
    far_down, own_down, rest_down = order.then(down_grad(order.meta, act, act_got, sum_low, sum_got))
    pre_got, far_down = order.then((pre_got, far_down))
    got_down = sent(far_down)
    grad_resid, resid_low, grad_mixed, grads_one = order.then(
        back_up(order.meta, pre, up, first, grad_sum, unit_one, inverse_one, vecs)
    )
    far_up, own_up, rest_up = order.then(up_grad(order.meta, hidden_low, both_got, pre, pre_got))
    got_down, far_up, resid_low = order.then((got_down, far_up, resid_low))
    got_up = sent(far_up)
    late_down = passed(order.then(turned(rest_down, got_down)))
    grads, vec = order.then(
        attend_back(
            order.meta, qkv, mixed, raised, inverse, grad_mixed, grads_one, grads_two, grad_bias_up, batches, rows
        )
    )
    grad_input = order.then(back_project(order.meta, grads, first, grad_resid))
    got_up, late_down, resid_low, grads, vec = order.then((got_up, late_down, resid_low, grads, vec))
    resid_got, grads_got, vec_got = swap(resid_low, CORE), swap(grads, CORE), swap(vec, CORE)
    pass_up = order.then(turned(rest_up, got_up))
    kept_down, given_down = order.then(summed(own_down, got_down, late_down))
    resid_got, grads_got, vec_got, pass_up, given_down = order.then((resid_got, grads_got, vec_got, pass_up, given_down))
    late_up, taken_down = passed(pass_up), pairs(given_down, 1)
    (far_a, own_a, rest_a), (far_b, own_b, rest_b) = order.then(
        first_grad(
            order.meta, tokens, tokens_got, mixed, both_got, grads, grads_got, resid_low, resid_got, vec, vec_got
        )
    )
    late_up, taken_down, far_a, out_pool = order.then((late_up, taken_down, far_a, out_pool))
    got_a = sent(far_a)
    far_b, half_down = order.then((far_b, plus(kept_down, taken_down)))
    got_b = sent(far_b)
    over_down = pairs(half_down, 2)
    kept_up, given_up = order.then(summed(own_up, got_up, late_up))
    got_a = order.then(got_a)
    late_a = passed(order.then(turned(rest_a, got_a)))
    taken_up = pairs(given_up, 1)
    layer_out = order.then(pick(out_pool, sources))
    got_b = order.then(got_b)
    late_b = passed(order.then(turned(rest_b, got_b)))
    late_a = order.then(late_a)
    kept_a, given_a = order.then(summed(own_a, got_a, late_a))
    taken_a = pairs(given_a, 1)
    over_down, taken_up = order.then((over_down, taken_up))
    total_down, half_up = order.then((plus(half_down, over_down), plus(kept_up, taken_up)))
    late_b = order.then(late_b)
    kept_b, given_b = order.then(summed(own_b, got_b, late_b))
    taken_b = pairs(given_b, 1)
    taken_a = order.then(taken_a)
    half_a = order.then(plus(kept_a, taken_a))
    over_a = pairs(half_a, 2)
    over_up, other_down = pairs(half_up, 2), pairs(total_down, 1)
    taken_b = order.then(taken_b)
    half_b = order.then(plus(kept_b, taken_b))
    over_b = pairs(half_b, 2)
    over_a = order.then(over_a)
    total_a = order.then(plus(half_a, over_a))
    other_a = pairs(total_a, 1)
    over_up, other_down = order.then((over_up, other_down))
    total_up = order.then(plus(half_up, over_up))
    other_up = pairs(total_up, 1)
    g_down = order.then(jnp.concatenate(unfolded(total_down, other_down), 1))
    over_b = order.then(over_b)
    total_b = order.then(plus(half_b, over_b))
    other_b = pairs(total_b, 1)
    other_a, other_up = order.then((other_a, other_up))
    g_up = order.then(jnp.concatenate(unfolded(total_up, other_up), 1))
    g_a = order.then(jnp.concatenate(unfolded(total_a, other_a), 1))
    left, right = unfolded(total_b, other_b)
    g_b = jnp.concatenate([left[:256], right[:256]], 1)
    line = lambda i: left[256 + i, :128]
    return (
        layer_out, grad_input.reshape(batches, rows, width),
        g_a[0:128], g_a[128:256], g_b[0:128], g_b[128:256],
        line(0), line(1), line(2), line(3), line(4),
        g_up, left[264, :512], g_down, line(5), line(6), line(7),
    )


def pick(pool, targets):
    return jnp.stack(
        [lax.dynamic_index_in_dim(pool, targets[i], 0, keepdims=False) for i in range(targets.shape[0])]
    )


def local_general(
    inputs, lengths, dealing, w_query, w_key, w_value, w_out, b_query, b_value, b_out,
    ln1_gain, ln1_bias, w_up, b_up, w_down, b_down, ln2_gain, ln2_bias, cotangent,
):
    batches, rows, width = inputs.shape
    shards = lax.axis_size("shard")
    replicas = lax.axis_size("rep")
    group = batches * replicas
    shard_index = lax.axis_index("shard")
    rep_index = lax.axis_index("rep")
    anchor = shard_index * group
    slots = anchor + rep_index * batches + jnp.arange(batches, dtype=jnp.int32)
    seq_lengths = jnp.take(lengths, slots)
    local_dealing = lax.dynamic_slice_in_dim(dealing, anchor, group) - anchor
    sources = jnp.take(dealing, slots) - anchor
    places = jnp.arange(group, dtype=jnp.int32)
    wanted = jnp.sum(
        jnp.where(local_dealing[None, :] == (slots - anchor)[:, None], places[None, :], 0), 1
    )

    def gather(block):
        return lax.all_gather(block, "shard", axis=0, tiled=True)

    block = w_query.shape[0]
    wide = w_up.shape[1]
    small = (b_query, b_value, b_out, ln1_gain, ln1_bias, b_down, ln2_gain, ln2_bias, b_up)
    vec = jnp.concatenate(small)
    first = jnp.concatenate([w_query, w_key, w_value, w_out], 0)
    all_vec = lax.all_gather(vec, "shard", axis=0, tiled=True).reshape(shards, -1)
    all_first = gather(first).reshape(shards, 4, block, width)
    cuts = [0]
    for part in small:
        cuts.append(cuts[-1] + part.shape[0])
    (bias_query, bias_value, bias_out, gain_one, shift_one, bias_down, gain_two, shift_two, bias_up) = [
        all_vec[:, cuts[i] : cuts[i + 1]].reshape(-1).astype(F32) for i in range(len(small))
    ]
    full_query, full_key, full_value, full_out = [
        all_first[:, i].reshape(width, width) for i in range(4)
    ]
    full_up = gather(w_up)
    full_down = gather(w_down)
    cot = pick(lax.all_gather(cotangent, "rep", axis=0, tiled=True), wanted)

    tokens = inputs.reshape(batches * rows, width)
    query = (matmul(tokens, full_query) + bias_query).astype(BF16)
    keyed = matmul(tokens, full_key).astype(BF16)
    value = (matmul(tokens, full_value) + bias_value).astype(BF16)
    heads = lambda a: a.reshape(batches, rows, H, HD).transpose(0, 2, 1, 3)
    flat = lambda a: a.transpose(0, 2, 1, 3).reshape(batches * rows, width)
    qh, kh, vh = heads(query), heads(keyed), heads(value)
    allowed = lax.broadcasted_iota(jnp.int32, (batches, 1, 1, rows), 3) < seq_lengths[:, None, None, None]
    scale = HD ** (-0.5)
    scores = jnp.einsum("bhqd,bhkd->bhqk", qh, kh, preferred_element_type=F32) * scale
    scores = jnp.where(allowed, scores, NEG)
    raised = jnp.exp(scores - jnp.max(scores, -1, keepdims=True))
    probs = raised / jnp.sum(raised, -1, keepdims=True)
    probs_low = probs.astype(BF16)
    mixed_low = flat(jnp.einsum("bhqk,bhkd->bhqd", probs_low, vh, preferred_element_type=F32).astype(BF16))
    hidden, unit_one, inverse_one = normalize(
        tokens.astype(F32) + matmul(mixed_low, full_out) + bias_out, gain_one, shift_one
    )
    hidden_low = hidden.astype(BF16)
    pre = matmul(hidden_low, full_up) + bias_up
    act, slope = gelu_both(pre)
    act_low = act.astype(BF16)
    summed = hidden + matmul(act_low, full_down) + bias_down
    normed, unit_two, inverse_two = normalize(summed, gain_two, shift_two)
    valid = (lax.broadcasted_iota(jnp.int32, (batches, rows, 1), 1) < seq_lengths[:, None, None]).reshape(-1, 1)
    out = jnp.where(valid, normed, 0.0).astype(BF16).reshape(batches, rows, width)
    layer_out = pick(lax.all_gather(out, "rep", axis=0, tiled=True), sources)

    grad_out = jnp.where(valid, cot.reshape(-1, width).astype(F32), 0.0)
    grad_gain_two = jnp.sum(grad_out * unit_two, 0)
    grad_shift_two = jnp.sum(grad_out, 0)
    grad_sum = norm_back(grad_out, unit_two, inverse_two, gain_two)
    grad_bias_down = jnp.sum(grad_sum, 0)
    grad_sum_low = grad_sum.astype(BF16)

    def reduced(part):
        return lax.psum_scatter(part, "shard", scatter_dimension=0, tiled=True)

    def over_rep(part):
        return lax.psum(part, "rep").astype(F32)

    g_down = reduced(left_trans(act_low, grad_sum_low).astype(BF16))
    grad_pre = (right_trans(grad_sum_low, full_down) * slope).astype(BF16)
    grad_bias_up = jnp.sum(grad_pre.astype(F32), 0)
    g_up = reduced(left_trans(hidden_low, grad_pre).astype(BF16))
    grad_hidden = grad_sum + right_trans(grad_pre, full_up)
    grad_gain_one = jnp.sum(grad_hidden * unit_one, 0)
    grad_shift_one = jnp.sum(grad_hidden, 0)
    grad_resid = norm_back(grad_hidden, unit_one, inverse_one, gain_one)
    grad_bias_out = jnp.sum(grad_resid, 0)
    grad_resid_low = grad_resid.astype(BF16)
    grad_w_out = left_trans(mixed_low, grad_resid_low).astype(BF16)
    grad_mixed = heads(right_trans(grad_resid_low, full_out).astype(BF16))
    grad_probs = jnp.einsum("bhqd,bhkd->bhqk", grad_mixed, vh, preferred_element_type=F32)
    inner = jnp.sum(probs * grad_probs, -1, keepdims=True)
    grad_scores = (probs * (grad_probs - inner) * scale).astype(BF16)
    query_low = flat(jnp.einsum("bhqk,bhkd->bhqd", grad_scores, kh, preferred_element_type=F32).astype(BF16))
    key_low = flat(jnp.einsum("bhqk,bhqd->bhkd", grad_scores, qh, preferred_element_type=F32).astype(BF16))
    value_low = flat(jnp.einsum("bhqk,bhqd->bhkd", probs_low, grad_mixed, preferred_element_type=F32).astype(BF16))
    grad_bias_query = jnp.sum(query_low.astype(F32), 0)
    grad_bias_value = jnp.sum(value_low.astype(F32), 0)
    blocks = [
        part.reshape(shards, block, width)
        for part in (
            left_trans(tokens, query_low).astype(BF16),
            left_trans(tokens, key_low).astype(BF16),
            left_trans(tokens, value_low).astype(BF16),
            grad_w_out,
        )
    ]
    g_first = reduced(jnp.concatenate(blocks, 1).reshape(shards * 4 * block, width))
    grad_tokens = (
        grad_resid
        + right_trans(query_low, full_query)
        + right_trans(key_low, full_key)
        + right_trans(value_low, full_value)
    )
    grad_input = grad_tokens.astype(BF16).reshape(batches, rows, width)
    vec_terms = (
        grad_bias_query, grad_bias_value, grad_bias_out, grad_gain_one, grad_shift_one,
        grad_bias_down, grad_gain_two, grad_shift_two, grad_bias_up,
    )
    g_vec = jnp.concatenate([part.reshape(shards, -1) for part in vec_terms], 1)
    g_vec = lax.psum(g_vec, ("shard", "rep"))
    g_vec = lax.dynamic_index_in_dim(g_vec, shard_index, 0, keepdims=False)
    (g_bquery, g_bvalue, g_bout, g_gain_one, g_shift_one, g_bdown, g_gain_two, g_shift_two, g_bup) = [
        g_vec[cuts[i] : cuts[i + 1]] for i in range(len(small))
    ]
    g_down = over_rep(g_down)
    g_up = over_rep(g_up)
    g_first = over_rep(g_first).reshape(4, block, width)
    return (
        layer_out, grad_input, g_first[0], g_first[1], g_first[2], g_first[3],
        g_bquery, g_bvalue, g_bout, g_gain_one, g_shift_one,
        g_up, g_bup, g_down, g_bdown, g_gain_two, g_shift_two,
    )


def solution(mesh):
    seqs = P(("shard", "rep"), None, None)
    mat = P("shard", None)
    vec = P("shard")
    in_specs = (
        seqs, P(), P(), mat, mat, mat, mat, vec, vec, vec, vec, vec, mat, vec, mat, vec, vec, vec, seqs,
    )
    out_specs = (
        seqs, seqs, mat, mat, mat, mat, vec, vec, vec, vec, vec, mat, vec, mat, vec, vec, vec,
    )
    shape = dict(mesh.shape)
    local = local_eight if shape["shard"] == 8 and shape["rep"] == 4 else local_general
    return jax.shard_map(local, mesh=mesh, in_specs=in_specs, out_specs=out_specs, check_vma=False)
```

```python
import math

import jax
import jax.numpy as jnp
from jax import lax
from jax.experimental import pallas as pl
from jax.experimental.pallas import tpu as pltpu
from jax.sharding import PartitionSpec as P

H = 16
HD = 64
EPS = 1e-05
NEG = -1e30
F32 = jnp.float32
BF16 = jnp.bfloat16


def matmul(left, right):
    return jnp.dot(left, right, preferred_element_type=F32)


def left_trans(left, right):
    return lax.dot_general(left, right, (((0,), (0,)), ((), ())), preferred_element_type=F32)


def right_trans(left, right):
    return lax.dot_general(left, right, (((1,), (1,)), ((), ())), preferred_element_type=F32)


def normalize(values, gain, shift):
    center = values - jnp.mean(values, -1, keepdims=True)
    inverse = lax.rsqrt(jnp.mean(center * center, -1, keepdims=True) + EPS)
    unit = center * inverse
    return (unit * gain + shift, unit, inverse)


def norm_back(grad, unit, inverse, gain):
    scaled = grad * gain
    return inverse * (
        scaled
        - jnp.mean(scaled, -1, keepdims=True)
        - unit * jnp.mean(scaled * unit, -1, keepdims=True)
    )


def gelu_both(pre):
    cumul = 0.5 * (1.0 + lax.erf(pre * 0.7071067811865476))
    density = jnp.exp(-0.5 * pre * pre) * 0.3989422804014327
    return (pre * cumul, cumul + pre * density)


VMEM = 56 * 1024 * 1024
TIGHT = ()
ANY = pl.BlockSpec(memory_space=pl.ANY)
DMA = pltpu.SemaphoreType.DMA


def spec(shape, index):
    return pl.BlockSpec(shape, index)


def whole(shape):
    zeros = (0,) * len(shape)
    return pl.BlockSpec(shape, lambda *_: zeros)


def sds(shape, dtype):
    return jax.ShapeDtypeStruct(shape, dtype)


def room(specs, shapes, scratch):
    total = 8 * 1024 * 1024
    for block, shape in zip(specs, shapes):
        if block.block_shape is not None:
            total += 2 * math.prod(block.block_shape) * shape.dtype.itemsize
    for item in scratch:
        if item.memory_space == pltpu.VMEM:
            total += math.prod(item.shape) * jnp.dtype(item.dtype).itemsize
    return total


def call(kernel, grid, in_specs, out_specs, out_shape, scratch):
    def run(*args):
        outs = out_shape if isinstance(out_shape, (list, tuple)) else [out_shape]
        specs = out_specs if isinstance(out_specs, (list, tuple)) else [out_specs]
        limit = VMEM
        if kernel.__qualname__.split(".")[0] in TIGHT:
            limit = room(list(in_specs) + list(specs), list(args[1:]) + list(outs), scratch)
        return pl.pallas_call(
            kernel,
            grid_spec=pltpu.PrefetchScalarGridSpec(
                num_scalar_prefetch=1,
                grid=grid,
                in_specs=in_specs,
                out_specs=out_specs,
                scratch_shapes=list(scratch),
            ),
            out_shape=out_shape,
            compiler_params=pltpu.CompilerParams(vmem_limit_bytes=limit),
            cost_estimate=pl.CostEstimate(flops=1024, bytes_accessed=1024, transcendentals=0),
        )(*args)

    return run


def dot_nn(a, b):
    return lax.dot_general(a, b, (((1,), (0,)), ((), ())), preferred_element_type=F32)


def dot_nt(a, b):
    return lax.dot_general(a, b, (((1,), (1,)), ((), ())), preferred_element_type=F32)


def dot_tn(a, b):
    return lax.dot_general(a, b, (((0,), (0,)), ((), ())), preferred_element_type=F32)


def fetch(meta, parts, target, sems, low, high, columns=None):
    cut = parts[3].shape[0]
    each = len(parts) // 2
    for core in range(2):
        for chip in range(4):
            at = meta[0] ^ (2 * chip + core)
            if chip < 3:
                pieces = [(parts[each * core + chip], low, high, 0)]
            else:
                pieces = []
                if low < cut:
                    pieces.append((parts[each * core + 3], low, min(high, cut), 0))
                if high > cut:
                    start = max(low, cut)
                    pieces.append((parts[each * core + 4], start - cut, high - cut, start - low))
            for ref, begin, end, offset in pieces:
                source = ref.at[pl.ds(begin, end - begin)]
                if columns is not None:
                    source = ref.at[pl.ds(begin, end - begin), columns]
                goal = target.at[at]
                if len(pieces) > 1:
                    goal = target.at[at, pl.ds(offset, end - begin)]
                pltpu.make_async_copy(source, goal, sems.at[at]).start()


def arrived(target, sem):
    pltpu.make_async_copy(target, target, sem).wait()


def hand_over(meta, source, target, sems, block):
    copies = []
    for chip in range(4):
        at = pl.ds(pl.multiple_of((meta[0] ^ (2 * chip + 1)) * block, block), block)
        copies.append(pltpu.make_async_copy(source.at[:, at], target.at[chip], sems.at[chip]))
        copies[-1].start()
    return copies


def project(meta, tokens, first):
    rows, width = tokens.shape
    tile = 512
    count = width // tile

    def kernel(meta, x_ref, *refs):
        parts, (out_ref, vec_ref, up_ref, give_ref, held, short, made, sems, short_sems, out_sems, give_sems) = refs[: len(first)], refs[len(first) :]
        for w in range(3):
            fetch(meta, parts, held.at[w], sems.at[w], 128 * w, 128 * (w + 1))
            if w == 0:
                fetch(meta, parts, short, short_sems, 512, 528)
        gifts = hand_over(meta, x_ref, give_ref, give_sems, 128)
        for b in range(8):
            arrived(short.at[b], short_sems.at[b])
        for b in range(8):
            two = short[b].astype(F32)
            for v in range(8):
                vec_ref[v : v + 1, 128 * b : 128 * (b + 1)] = two[0:1, 128 * v : 128 * (v + 1)]
            up_ref[0:1, 512 * b : 512 * (b + 1)] = two[1:2, :512]

        def body(i, carry):
            w, n = i // count, i % count

            @pl.when(n == 0)
            def _():
                for b in range(8):
                    arrived(held.at[w, b], sems.at[w, b])

            at = pl.ds(pl.multiple_of(n * tile, tile), tile)
            weight = held[w, :, :, at].reshape(width, tile)
            bias = jnp.where(w == 0, vec_ref[0:1, at], vec_ref[1:2, at])
            bias = jnp.where(w == 1, jnp.zeros_like(bias), bias)
            made[w, :, at] = (dot_nn(x_ref[...], weight) + bias).astype(BF16)

            @pl.when(n == count - 1)
            def _():
                pltpu.make_async_copy(made.at[w], out_ref.at[w], out_sems.at[w]).start()

            return carry

        lax.fori_loop(0, 3 * count, body, 0)
        for w in range(3):
            pltpu.make_async_copy(made.at[w], out_ref.at[w], out_sems.at[w]).wait()
        for copy in gifts:
            copy.wait()

    return call(
        kernel,
        (1,),
        [whole((rows, width))] + [ANY] * len(first),
        [ANY, whole((8, width)), whole((1, 4 * width)), ANY],
        [sds((3, rows, width), BF16), sds((8, width), F32), sds((1, 4 * width), F32), sds((4, rows, 128), BF16)],
        [
            pltpu.VMEM((3, 8, 128, width), BF16), pltpu.VMEM((8, 16, width), BF16),
            pltpu.VMEM((3, rows, width), BF16), DMA((3, 8)), DMA((8,)), DMA((3,)), DMA((4,)),
        ],
    )(meta, tokens, *first)


HEADS = 4


def attend(meta, qkv, batches, rows):
    total, width = qkv.shape[1:]
    span = HEADS * HD
    steps = width // span

    def kernel(meta, q_ref, k_ref, v_ref, mixed_ref, raised_ref, inverse_ref):
        length = meta[1 + pl.program_id(0)]
        allowed = lax.broadcasted_iota(jnp.int32, (1, rows), 1) < length
        shift = jnp.where(allowed, 0.0, NEG)
        left = lax.broadcasted_iota(jnp.int32, (rows, 128), 1) < HD
        one = jnp.ones((rows, 128), BF16)
        for pair in range(HEADS // 2):
            cols = slice(128 * pair, 128 * (pair + 1))
            query, keyed, value = q_ref[0, :, cols] * jnp.asarray(HD**-0.5, BF16), k_ref[0, :, cols], v_ref[0, :, cols]
            outs = []
            for half in range(2):
                mine = left if half == 0 else jnp.logical_not(left)
                scores = dot_nt(jnp.where(mine, query, jnp.zeros_like(query)), keyed) + shift
                raised = jnp.exp(scores - jnp.max(scores, -1, keepdims=True)).astype(BF16)
                raised_ref[0, 2 * pair + half] = raised
                outs.append(dot_nn(raised, jnp.where(mine, value, one)))
            inverse = 1.0 / pltpu.roll(jnp.where(left, outs[1], outs[0]), HD, 1)
            inverse_ref[:, cols] = inverse
            mixed_ref[:, cols] = (jnp.where(left, outs[0], outs[1]) * inverse).astype(BF16)

    part = lambda w: spec((1, rows, span), lambda b, h, meta: (w, b, h))
    here = spec((rows, span), lambda b, h, meta: (b, h))
    return call(
        kernel,
        (batches, steps),
        [part(0), part(1), part(2)],
        [here, spec((1, HEADS, rows, rows), lambda b, h, meta: (b, h, 0, 0)), here],
        [sds((total, width), BF16), sds((batches, H, rows, rows), BF16), sds((total, width), F32)],
        [],
    )(meta, qkv, qkv, qkv)


def mix_out(meta, mixed, tokens, first, vecs):
    total, width = mixed.shape
    tile = 128

    def kernel(meta, mixed_ref, tokens_ref, vec_ref, *refs):
        parts, (unit_ref, inv_ref, low_ref, give_ref, held, sems, give_sems) = refs[: len(first)], refs[len(first) :]
        fetch(meta, parts, held, sems, 384, 512)
        gifts = hand_over(meta, mixed_ref, give_ref.at[0], give_sems.at[0], 128)
        for b in range(8):
            arrived(held.at[b], sems.at[b])

        def body(i, carry):
            here = pl.ds(pl.multiple_of(i * tile, tile), tile)
            branch = dot_nn(mixed_ref[here], held[...].reshape(width, width)) + vec_ref[2:3]
            hidden, unit, inverse = normalize(tokens_ref[here].astype(F32) + branch, vec_ref[3:4], vec_ref[4:5])
            unit_ref[here] = unit
            inv_ref[here] = jnp.broadcast_to(inverse, (tile, 128))
            low_ref[here] = hidden.astype(BF16)
            return carry

        lax.fori_loop(0, total // tile, body, 0)
        gifts += hand_over(meta, low_ref, give_ref.at[1], give_sems.at[1], 128)
        for copy in gifts:
            copy.wait()

    block = (total, width)
    return call(
        kernel,
        (1,),
        [whole(block), whole(block), whole(vecs.shape)] + [ANY] * len(first),
        [whole(block), whole((total, 128)), whole(block), ANY],
        [sds(block, F32), sds((total, 128), F32), sds(block, BF16), sds((2, 4, total, 128), BF16)],
        [pltpu.VMEM((8, 128, width), BF16), DMA((8,)), DMA((2, 4))],
    )(meta, mixed, tokens, vecs, *first)


def feed_up(meta, low, up, bias):
    total, width = low.shape
    wide = up[0].shape[1]
    strip, tile = 1024, 512
    strips, inner = wide // strip, strip // tile

    def kernel(meta, x_ref, bias_ref, *refs):
        parts, (act_ref, slope_ref, give_ref, held, act, slope, sems, out_sems, give_sems) = refs[: len(up)], refs[len(up) :]
        for t in range(strips):
            fetch(meta, parts, held.at[t], sems.at[t], 0, 128, pl.ds(strip * t, strip))

        def leave(i):
            at = pl.ds(pl.multiple_of(i * tile, tile), tile)
            return (
                pltpu.make_async_copy(act.at[i], act_ref.at[:, at], out_sems.at[0, i]),
                pltpu.make_async_copy(slope.at[i], slope_ref.at[:, at], out_sems.at[1, i]),
            )

        def body(i, carry):
            t, n = i // inner, i % inner

            @pl.when(n == 0)
            def _():
                for b in range(8):
                    arrived(held.at[t, b], sems.at[t, b])

            weight = held[t, :, :, pl.ds(pl.multiple_of(n * tile, tile), tile)].reshape(width, tile)
            pre = dot_nn(x_ref[...], weight) + bias_ref[:, pl.ds(pl.multiple_of(i * tile, tile), tile)]
            value, grad = gelu_both(pre)
            act[i] = value.astype(BF16)
            slope[i] = grad.astype(BF16)
            for copy in leave(i):
                copy.start()
            code = meta[0] ^ i

            @pl.when(code % 2 == 1)
            def _():
                pltpu.make_async_copy(act.at[i], give_ref.at[code // 2], give_sems.at[code // 2]).start()

            return carry

        lax.fori_loop(0, strips * inner, body, 0)
        for i in range(strips * inner):
            for copy in leave(i):
                copy.wait()
        for chip in range(4):
            arrived(give_ref.at[chip], give_sems.at[chip])

    out = sds((total, wide), BF16)
    tiles = wide // tile
    return call(
        kernel,
        (1,),
        [whole((total, width)), whole((1, wide))] + [ANY] * len(up),
        [ANY, ANY, ANY],
        [out, out, sds((4, total, tile), BF16)],
        [
            pltpu.VMEM((strips, 8, 128, strip), BF16), pltpu.VMEM((tiles, total, tile), BF16),
            pltpu.VMEM((tiles, total, tile), BF16), DMA((strips, 8)), DMA((2, tiles)), DMA((4,)),
        ],
    )(meta, low, bias, *up)


def feed_down(meta, act, slope, down, unit_one, cot_pool, vecs, batches, rows):
    total, wide = act.shape
    width = down[0].shape[1]
    chunk = 128

    def kernel(meta, act_ref, slope_ref, unit_ref, cot_ref, vec_ref, *refs):
        parts = refs[: len(down)]
        (
            out_ref, sum_ref, low_ref, grad_ref, pre_ref, bias_ref, out, grad_sums, low, early,
            held, left, right, total_ref, unit, cot, sems, left_sems, right_sems, out_sems, more,
        ) = refs[len(down) :]
        for b in range(8):
            pltpu.make_async_copy(act_ref.at[:, pl.ds(512 * b, 512)], left.at[b], left_sems.at[b]).start()
        fetch(meta, parts, held, sems, 0, 512)
        rest = [pltpu.make_async_copy(unit_ref, unit, more.at[0])] + [
            pltpu.make_async_copy(cot_ref.at[meta[3 + i]], cot.at[i], more.at[1 + i]) for i in range(batches)
        ]
        for copy in rest:
            copy.start()
        for b in range(8):
            pltpu.make_async_copy(slope_ref.at[:, pl.ds(512 * b, 512)], right.at[b], right_sems.at[b]).start()

        def add(b, carry):
            arrived(left.at[b], left_sems.at[b])
            arrived(held.at[b], sems.at[b])
            part = dot_nn(left[b], held[b])

            @pl.when(b == 0)
            def _():
                total_ref[...] = part

            @pl.when(b > 0)
            def _():
                total_ref[...] += part

            return carry

        lax.fori_loop(0, 8, add, 0)
        for copy in rest:
            copy.wait()
        grad_ref[...] = jnp.zeros_like(grad_ref)

        def body(i, carry):
            here = pl.ds(pl.multiple_of(i * chunk, chunk), chunk)
            batch = i // (rows // chunk)
            at = pl.multiple_of((i % (rows // chunk)) * chunk, chunk)
            summed = (unit[here] * vec_ref[3:4] + vec_ref[4:5]) + total_ref[here] + vec_ref[5:6]
            normed, unit_two, inverse = normalize(summed, vec_ref[6:7], vec_ref[7:8])
            place = at + lax.broadcasted_iota(jnp.int32, (chunk, 1), 0)
            valid = place < meta[1 + batch]
            out[here] = jnp.where(valid, normed, 0.0).astype(BF16)
            grad_out = jnp.where(valid, cot[batch, pl.ds(at, chunk)].astype(F32), 0.0)
            grad_sum = norm_back(grad_out, unit_two, inverse, vec_ref[6:7])
            grad_sums[here] = grad_sum
            low[here] = grad_sum.astype(BF16)
            grad_ref[0:1] += jnp.sum(grad_out * unit_two, 0, keepdims=True)
            grad_ref[1:2] += jnp.sum(grad_out, 0, keepdims=True)
            grad_ref[2:3] += jnp.sum(grad_sum, 0, keepdims=True)
            return carry

        lax.fori_loop(0, total // chunk, body, 0)
        leaving = [
            pltpu.make_async_copy(source, target, early.at[i])
            for i, (source, target) in enumerate(((low, low_ref), (out, out_ref), (grad_sums, sum_ref)))
        ]
        for copy in leaving:
            copy.start()

        def leave(b):
            at = pl.ds(pl.multiple_of(512 * b, 512), 512)
            return pltpu.make_async_copy(left.at[b], pre_ref.at[:, at], out_sems.at[b])

        def through(b, carry):
            arrived(right.at[b], right_sems.at[b])
            grad = (dot_nt(low[...], held[b]) * right[b].astype(F32)).astype(BF16)
            left[b] = grad
            leave(b).start()
            bias_ref[:, pl.ds(pl.multiple_of(512 * b, 512), 512)] = jnp.sum(grad.astype(F32), 0, keepdims=True)
            return carry

        lax.fori_loop(0, 8, through, 0)
        for b in range(8):
            leave(b).wait()
        for copy in leaving:
            copy.wait()

    block = (total, width)
    return call(
        kernel,
        (1,),
        [ANY, ANY, ANY, ANY, whole(vecs.shape)] + [ANY] * len(down),
        [ANY, ANY, ANY, whole((8, width)), ANY, whole((1, wide))],
        [
            sds(block, BF16), sds(block, F32), sds(block, BF16), sds((8, width), F32),
            sds((total, wide), BF16), sds((1, wide), F32),
        ],
        [
            pltpu.VMEM(block, BF16), pltpu.VMEM(block, F32), pltpu.VMEM(block, BF16), DMA((3,)),
            pltpu.VMEM((8, 512, width), BF16), pltpu.VMEM((8, total, 512), BF16), pltpu.VMEM((8, total, 512), BF16),
            pltpu.VMEM(block, F32), pltpu.VMEM(block, F32), pltpu.VMEM((batches, rows, width), BF16),
            DMA((8,)), DMA((8,)), DMA((8,)), DMA((8,)), DMA((1 + batches,)),
        ],
    )(meta, act, slope, unit_one, cot_pool, vecs, *down)


def back_up(meta, pre, up, first, grad_sum, unit_one, inverse_one, vecs):
    total, wide = pre.shape
    width = grad_sum.shape[1]
    chunk, strip = 128, 1024
    strips = wide // strip

    def kernel(meta, pre_ref, sum_ref, unit_ref, inv_ref, vec_ref, *refs):
        parts, others = refs[: len(up)], refs[len(up) : len(up) + len(first)]
        (
            resid_ref, low_ref, mixed_ref, grad_ref,
            held, pres, out_held, hidden, unit, low, mixed, sems, pre_sems, out_sems, more, leave_sems,
        ) = refs[len(up) + len(first) :]
        for t in range(strips):
            at = pl.ds(strip * t, strip)
            pltpu.make_async_copy(pre_ref.at[:, at], pres.at[t], pre_sems.at[t]).start()
            fetch(meta, parts, held.at[t], sems.at[t], 0, 128, at)
            if t == 0:
                incoming = pltpu.make_async_copy(sum_ref, hidden, more.at[0])
                incoming.start()
        other = pltpu.make_async_copy(unit_ref, unit, more.at[1])
        other.start()
        fetch(meta, others, out_held, out_sems, 384, 512)
        incoming.wait()

        def through(t, carry):
            arrived(pres.at[t], pre_sems.at[t])
            for b in range(8):
                arrived(held.at[t, b], sems.at[t, b])
            hidden[...] += dot_nt(pres[t], held[t].reshape(width, strip))
            return carry

        lax.fori_loop(0, strips, through, 0)
        other.wait()
        grad_ref[...] = jnp.zeros_like(grad_ref)

        def body(i, carry):
            here = pl.ds(pl.multiple_of(i * chunk, chunk), chunk)
            grad, unit_here = hidden[here], unit[here]
            grad_ref[0:1] += jnp.sum(grad * unit_here, 0, keepdims=True)
            grad_ref[1:2] += jnp.sum(grad, 0, keepdims=True)
            resid = norm_back(grad, unit_here, inv_ref[here, 0:1], vec_ref[3:4])
            grad_ref[2:3] += jnp.sum(resid, 0, keepdims=True)
            hidden[here] = resid
            low[here] = resid.astype(BF16)
            return carry

        lax.fori_loop(0, total // chunk, body, 0)
        leaving = [
            pltpu.make_async_copy(low, low_ref, leave_sems.at[0]), pltpu.make_async_copy(hidden, resid_ref, leave_sems.at[1])
        ]
        for copy in leaving:
            copy.start()
        for b in range(8):
            arrived(out_held.at[b], out_sems.at[b])

        def leave(j):
            at = pl.ds(pl.multiple_of(512 * j, 512), 512)
            return pltpu.make_async_copy(mixed.at[:, at], mixed_ref.at[:, at], leave_sems.at[2 + j])

        def out(j, carry):
            weight = out_held[pl.ds(4 * j, 4)].reshape(512, width)
            mixed[:, pl.ds(pl.multiple_of(512 * j, 512), 512)] = dot_nt(low[...], weight).astype(BF16)
            leave(j).start()
            return carry

        lax.fori_loop(0, 2, out, 0)
        for copy in leaving + [leave(0), leave(1)]:
            copy.wait()

    block = (total, width)
    return call(
        kernel,
        (1,),
        [ANY, ANY, ANY, whole((total, 128)), whole(vecs.shape)] + [ANY] * (len(up) + len(first)),
        [ANY, ANY, ANY, whole((8, width))],
        [sds(block, F32), sds(block, BF16), sds(block, BF16), sds((8, width), F32)],
        [
            pltpu.VMEM((strips, 8, 128, strip), BF16), pltpu.VMEM((strips, total, strip), BF16),
            pltpu.VMEM((8, 128, width), BF16), pltpu.VMEM(block, F32), pltpu.VMEM(block, F32), pltpu.VMEM(block, BF16),
            pltpu.VMEM(block, BF16), DMA((strips, 8)), DMA((strips,)), DMA((8,)), DMA((2,)), DMA((4,)),
        ],
    )(meta, pre, grad_sum, unit_one, inverse_one, vecs, *up, *first)


def attend_back(meta, qkv, mixed, raised, inverse, grad_mixed, grads_one, grads_two, bias_up, batches, rows):
    total, width = grad_mixed.shape
    span = HEADS * HD
    steps = width // span

    def kernel(meta, q_ref, k_ref, v_ref, mixed_ref, g_ref, raised_ref, inv_ref, one_ref, two_ref, up_ref, out_ref, vec_ref, sums):
        batch, step = pl.program_id(0), pl.program_id(1)
        left = lax.broadcasted_iota(jnp.int32, (rows, 128), 1) < HD
        none = jnp.zeros((rows, 128), BF16)

        @pl.when((batch == 0) & (step == 0))
        def _():
            sums[...] = jnp.zeros_like(sums)

        for pair in range(HEADS // 2):
            cols = slice(128 * pair, 128 * (pair + 1))
            query, keyed, value = q_ref[0, :, cols] * jnp.asarray(HD**-0.5, BF16), k_ref[0, :, cols], v_ref[0, :, cols]
            grad = g_ref[:, cols].astype(F32) * inv_ref[:, cols]
            both = grad * mixed_ref[:, cols].astype(F32)
            grad = grad.astype(BF16)
            got = ([], [], [])
            for half in range(2):
                mine = left if half == 0 else jnp.logical_not(left)
                low = raised_ref[0, 2 * pair + half]
                inner = jnp.sum(jnp.where(mine, both, 0.0), -1, keepdims=True)
                slope = dot_nt(jnp.where(mine, grad, none), value) - inner
                scores = (low.astype(F32) * slope).astype(BF16)
                got[0].append(dot_nn(scores, keyed))
                got[1].append(dot_tn(scores, query))
                got[2].append(dot_tn(low, grad))
            for i in range(3):
                part = jnp.where(left, got[i][0], got[i][1])
                if i == 0:
                    part = part * (HD**-0.5)
                part = part.astype(BF16)
                out_ref[i, :, cols] = part
                if i != 1:
                    at = pl.ds(pl.multiple_of(step * span, span) + 128 * pair, 128)
                    sums[i : i + 1, at] += jnp.sum(part.astype(F32), 0, keepdims=True)

        @pl.when((batch == batches - 1) & (step == steps - 1))
        def _():
            vec_ref[...] = jnp.zeros_like(vec_ref)
            rows_of = (
                sums[0:1], sums[2:3], one_ref[2:3], one_ref[0:1], one_ref[1:2], two_ref[2:3], two_ref[0:1], two_ref[1:2]
            )
            table = jnp.concatenate(rows_of, 0).astype(BF16)
            for b in range(8):
                vec_ref[b, 0:8, 0:128] = table[:, 128 * b : 128 * (b + 1)]
                vec_ref[b, 8:9, 0:512] = up_ref[:, 512 * b : 512 * (b + 1)].astype(BF16)

    part = lambda w: spec((1, rows, span), lambda b, h, meta: (w, b, h))
    here = spec((rows, span), lambda b, h, meta: (b, h))
    return call(
        kernel,
        (batches, steps),
        [
            part(0), part(1), part(2), here, here, spec((1, HEADS, rows, rows), lambda b, h, meta: (b, h, 0, 0)), here,
            whole((8, width)), whole((8, width)), whole((1, 4 * width)),
        ],
        [spec((3, rows, span), lambda b, h, meta: (0, b, h)), whole((8, 16, width))],
        [sds((3, total, width), BF16), sds((8, 16, width), BF16)],
        [pltpu.VMEM((8, width), F32)],
    )(meta, qkv, qkv, qkv, mixed, grad_mixed, raised, inverse, grads_one, grads_two, bias_up)


def back_project(meta, grads, first, grad_resid):
    total, width = grad_resid.shape

    def kernel(meta, g_ref, resid_ref, *refs):
        parts, (out_ref, held, resid, made, sems, more, out_sems) = refs[: len(first)], refs[len(first) :]
        fetch(meta, parts, held, sems, 0, 384)
        incoming = pltpu.make_async_copy(resid_ref, resid, more)
        incoming.start()
        incoming.wait()

        def leave(j):
            at = pl.ds(pl.multiple_of(256 * j, 256), 256)
            return pltpu.make_async_copy(made.at[:, at], out_ref.at[:, at], out_sems.at[j])

        def body(j, carry):
            for b in range(2):
                arrived(held.at[2 * j + b], sems.at[2 * j + b])
            at = pl.ds(pl.multiple_of(256 * j, 256), 256)
            part = resid[:, at]
            for w in range(3):
                weight = held[pl.ds(2 * j, 2), 128 * w : 128 * (w + 1)].reshape(256, width)
                part = part + dot_nt(g_ref[w], weight)
            made[:, at] = part.astype(BF16)
            leave(j).start()
            return carry

        lax.fori_loop(0, 4, body, 0)
        for j in range(4):
            leave(j).wait()

    block = (total, width)
    return call(
        kernel,
        (1,),
        [whole((3, total, width)), ANY] + [ANY] * len(first),
        ANY,
        sds(block, BF16),
        [
            pltpu.VMEM((8, 384, width), BF16), pltpu.VMEM(block, F32), pltpu.VMEM(block, BF16), DMA((8,)), DMA(()),
            DMA((4,)),
        ],
    )(meta, grads, grad_resid, *first)


def ship(made, outs, sems, half, i):
    def copy(target):
        return pltpu.make_async_copy(made.at[half, i], target, sems.at[half, i])

    if isinstance(i, int):
        copy(outs[half].at[i] if i < 2 else outs[2 * i - 2 + half]).start()
        return

    @pl.when(i < 2)
    def _():
        copy(outs[half].at[jnp.minimum(i, 1)]).start()

    @pl.when(i == 2)
    def _():
        copy(outs[2 + half]).start()

    @pl.when(i == 3)
    def _():
        copy(outs[4 + half]).start()


def shipped(made, sems):
    for half in range(2):
        for i in range(4):
            arrived(made.at[half, i], sems.at[half, i])


def chip_of(half, i):
    return (i + 2) % 4 if half == 0 else (2 * i + 1) % 5


def six(rows, cols):
    return [sds((2, rows, cols), BF16)] * 2 + [sds((rows, cols), BF16)] * 4


def load_lefts(meta, own_ref, got_ref, lefts, sems, block, total):
    for chip in (2, 3, 1, 0):
        at = pl.ds(pl.multiple_of((meta[0] ^ (2 * chip)) * block, block), block)
        pltpu.make_async_copy(own_ref.at[:, at], lefts.at[chip, pl.ds(0, total)], sems.at[chip]).start()
        pltpu.make_async_copy(got_ref.at[chip], lefts.at[chip, pl.ds(total, total)], sems.at[chip]).start()


def load_right(own, got, target, sem, total):
    pltpu.make_async_copy(own, target.at[pl.ds(0, total)], sem).start()
    pltpu.make_async_copy(got, target.at[pl.ds(total, total)], sem).start()


def down_grad(meta, act, act_got, low, low_got):
    total, width = low.shape
    block, share = 512, width // 2

    def kernel(meta, left_ref, left_got, right_ref, right_got, *refs):
        outs, (lefts, rights, made, left_sems, right_sems, out_sems) = refs[:6], refs[6:]
        for half in range(2):
            at = pl.ds(share * half, share)
            load_right(right_ref.at[:, at], right_got.at[:, at], rights.at[half], right_sems.at[half], total)
            if half == 0:
                load_lefts(meta, left_ref, left_got, lefts, left_sems, block, total)
        for half in range(2):
            arrived(rights.at[half], right_sems.at[half])

            def body(i, carry):
                chip = chip_of(half, i)
                if half == 0:
                    arrived(lefts.at[chip], left_sems.at[chip])
                made[half, i] = dot_tn(lefts[chip], rights[half]).astype(BF16)
                ship(made, outs, out_sems, half, i)
                return carry

            lax.fori_loop(0, 4, body, 0)
        shipped(made, out_sems)

    outs = call(
        kernel,
        (1,),
        [ANY] * 4,
        [ANY] * 6,
        six(block, share),
        [
            pltpu.VMEM((4, 2 * total, block), BF16), pltpu.VMEM((2, 2 * total, share), BF16),
            pltpu.VMEM((2, 4, block, share), BF16), DMA((4,)), DMA((2,)), DMA((2, 4)),
        ],
    )(meta, act, act_got, low, low_got)
    return outs[:2], outs[2:4], outs[4:]


def load_columns(meta, own_ref, got_ref, target, sem, total):
    for chip in range(4):
        at = pl.ds(pl.multiple_of((meta[0] ^ (2 * chip)) * 128, 128), 128)
        cols = pl.ds(128 * chip, 128)
        pltpu.make_async_copy(own_ref.at[:, at], target.at[pl.ds(0, total), cols], sem).start()
        pltpu.make_async_copy(got_ref.at[chip], target.at[pl.ds(total, total), cols], sem).start()


ORDER = ((2, 3, 0, 1), (1, 3, 0, 2))


def up_grad(meta, hidden, hidden_got, pre, pre_got):
    total, width = hidden.shape
    wide = pre.shape[1]
    tile = 1024
    tiles = wide // tile // 2

    def kernel(meta, x_ref, x_got, pre_ref, pre_got, *refs):
        outs, (lefts, rights, made, left_sem, right_sems, out_sems) = refs[:6], refs[6:]
        for t in range(2 * tiles):
            at = pl.ds(tile * t, tile)
            load_right(pre_ref.at[:, at], pre_got.at[:, at], rights.at[t], right_sems.at[t], total)
            if t == 0:
                load_columns(meta, x_ref, x_got.at[1], lefts, left_sem, total)
        arrived(lefts, left_sem)
        for half in range(2):

            def body(t, carry):
                arrived(rights.at[half * tiles + t], right_sems.at[half * tiles + t])
                part = dot_tn(lefts[...], rights[half * tiles + t]).astype(BF16)
                at = pl.ds(pl.multiple_of(t * tile, tile), tile)
                for i, chip in enumerate(ORDER[half]):
                    made[half, i, :, at] = part[128 * chip : 128 * (chip + 1)]
                return carry

            lax.fori_loop(0, tiles, body, 0)
            for i in range(4):
                ship(made, outs, out_sems, half, i)
        shipped(made, out_sems)

    outs = call(
        kernel,
        (1,),
        [ANY] * 4,
        [ANY] * 6,
        six(128, wide // 2),
        [
            pltpu.VMEM((2 * total, 512), BF16), pltpu.VMEM((2 * tiles, 2 * total, tile), BF16),
            pltpu.VMEM((2, 4, 128, wide // 2), BF16), DMA(()), DMA((2 * tiles,)), DMA((2, 4)),
        ],
    )(meta, hidden, hidden_got, pre, pre_got)
    return outs[:2], outs[2:4], outs[4:]


def first_grad(meta, tokens, tokens_got, mixed, mixed_got, grads, grads_got, low, low_got, vec, vec_got):
    total, width = tokens.shape
    share = width // 2

    def kernel(meta, x_ref, x_got, m_ref, m_got, g_ref, g_got, low_ref, low_got, vec_ref, vec_got, *refs):
        outs = refs[:6], refs[6:12]
        lefts, rights, made_a, made_b, short, left_sems, right_sems, sems_a, sems_b, short_sems = refs[12:]
        for w in range(4):
            own, got = (g_ref.at[w], g_got.at[w]) if w < 3 else (low_ref, low_got)
            load_right(own, got, rights.at[w], right_sems.at[w], total)
            if w == 0:
                load_columns(meta, x_ref, x_got, lefts.at[0], left_sems.at[0], total)
                for chip in range(4):
                    at = meta[0] ^ (2 * chip)
                    pltpu.make_async_copy(vec_ref.at[at], short.at[chip, 0], short_sems.at[chip]).start()
                    pltpu.make_async_copy(vec_got.at[at], short.at[chip, 1], short_sems.at[chip]).start()
            if w == 2:
                load_columns(meta, m_ref, m_got.at[0], lefts.at[1], left_sems.at[1], total)
        arrived(lefts.at[0], left_sems.at[0])
        for group, (made, sems) in enumerate(((made_a, sems_a), (made_b, sems_b))):

            def body(k, carry):
                arrived(rights.at[2 * group + k], right_sems.at[2 * group + k])
                if group == 1:

                    @pl.when(k == 1)
                    def _():
                        arrived(lefts.at[1], left_sems.at[1])

                part = dot_tn(lefts[k * group], rights[2 * group + k]).astype(BF16)
                rows = pl.ds(pl.multiple_of(128 * k, 128), 128)
                for half in range(2):
                    for i, chip in enumerate(ORDER[half]):
                        made[half, i, rows] = part[128 * chip : 128 * (chip + 1), share * half : share * (half + 1)]
                return carry

            lax.fori_loop(0, 2, body, 0)
            if group == 1:
                for i, chip in enumerate(ORDER[0]):
                    arrived(short.at[chip], short_sems.at[chip])
                    both = short[chip, 0].astype(F32) + short[chip, 1].astype(F32)
                    made[0, i, 256:] = both[:, :share].astype(BF16)
                    made[1, i, 256:] = jnp.zeros((16, share), BF16)
            for half in range(2):
                for i in range(4):
                    ship(made, outs[group], sems, half, i)
        shipped(made_a, sems_a)
        shipped(made_b, sems_b)

    outs = call(
        kernel,
        (1,),
        [ANY] * 10,
        [ANY] * 12,
        six(256, share) + six(272, share),
        [
            pltpu.VMEM((2, 2 * total, 512), BF16), pltpu.VMEM((4, 2 * total, width), BF16),
            pltpu.VMEM((2, 4, 256, share), BF16), pltpu.VMEM((2, 4, 272, share), BF16),
            pltpu.VMEM((4, 2, 16, width), BF16), DMA((2,)), DMA((4,)), DMA((2, 4)), DMA((2, 4)), DMA((4,)),
        ],
    )(meta, tokens, tokens_got, mixed, mixed_got, grads, grads_got, low, low_got, vec, vec_got)
    return [(some[:2], some[2:4], some[4:]) for some in (outs[:6], outs[6:])]


def pack(weights, small):
    block, width = weights[0].shape
    high = block * len(weights) + 16

    def kernel(*refs):
        out_ref = refs[-1]
        for i in range(len(weights)):
            out_ref[block * i : block * (i + 1)] = refs[i][...]
        out_ref[block * len(weights) :] = jnp.zeros((16, width), BF16)
        start = 0
        for ref in refs[len(weights) : -1]:
            count = ref.shape[1]
            row, column = block * len(weights) + start // width, start % width
            out_ref[row : row + 1, column : column + count] = ref[...]
            start += count

    return pl.pallas_call(
        kernel,
        out_shape=jax.ShapeDtypeStruct((high, width), BF16),
        compiler_params=pltpu.CompilerParams(vmem_limit_bytes=VMEM),
        cost_estimate=pl.CostEstimate(flops=1024, bytes_accessed=1024, transcendentals=0),
    )(*weights, *[part.reshape(1, -1) for part in small])


def chosen(meta, pool, first):
    rows, width = pool.shape[1:]

    def kernel(meta, pool_ref, out_ref):
        out_ref[...] = pool_ref[...]

    return call(
        kernel,
        (2,),
        [spec((1, rows, width), lambda i, meta: (meta[first + i], 0, 0))],
        spec((1, rows, width), lambda i, meta: (i, 0, 0)),
        sds((2, rows, width), BF16),
        [],
    )(meta, pool)


CORE, ALONG_X, ALONG_Y = 1, 2, 4


def swap(value, mask):
    return lax.ppermute(value, "shard", [(i, i ^ mask) for i in range(8)])


def plus(*parts):
    total = parts[0].astype(F32)
    for part in parts[1:]:
        total = total + part.astype(F32)
    return total.astype(BF16)


class Order:
    def __init__(self, meta):
        self.meta = meta

    def place(self, *values):
        *values, self.meta = lax.optimization_barrier(values + (self.meta,))
        return values

    def then(self, value):
        self.meta, value = lax.optimization_barrier((self.meta, value))
        return value

    def run(self, function, *values):
        return self.then(function(*self.place(*values)))


def tie(*values):
    return lax.optimization_barrier(values)


def both_cores(*mine):
    return mine + tuple(swap(part, CORE) for part in mine)


def pairs(value, mask):
    return lax.ppermute(value, "rep", [(i, i ^ mask) for i in range(4)])


def turned(rest, got):
    return plus(rest[0], got[0][1]), plus(rest[1], got[1][1])


def passed(values):
    return swap(values[0], ALONG_X), swap(values[1], ALONG_Y)


def sent(values):
    return swap(values[0], ALONG_Y), swap(values[1], ALONG_X)


def summed(own, got, late):
    odd = lax.axis_index("rep") % 2 == 1
    first, second = plus(own[0], got[0][0], late[0]), plus(own[1], got[1][0], late[1])
    return jnp.where(odd, second, first), jnp.where(odd, first, second)


def merge(meta, own, got, late, rest, got_next):
    rows, cols = own[0].shape
    high, wide = rest[0].shape
    steps = 4

    def kernel(meta, own_a, own_b, got_a, got_b, late_a, late_b, rest_a, rest_b, next_a, next_b, *outs):
        kept_ref, given_ref, pass_a, pass_b = outs
        first = own_a[...].astype(F32) + got_a[0].astype(F32) + late_a[...].astype(F32)
        second = own_b[...].astype(F32) + got_b[0].astype(F32) + late_b[...].astype(F32)
        odd = meta[7] == 1
        kept_ref[...] = jnp.where(odd, second, first).astype(BF16)
        given_ref[...] = jnp.where(odd, first, second).astype(BF16)
        pass_a[...] = (rest_a[...].astype(F32) + next_a[0].astype(F32)).astype(BF16)
        pass_b[...] = (rest_b[...].astype(F32) + next_b[0].astype(F32)).astype(BF16)

    flat = spec((rows // steps, cols), lambda i, meta: (i, 0))
    mine = spec((1, rows // steps, cols), lambda i, meta: (0, i, 0))
    low = spec((high // steps, wide), lambda i, meta: (i, 0))
    other = spec((1, high // steps, wide), lambda i, meta: (1, i, 0))
    kept, given, *passing = call(
        kernel,
        (steps,),
        [flat, flat, mine, mine, flat, flat, low, low, other, other],
        [flat, flat, low, low],
        [sds((rows, cols), BF16)] * 2 + [sds((high, wide), BF16)] * 2,
        [],
    )(meta, *own, *got, *late, *rest, *got_next)
    return kept, given, tuple(passing)


def unfolded(mine, other):
    odd = lax.axis_index("rep") % 2 == 1
    return jnp.where(odd, other, mine).astype(F32), jnp.where(odd, mine, other).astype(F32)


def local_eight(
    inputs, lengths, dealing, w_query, w_key, w_value, w_out, b_query, b_value, b_out,
    ln1_gain, ln1_bias, w_up, b_up, w_down, b_down, ln2_gain, ln2_bias, cotangent,
):
    batches, rows, width = inputs.shape
    wide = w_up.shape[1]
    total = batches * rows
    group = batches * 4
    shard_index = lax.axis_index("shard")
    anchor = shard_index * group
    slots = anchor + lax.axis_index("rep") * batches + jnp.arange(batches, dtype=jnp.int32)
    local_dealing = lax.dynamic_slice_in_dim(dealing, anchor, group) - anchor
    sources = jnp.take(dealing, slots) - anchor
    places = jnp.arange(group, dtype=jnp.int32)
    wanted = jnp.sum(
        jnp.where(local_dealing[None, :] == (slots - anchor)[:, None], places[None, :], 0), 1
    )
    meta = jnp.concatenate([shard_index[None].astype(jnp.int32), jnp.take(lengths, slots), wanted, jnp.clip(sources, 0, group - 1), (lax.axis_index("rep") % 2)[None].astype(jnp.int32)])
    order = Order(meta)
    tokens = inputs.reshape(total, width)

    small = (b_query, b_value, b_out, ln1_gain, ln1_bias, b_down, ln2_gain, ln2_bias, b_up)
    own_first = pack((w_query, w_key, w_value, w_out), small)
    first_x, first_y = swap(own_first, ALONG_X), swap(own_first, ALONG_Y)
    first_x, first_y, to_both = order.then((first_x, first_y, w_up))
    first_far, up_x = swap(first_x, ALONG_Y), swap(to_both, ALONG_X)
    first_c = [swap(part, CORE) for part in (own_first, first_x, first_y)]
    first_far, up_x, to_x, to_y, *first_c = order.then((first_far, up_x, w_down, w_up, *first_c))
    first = (own_first, first_x, first_y, first_far, *first_c, swap(first_far, CORE))
    up_y, down_x = swap(to_y, ALONG_Y), swap(to_x, ALONG_X)
    up_c = [swap(part, CORE) for part in (w_up, up_x)]
    cot_pool = lax.all_gather(cotangent, "rep", axis=0, tiled=True)
    qkv, vecs, bias_up, tokens_give = order.then(project(order.meta, tokens, first))
    mixed, raised, inverse = order.then(attend(order.meta, qkv, batches, rows))
    up_y, down_x, tokens_give, to_y, *up_c = order.then((up_y, down_x, tokens_give, w_down, *up_c))
    up_far, down_y = swap(up_y, ALONG_X), swap(to_y, ALONG_Y)
    up_c.append(swap(up_y, CORE))
    tokens_got = swap(tokens_give, CORE)
    unit_one, inverse_one, hidden_low, both_give = order.then(mix_out(order.meta, mixed, tokens, first, vecs))
    to_top = order.then(down_x[:256])
    up_far, down_y, tokens_got, both_give, to_top, *up_c = order.then((up_far, down_y, tokens_got, both_give, to_top, *up_c))
    up = (w_up, up_x, up_y, up_far, *up_c, swap(up_far, CORE))
    down_top, down_end = swap(to_top, ALONG_Y), swap(down_y[256:], ALONG_X)
    up, *to_core = order.then((up, w_down, down_x, down_y))
    down_c = [swap(part, CORE) for part in to_core]
    act, slope, act_give = order.then(feed_up(order.meta, hidden_low, up, bias_up))
    down_top, down_end, act_give, both_give, *down_c = order.then((down_top, down_end, act_give, both_give, *down_c))
    down = (w_down, down_x, down_y, down_top, down_end) + tuple(down_c)
    down += tuple(swap(part, CORE) for part in (down_top, down_end))
    *down, act_give, both_give = order.then((*down, act_give, both_give))
    act_got, both_got = swap(act_give, CORE), swap(both_give, CORE)
    out, grad_sum, sum_low, grads_two, pre, grad_bias_up = order.then(
        feed_down(order.meta, act, slope, down, unit_one, cot_pool, vecs, batches, rows)
    )
    sum_got = swap(sum_low, CORE)
    out, act_got, both_got, sum_got, pre = order.then((out, act_got, both_got, sum_got, pre))
    pre_got = swap(pre, CORE)
    out_pool = lax.all_gather(out.reshape(batches, rows, width), "rep", axis=0, tiled=True)
    far_down, own_down, rest_down = order.then(down_grad(order.meta, act, act_got, sum_low, sum_got))
    pre_got, far_down = order.then((pre_got, far_down))
    got_down = sent(far_down)
    grad_resid, resid_low, grad_mixed, grads_one = order.then(
        back_up(order.meta, pre, up, first, grad_sum, unit_one, inverse_one, vecs)
    )
    far_up, own_up, rest_up = order.then(up_grad(order.meta, hidden_low, both_got, pre, pre_got))
    got_down, far_up, resid_low = order.then((got_down, far_up, resid_low))
    got_up = sent(far_up)
    late_down = passed(order.then(turned(rest_down, got_down)))
    grads, vec = order.then(
        attend_back(
            order.meta, qkv, mixed, raised, inverse, grad_mixed, grads_one, grads_two, grad_bias_up, batches, rows
        )
    )
    grad_input = order.then(back_project(order.meta, grads, first, grad_resid))
    got_up, late_down, resid_low, grads, vec = order.then((got_up, late_down, resid_low, grads, vec))
    resid_got, grads_got, vec_got = swap(resid_low, CORE), swap(grads, CORE), swap(vec, CORE)
    kept_down, given_down, pass_up = order.then(
        merge(order.meta, own_down, got_down, late_down, rest_up, got_up)
    )
    resid_got, grads_got, vec_got, pass_up, given_down = order.then((resid_got, grads_got, vec_got, pass_up, given_down))
    late_up, taken_down = passed(pass_up), pairs(given_down, 1)
    (far_a, own_a, rest_a), (far_b, own_b, rest_b) = order.then(
        first_grad(
            order.meta, tokens, tokens_got, mixed, both_got, grads, grads_got, resid_low, resid_got, vec, vec_got
        )
    )
    late_up, taken_down, far_a, out_pool = order.then((late_up, taken_down, far_a, out_pool))
    got_a = sent(far_a)
    far_b, half_down = order.then((far_b, plus(kept_down, taken_down)))
    got_b = sent(far_b)
    over_down = pairs(half_down, 2)
    kept_up, given_up = order.then(summed(own_up, got_up, late_up))
    got_a = order.then(got_a)
    late_a = passed(order.then(turned(rest_a, got_a)))
    taken_up = pairs(given_up, 1)
    layer_out = order.then(chosen(order.meta, out_pool, 5))
    got_b = order.then(got_b)
    late_b = passed(order.then(turned(rest_b, got_b)))
    late_a = order.then(late_a)
    kept_a, given_a = order.then(summed(own_a, got_a, late_a))
    taken_a = pairs(given_a, 1)
    over_down, taken_up = order.then((over_down, taken_up))
    total_down, half_up = order.then((plus(half_down, over_down), plus(kept_up, taken_up)))
    late_b = order.then(late_b)
    kept_b, given_b = order.then(summed(own_b, got_b, late_b))
    taken_b = pairs(given_b, 1)
    taken_a = order.then(taken_a)
    half_a = order.then(plus(kept_a, taken_a))
    over_a = pairs(half_a, 2)
    over_up, other_down = pairs(half_up, 2), pairs(total_down, 1)
    taken_b = order.then(taken_b)
    half_b = order.then(plus(kept_b, taken_b))
    over_b = pairs(half_b, 2)
    over_a = order.then(over_a)
    total_a = order.then(plus(half_a, over_a))
    other_a = pairs(total_a, 1)
    over_up, other_down = order.then((over_up, other_down))
    total_up = order.then(plus(half_up, over_up))
    other_up = pairs(total_up, 1)
    g_down = order.then(jnp.concatenate(unfolded(total_down, other_down), 1))
    over_b = order.then(over_b)
    total_b = order.then(plus(half_b, over_b))
    other_b = pairs(total_b, 1)
    other_a, other_up = order.then((other_a, other_up))
    g_up = order.then(jnp.concatenate(unfolded(total_up, other_up), 1))
    g_a = order.then(jnp.concatenate(unfolded(total_a, other_a), 1))
    left, right = unfolded(total_b, other_b)
    g_b = jnp.concatenate([left[:256], right[:256]], 1)
    line = lambda i: left[256 + i, :128]
    return (
        layer_out, grad_input.reshape(batches, rows, width),
        g_a[0:128], g_a[128:256], g_b[0:128], g_b[128:256],
        line(0), line(1), line(2), line(3), line(4),
        g_up, left[264, :512], g_down, line(5), line(6), line(7),
    )


def pick(pool, targets):
    return jnp.stack(
        [lax.dynamic_index_in_dim(pool, targets[i], 0, keepdims=False) for i in range(targets.shape[0])]
    )


def local_general(
    inputs, lengths, dealing, w_query, w_key, w_value, w_out, b_query, b_value, b_out,
    ln1_gain, ln1_bias, w_up, b_up, w_down, b_down, ln2_gain, ln2_bias, cotangent,
):
    batches, rows, width = inputs.shape
    shards = lax.axis_size("shard")
    replicas = lax.axis_size("rep")
    group = batches * replicas
    shard_index = lax.axis_index("shard")
    rep_index = lax.axis_index("rep")
    anchor = shard_index * group
    slots = anchor + rep_index * batches + jnp.arange(batches, dtype=jnp.int32)
    seq_lengths = jnp.take(lengths, slots)
    local_dealing = lax.dynamic_slice_in_dim(dealing, anchor, group) - anchor
    sources = jnp.take(dealing, slots) - anchor
    places = jnp.arange(group, dtype=jnp.int32)
    wanted = jnp.sum(
        jnp.where(local_dealing[None, :] == (slots - anchor)[:, None], places[None, :], 0), 1
    )

    def gather(block):
        return lax.all_gather(block, "shard", axis=0, tiled=True)

    block = w_query.shape[0]
    wide = w_up.shape[1]
    small = (b_query, b_value, b_out, ln1_gain, ln1_bias, b_down, ln2_gain, ln2_bias, b_up)
    vec = jnp.concatenate(small)
    first = jnp.concatenate([w_query, w_key, w_value, w_out], 0)
    all_vec = lax.all_gather(vec, "shard", axis=0, tiled=True).reshape(shards, -1)
    all_first = gather(first).reshape(shards, 4, block, width)
    cuts = [0]
    for part in small:
        cuts.append(cuts[-1] + part.shape[0])
    (bias_query, bias_value, bias_out, gain_one, shift_one, bias_down, gain_two, shift_two, bias_up) = [
        all_vec[:, cuts[i] : cuts[i + 1]].reshape(-1).astype(F32) for i in range(len(small))
    ]
    full_query, full_key, full_value, full_out = [
        all_first[:, i].reshape(width, width) for i in range(4)
    ]
    full_up = gather(w_up)
    full_down = gather(w_down)
    cot = pick(lax.all_gather(cotangent, "rep", axis=0, tiled=True), wanted)

    tokens = inputs.reshape(batches * rows, width)
    query = (matmul(tokens, full_query) + bias_query).astype(BF16)
    keyed = matmul(tokens, full_key).astype(BF16)
    value = (matmul(tokens, full_value) + bias_value).astype(BF16)
    heads = lambda a: a.reshape(batches, rows, H, HD).transpose(0, 2, 1, 3)
    flat = lambda a: a.transpose(0, 2, 1, 3).reshape(batches * rows, width)
    qh, kh, vh = heads(query), heads(keyed), heads(value)
    allowed = lax.broadcasted_iota(jnp.int32, (batches, 1, 1, rows), 3) < seq_lengths[:, None, None, None]
    scale = HD ** (-0.5)
    scores = jnp.einsum("bhqd,bhkd->bhqk", qh, kh, preferred_element_type=F32) * scale
    scores = jnp.where(allowed, scores, NEG)
    raised = jnp.exp(scores - jnp.max(scores, -1, keepdims=True))
    probs = raised / jnp.sum(raised, -1, keepdims=True)
    probs_low = probs.astype(BF16)
    mixed_low = flat(jnp.einsum("bhqk,bhkd->bhqd", probs_low, vh, preferred_element_type=F32).astype(BF16))
    hidden, unit_one, inverse_one = normalize(
        tokens.astype(F32) + matmul(mixed_low, full_out) + bias_out, gain_one, shift_one
    )
    hidden_low = hidden.astype(BF16)
    pre = matmul(hidden_low, full_up) + bias_up
    act, slope = gelu_both(pre)
    act_low = act.astype(BF16)
    summed = hidden + matmul(act_low, full_down) + bias_down
    normed, unit_two, inverse_two = normalize(summed, gain_two, shift_two)
    valid = (lax.broadcasted_iota(jnp.int32, (batches, rows, 1), 1) < seq_lengths[:, None, None]).reshape(-1, 1)
    out = jnp.where(valid, normed, 0.0).astype(BF16).reshape(batches, rows, width)
    layer_out = pick(lax.all_gather(out, "rep", axis=0, tiled=True), sources)

    grad_out = jnp.where(valid, cot.reshape(-1, width).astype(F32), 0.0)
    grad_gain_two = jnp.sum(grad_out * unit_two, 0)
    grad_shift_two = jnp.sum(grad_out, 0)
    grad_sum = norm_back(grad_out, unit_two, inverse_two, gain_two)
    grad_bias_down = jnp.sum(grad_sum, 0)
    grad_sum_low = grad_sum.astype(BF16)

    def reduced(part):
        return lax.psum_scatter(part, "shard", scatter_dimension=0, tiled=True)

    def over_rep(part):
        return lax.psum(part, "rep").astype(F32)

    g_down = reduced(left_trans(act_low, grad_sum_low).astype(BF16))
    grad_pre = (right_trans(grad_sum_low, full_down) * slope).astype(BF16)
    grad_bias_up = jnp.sum(grad_pre.astype(F32), 0)
    g_up = reduced(left_trans(hidden_low, grad_pre).astype(BF16))
    grad_hidden = grad_sum + right_trans(grad_pre, full_up)
    grad_gain_one = jnp.sum(grad_hidden * unit_one, 0)
    grad_shift_one = jnp.sum(grad_hidden, 0)
    grad_resid = norm_back(grad_hidden, unit_one, inverse_one, gain_one)
    grad_bias_out = jnp.sum(grad_resid, 0)
    grad_resid_low = grad_resid.astype(BF16)
    grad_w_out = left_trans(mixed_low, grad_resid_low).astype(BF16)
    grad_mixed = heads(right_trans(grad_resid_low, full_out).astype(BF16))
    grad_probs = jnp.einsum("bhqd,bhkd->bhqk", grad_mixed, vh, preferred_element_type=F32)
    inner = jnp.sum(probs * grad_probs, -1, keepdims=True)
    grad_scores = (probs * (grad_probs - inner) * scale).astype(BF16)
    query_low = flat(jnp.einsum("bhqk,bhkd->bhqd", grad_scores, kh, preferred_element_type=F32).astype(BF16))
    key_low = flat(jnp.einsum("bhqk,bhqd->bhkd", grad_scores, qh, preferred_element_type=F32).astype(BF16))
    value_low = flat(jnp.einsum("bhqk,bhqd->bhkd", probs_low, grad_mixed, preferred_element_type=F32).astype(BF16))
    grad_bias_query = jnp.sum(query_low.astype(F32), 0)
    grad_bias_value = jnp.sum(value_low.astype(F32), 0)
    blocks = [
        part.reshape(shards, block, width)
        for part in (
            left_trans(tokens, query_low).astype(BF16),
            left_trans(tokens, key_low).astype(BF16),
            left_trans(tokens, value_low).astype(BF16),
            grad_w_out,
        )
    ]
    g_first = reduced(jnp.concatenate(blocks, 1).reshape(shards * 4 * block, width))
    grad_tokens = (
        grad_resid
        + right_trans(query_low, full_query)
        + right_trans(key_low, full_key)
        + right_trans(value_low, full_value)
    )
    grad_input = grad_tokens.astype(BF16).reshape(batches, rows, width)
    vec_terms = (
        grad_bias_query, grad_bias_value, grad_bias_out, grad_gain_one, grad_shift_one,
        grad_bias_down, grad_gain_two, grad_shift_two, grad_bias_up,
    )
    g_vec = jnp.concatenate([part.reshape(shards, -1) for part in vec_terms], 1)
    g_vec = lax.psum(g_vec, ("shard", "rep"))
    g_vec = lax.dynamic_index_in_dim(g_vec, shard_index, 0, keepdims=False)
    (g_bquery, g_bvalue, g_bout, g_gain_one, g_shift_one, g_bdown, g_gain_two, g_shift_two, g_bup) = [
        g_vec[cuts[i] : cuts[i + 1]] for i in range(len(small))
    ]
    g_down = over_rep(g_down)
    g_up = over_rep(g_up)
    g_first = over_rep(g_first).reshape(4, block, width)
    return (
        layer_out, grad_input, g_first[0], g_first[1], g_first[2], g_first[3],
        g_bquery, g_bvalue, g_bout, g_gain_one, g_shift_one,
        g_up, g_bup, g_down, g_bdown, g_gain_two, g_shift_two,
    )


def solution(mesh):
    seqs = P(("shard", "rep"), None, None)
    mat = P("shard", None)
    vec = P("shard")
    in_specs = (
        seqs, P(), P(), mat, mat, mat, mat, vec, vec, vec, vec, vec, mat, vec, mat, vec, vec, vec, seqs,
    )
    out_specs = (
        seqs, seqs, mat, mat, mat, mat, vec, vec, vec, vec, vec, mat, vec, mat, vec, vec, vec,
    )
    shape = dict(mesh.shape)
    local = local_eight if shape["shard"] == 8 and shape["rep"] == 4 else local_general
    return jax.shard_map(local, mesh=mesh, in_specs=in_specs, out_specs=out_specs, check_vma=False)
```

```python
import math

import jax
import jax.numpy as jnp
from jax import lax
from jax.experimental import pallas as pl
from jax.experimental.pallas import tpu as pltpu
from jax.sharding import PartitionSpec as P

H = 16
HD = 64
EPS = 1e-05
NEG = -1e30
F32 = jnp.float32
BF16 = jnp.bfloat16


def matmul(left, right):
    return jnp.dot(left, right, preferred_element_type=F32)


def left_trans(left, right):
    return lax.dot_general(left, right, (((0,), (0,)), ((), ())), preferred_element_type=F32)


def right_trans(left, right):
    return lax.dot_general(left, right, (((1,), (1,)), ((), ())), preferred_element_type=F32)


def normalize(values, gain, shift):
    center = values - jnp.mean(values, -1, keepdims=True)
    inverse = lax.rsqrt(jnp.mean(center * center, -1, keepdims=True) + EPS)
    unit = center * inverse
    return (unit * gain + shift, unit, inverse)


def norm_back(grad, unit, inverse, gain):
    scaled = grad * gain
    return inverse * (
        scaled
        - jnp.mean(scaled, -1, keepdims=True)
        - unit * jnp.mean(scaled * unit, -1, keepdims=True)
    )


def gelu_both(pre):
    cumul = 0.5 * (1.0 + lax.erf(pre * 0.7071067811865476))
    density = jnp.exp(-0.5 * pre * pre) * 0.3989422804014327
    return (pre * cumul, cumul + pre * density)


VMEM = 56 * 1024 * 1024
TIGHT = ()
ANY = pl.BlockSpec(memory_space=pl.ANY)
DMA = pltpu.SemaphoreType.DMA


def spec(shape, index):
    return pl.BlockSpec(shape, index)


def whole(shape):
    zeros = (0,) * len(shape)
    return pl.BlockSpec(shape, lambda *_: zeros)


def sds(shape, dtype):
    return jax.ShapeDtypeStruct(shape, dtype)


def room(specs, shapes, scratch):
    total = 8 * 1024 * 1024
    for block, shape in zip(specs, shapes):
        if block.block_shape is not None:
            total += 2 * math.prod(block.block_shape) * shape.dtype.itemsize
    for item in scratch:
        if item.memory_space == pltpu.VMEM:
            total += math.prod(item.shape) * jnp.dtype(item.dtype).itemsize
    return total


def call(kernel, grid, in_specs, out_specs, out_shape, scratch):
    def run(*args):
        outs = out_shape if isinstance(out_shape, (list, tuple)) else [out_shape]
        specs = out_specs if isinstance(out_specs, (list, tuple)) else [out_specs]
        limit = VMEM
        if kernel.__qualname__.split(".")[0] in TIGHT:
            limit = room(list(in_specs) + list(specs), list(args[1:]) + list(outs), scratch)
        return pl.pallas_call(
            kernel,
            grid_spec=pltpu.PrefetchScalarGridSpec(
                num_scalar_prefetch=1,
                grid=grid,
                in_specs=in_specs,
                out_specs=out_specs,
                scratch_shapes=list(scratch),
            ),
            out_shape=out_shape,
            compiler_params=pltpu.CompilerParams(vmem_limit_bytes=limit),
            cost_estimate=pl.CostEstimate(flops=1024, bytes_accessed=1024, transcendentals=0),
        )(*args)

    return run


def dot_nn(a, b):
    return lax.dot_general(a, b, (((1,), (0,)), ((), ())), preferred_element_type=F32)


def dot_nt(a, b):
    return lax.dot_general(a, b, (((1,), (1,)), ((), ())), preferred_element_type=F32)


def dot_tn(a, b):
    return lax.dot_general(a, b, (((0,), (0,)), ((), ())), preferred_element_type=F32)


def fetch(meta, parts, target, sems, low, high, columns=None):
    cut = parts[3].shape[0]
    each = len(parts) // 2
    for core in range(2):
        for chip in range(4):
            at = meta[0] ^ (2 * chip + core)
            if chip < 3:
                pieces = [(parts[each * core + chip], low, high, 0)]
            else:
                pieces = []
                if low < cut:
                    pieces.append((parts[each * core + 3], low, min(high, cut), 0))
                if high > cut:
                    start = max(low, cut)
                    pieces.append((parts[each * core + 4], start - cut, high - cut, start - low))
            for ref, begin, end, offset in pieces:
                source = ref.at[pl.ds(begin, end - begin)]
                if columns is not None:
                    source = ref.at[pl.ds(begin, end - begin), columns]
                goal = target.at[at]
                if len(pieces) > 1:
                    goal = target.at[at, pl.ds(offset, end - begin)]
                pltpu.make_async_copy(source, goal, sems.at[at]).start()


def arrived(target, sem):
    pltpu.make_async_copy(target, target, sem).wait()


def hand_over(meta, source, target, sems, block):
    copies = []
    for chip in range(4):
        at = pl.ds(pl.multiple_of((meta[0] ^ (2 * chip + 1)) * block, block), block)
        copies.append(pltpu.make_async_copy(source.at[:, at], target.at[chip], sems.at[chip]))
        copies[-1].start()
    return copies


def project(meta, tokens, first):
    rows, width = tokens.shape
    tile = 512
    count = width // tile

    def kernel(meta, x_ref, *refs):
        parts, (out_ref, vec_ref, up_ref, give_ref, held, short, made, sems, short_sems, out_sems, give_sems) = refs[: len(first)], refs[len(first) :]
        for w in range(3):
            fetch(meta, parts, held.at[w], sems.at[w], 128 * w, 128 * (w + 1))
            if w == 0:
                fetch(meta, parts, short, short_sems, 512, 528)
        gifts = hand_over(meta, x_ref, give_ref, give_sems, 128)
        for b in range(8):
            arrived(short.at[b], short_sems.at[b])
        for b in range(8):
            two = short[b].astype(F32)
            for v in range(8):
                vec_ref[v : v + 1, 128 * b : 128 * (b + 1)] = two[0:1, 128 * v : 128 * (v + 1)]
            up_ref[0:1, 512 * b : 512 * (b + 1)] = two[1:2, :512]

        def body(i, carry):
            w, n = i // count, i % count

            @pl.when(n == 0)
            def _():
                for b in range(8):
                    arrived(held.at[w, b], sems.at[w, b])

            at = pl.ds(pl.multiple_of(n * tile, tile), tile)
            weight = held[w, :, :, at].reshape(width, tile)
            bias = jnp.where(w == 0, vec_ref[0:1, at], vec_ref[1:2, at])
            bias = jnp.where(w == 1, jnp.zeros_like(bias), bias)
            made[w, :, at] = (dot_nn(x_ref[...], weight) + bias).astype(BF16)

            @pl.when(n == count - 1)
            def _():
                pltpu.make_async_copy(made.at[w], out_ref.at[w], out_sems.at[w]).start()

            return carry

        lax.fori_loop(0, 3 * count, body, 0)
        for w in range(3):
            pltpu.make_async_copy(made.at[w], out_ref.at[w], out_sems.at[w]).wait()
        for copy in gifts:
            copy.wait()

    return call(
        kernel,
        (1,),
        [whole((rows, width))] + [ANY] * len(first),
        [ANY, whole((8, width)), whole((1, 4 * width)), ANY],
        [sds((3, rows, width), BF16), sds((8, width), F32), sds((1, 4 * width), F32), sds((4, rows, 128), BF16)],
        [
            pltpu.VMEM((3, 8, 128, width), BF16), pltpu.VMEM((8, 16, width), BF16),
            pltpu.VMEM((3, rows, width), BF16), DMA((3, 8)), DMA((8,)), DMA((3,)), DMA((4,)),
        ],
    )(meta, tokens, *first)


HEADS = 4


def attend(meta, qkv, batches, rows):
    total, width = qkv.shape[1:]
    span = HEADS * HD
    steps = width // span

    def kernel(meta, q_ref, k_ref, v_ref, mixed_ref, raised_ref, inverse_ref):
        length = meta[1 + pl.program_id(0)]
        allowed = lax.broadcasted_iota(jnp.int32, (1, rows), 1) < length
        shift = jnp.where(allowed, 0.0, NEG)
        left = lax.broadcasted_iota(jnp.int32, (rows, 128), 1) < HD
        one = jnp.ones((rows, 128), BF16)
        for pair in range(HEADS // 2):
            cols = slice(128 * pair, 128 * (pair + 1))
            query, keyed, value = q_ref[0, :, cols] * jnp.asarray(HD**-0.5, BF16), k_ref[0, :, cols], v_ref[0, :, cols]
            outs = []
            for half in range(2):
                mine = left if half == 0 else jnp.logical_not(left)
                scores = dot_nt(jnp.where(mine, query, jnp.zeros_like(query)), keyed) + shift
                raised = jnp.exp(scores - jnp.max(scores, -1, keepdims=True)).astype(BF16)
                raised_ref[0, 2 * pair + half] = raised
                outs.append(dot_nn(raised, jnp.where(mine, value, one)))
            inverse = 1.0 / pltpu.roll(jnp.where(left, outs[1], outs[0]), HD, 1)
            inverse_ref[:, cols] = inverse
            mixed_ref[:, cols] = (jnp.where(left, outs[0], outs[1]) * inverse).astype(BF16)

    part = lambda w: spec((1, rows, span), lambda b, h, meta: (w, b, h))
    here = spec((rows, span), lambda b, h, meta: (b, h))
    return call(
        kernel,
        (batches, steps),
        [part(0), part(1), part(2)],
        [here, spec((1, HEADS, rows, rows), lambda b, h, meta: (b, h, 0, 0)), here],
        [sds((total, width), BF16), sds((batches, H, rows, rows), BF16), sds((total, width), F32)],
        [],
    )(meta, qkv, qkv, qkv)


def mix_out(meta, mixed, tokens, first, vecs):
    total, width = mixed.shape
    tile = 128

    def kernel(meta, mixed_ref, tokens_ref, vec_ref, *refs):
        parts, (unit_ref, inv_ref, low_ref, give_ref, held, sems, give_sems) = refs[: len(first)], refs[len(first) :]
        fetch(meta, parts, held, sems, 384, 512)
        gifts = hand_over(meta, mixed_ref, give_ref.at[0], give_sems.at[0], 128)
        for b in range(8):
            arrived(held.at[b], sems.at[b])

        def body(i, carry):
            here = pl.ds(pl.multiple_of(i * tile, tile), tile)
            branch = dot_nn(mixed_ref[here], held[...].reshape(width, width)) + vec_ref[2:3]
            hidden, unit, inverse = normalize(tokens_ref[here].astype(F32) + branch, vec_ref[3:4], vec_ref[4:5])
            unit_ref[here] = unit
            inv_ref[here] = jnp.broadcast_to(inverse, (tile, 128))
            low_ref[here] = hidden.astype(BF16)
            return carry

        lax.fori_loop(0, total // tile, body, 0)
        gifts += hand_over(meta, low_ref, give_ref.at[1], give_sems.at[1], 128)
        for copy in gifts:
            copy.wait()

    block = (total, width)
    return call(
        kernel,
        (1,),
        [whole(block), whole(block), whole(vecs.shape)] + [ANY] * len(first),
        [whole(block), whole((total, 128)), whole(block), ANY],
        [sds(block, F32), sds((total, 128), F32), sds(block, BF16), sds((2, 4, total, 128), BF16)],
        [pltpu.VMEM((8, 128, width), BF16), DMA((8,)), DMA((2, 4))],
    )(meta, mixed, tokens, vecs, *first)


def feed_up(meta, low, up, bias):
    total, width = low.shape
    wide = up[0].shape[1]
    strip, tile = 512, 512
    strips, inner = wide // strip, strip // tile

    def kernel(meta, x_ref, bias_ref, *refs):
        parts, (act_ref, slope_ref, give_ref, held, act, slope, sems, out_sems, give_sems) = refs[: len(up)], refs[len(up) :]
        for t in range(strips):
            fetch(meta, parts, held.at[t], sems.at[t], 0, 128, pl.ds(strip * t, strip))

        def leave(i):
            at = pl.ds(pl.multiple_of(i * tile, tile), tile)
            return (
                pltpu.make_async_copy(act.at[i], act_ref.at[:, at], out_sems.at[0, i]),
                pltpu.make_async_copy(slope.at[i], slope_ref.at[:, at], out_sems.at[1, i]),
            )

        def body(i, carry):
            t, n = i // inner, i % inner

            @pl.when(n == 0)
            def _():
                for b in range(8):
                    arrived(held.at[t, b], sems.at[t, b])

            weight = held[t, :, :, pl.ds(pl.multiple_of(n * tile, tile), tile)].reshape(width, tile)
            pre = dot_nn(x_ref[...], weight) + bias_ref[:, pl.ds(pl.multiple_of(i * tile, tile), tile)]
            value, grad = gelu_both(pre)
            act[i] = value.astype(BF16)
            slope[i] = grad.astype(BF16)
            for copy in leave(i):
                copy.start()
            code = meta[0] ^ i

            @pl.when(code % 2 == 1)
            def _():
                pltpu.make_async_copy(act.at[i], give_ref.at[code // 2], give_sems.at[code // 2]).start()

            return carry

        lax.fori_loop(0, strips * inner, body, 0)
        for i in range(strips * inner):
            for copy in leave(i):
                copy.wait()
        for chip in range(4):
            arrived(give_ref.at[chip], give_sems.at[chip])

    out = sds((total, wide), BF16)
    tiles = wide // tile
    return call(
        kernel,
        (1,),
        [whole((total, width)), whole((1, wide))] + [ANY] * len(up),
        [ANY, ANY, ANY],
        [out, out, sds((4, total, tile), BF16)],
        [
            pltpu.VMEM((strips, 8, 128, strip), BF16), pltpu.VMEM((tiles, total, tile), BF16),
            pltpu.VMEM((tiles, total, tile), BF16), DMA((strips, 8)), DMA((2, tiles)), DMA((4,)),
        ],
    )(meta, low, bias, *up)


def feed_down(meta, act, slope, down, unit_one, cot_pool, vecs, batches, rows):
    total, wide = act.shape
    width = down[0].shape[1]
    chunk = 128

    def kernel(meta, act_ref, slope_ref, unit_ref, cot_ref, vec_ref, *refs):
        parts = refs[: len(down)]
        (
            out_ref, sum_ref, low_ref, grad_ref, pre_ref, bias_ref, out, grad_sums, low, early,
            held, left, right, total_ref, unit, cot, sems, left_sems, right_sems, out_sems, more,
        ) = refs[len(down) :]
        for b in range(8):
            pltpu.make_async_copy(act_ref.at[:, pl.ds(512 * b, 512)], left.at[b], left_sems.at[b]).start()
        fetch(meta, parts, held, sems, 0, 512)
        rest = [pltpu.make_async_copy(unit_ref, unit, more.at[0])] + [
            pltpu.make_async_copy(cot_ref.at[meta[3 + i]], cot.at[i], more.at[1 + i]) for i in range(batches)
        ]

        def add(b, carry):
            arrived(left.at[b], left_sems.at[b])
            arrived(held.at[b], sems.at[b])

            @pl.when(b == 4)
            def _():
                for copy in rest:
                    copy.start()
                for c in range(8):
                    at = pl.ds(512 * c, 512)
                    pltpu.make_async_copy(slope_ref.at[:, at], right.at[c], right_sems.at[c]).start()

            part = dot_nn(left[b], held[b])

            @pl.when(b == 0)
            def _():
                total_ref[...] = part

            @pl.when(b > 0)
            def _():
                total_ref[...] += part

            return carry

        lax.fori_loop(0, 8, add, 0)
        for copy in rest:
            copy.wait()
        grad_ref[...] = jnp.zeros_like(grad_ref)

        def body(i, carry):
            here = pl.ds(pl.multiple_of(i * chunk, chunk), chunk)
            batch = i // (rows // chunk)
            at = pl.multiple_of((i % (rows // chunk)) * chunk, chunk)
            summed = (unit[here] * vec_ref[3:4] + vec_ref[4:5]) + total_ref[here] + vec_ref[5:6]
            normed, unit_two, inverse = normalize(summed, vec_ref[6:7], vec_ref[7:8])
            place = at + lax.broadcasted_iota(jnp.int32, (chunk, 1), 0)
            valid = place < meta[1 + batch]
            out[here] = jnp.where(valid, normed, 0.0).astype(BF16)
            grad_out = jnp.where(valid, cot[batch, pl.ds(at, chunk)].astype(F32), 0.0)
            grad_sum = norm_back(grad_out, unit_two, inverse, vec_ref[6:7])
            grad_sums[here] = grad_sum
            low[here] = grad_sum.astype(BF16)
            grad_ref[0:1] += jnp.sum(grad_out * unit_two, 0, keepdims=True)
            grad_ref[1:2] += jnp.sum(grad_out, 0, keepdims=True)
            grad_ref[2:3] += jnp.sum(grad_sum, 0, keepdims=True)
            return carry

        lax.fori_loop(0, total // chunk, body, 0)
        leaving = [
            pltpu.make_async_copy(source, target, early.at[i])
            for i, (source, target) in enumerate(((low, low_ref), (out, out_ref), (grad_sums, sum_ref)))
        ]
        for copy in leaving:
            copy.start()

        def leave(b):
            at = pl.ds(pl.multiple_of(512 * b, 512), 512)
            return pltpu.make_async_copy(left.at[b], pre_ref.at[:, at], out_sems.at[b])

        def through(b, carry):
            arrived(right.at[b], right_sems.at[b])
            grad = (dot_nt(low[...], held[b]) * right[b].astype(F32)).astype(BF16)
            left[b] = grad
            leave(b).start()
            bias_ref[:, pl.ds(pl.multiple_of(512 * b, 512), 512)] = jnp.sum(grad.astype(F32), 0, keepdims=True)
            return carry

        lax.fori_loop(0, 8, through, 0)
        for b in range(8):
            leave(b).wait()
        for copy in leaving:
            copy.wait()

    block = (total, width)
    return call(
        kernel,
        (1,),
        [ANY, ANY, ANY, ANY, whole(vecs.shape)] + [ANY] * len(down),
        [ANY, ANY, ANY, whole((8, width)), ANY, whole((1, wide))],
        [
            sds(block, BF16), sds(block, F32), sds(block, BF16), sds((8, width), F32),
            sds((total, wide), BF16), sds((1, wide), F32),
        ],
        [
            pltpu.VMEM(block, BF16), pltpu.VMEM(block, F32), pltpu.VMEM(block, BF16), DMA((3,)),
            pltpu.VMEM((8, 512, width), BF16), pltpu.VMEM((8, total, 512), BF16), pltpu.VMEM((8, total, 512), BF16),
            pltpu.VMEM(block, F32), pltpu.VMEM(block, F32), pltpu.VMEM((batches, rows, width), BF16),
            DMA((8,)), DMA((8,)), DMA((8,)), DMA((8,)), DMA((1 + batches,)),
        ],
    )(meta, act, slope, unit_one, cot_pool, vecs, *down)


def back_up(meta, pre, up, first, grad_sum, unit_one, inverse_one, vecs):
    total, wide = pre.shape
    width = grad_sum.shape[1]
    chunk, strip = 128, 1024
    strips = wide // strip

    def kernel(meta, pre_ref, sum_ref, unit_ref, inv_ref, vec_ref, *refs):
        parts, others = refs[: len(up)], refs[len(up) : len(up) + len(first)]
        (
            resid_ref, low_ref, mixed_ref, grad_ref,
            held, pres, out_held, hidden, unit, low, mixed, sems, pre_sems, out_sems, more, leave_sems,
        ) = refs[len(up) + len(first) :]
        for t in range(strips):
            at = pl.ds(strip * t, strip)
            pltpu.make_async_copy(pre_ref.at[:, at], pres.at[t], pre_sems.at[t]).start()
            fetch(meta, parts, held.at[t], sems.at[t], 0, 128, at)
            if t == 0:
                incoming = pltpu.make_async_copy(sum_ref, hidden, more.at[0])
                incoming.start()
        other = pltpu.make_async_copy(unit_ref, unit, more.at[1])
        other.start()
        fetch(meta, others, out_held, out_sems, 384, 512)
        incoming.wait()

        def through(t, carry):
            arrived(pres.at[t], pre_sems.at[t])
            for b in range(8):
                arrived(held.at[t, b], sems.at[t, b])
            hidden[...] += dot_nt(pres[t], held[t].reshape(width, strip))
            return carry

        lax.fori_loop(0, strips, through, 0)
        other.wait()
        grad_ref[...] = jnp.zeros_like(grad_ref)

        def body(i, carry):
            here = pl.ds(pl.multiple_of(i * chunk, chunk), chunk)
            grad, unit_here = hidden[here], unit[here]
            grad_ref[0:1] += jnp.sum(grad * unit_here, 0, keepdims=True)
            grad_ref[1:2] += jnp.sum(grad, 0, keepdims=True)
            resid = norm_back(grad, unit_here, inv_ref[here, 0:1], vec_ref[3:4])
            grad_ref[2:3] += jnp.sum(resid, 0, keepdims=True)
            hidden[here] = resid
            low[here] = resid.astype(BF16)
            return carry

        lax.fori_loop(0, total // chunk, body, 0)
        leaving = [
            pltpu.make_async_copy(low, low_ref, leave_sems.at[0]), pltpu.make_async_copy(hidden, resid_ref, leave_sems.at[1])
        ]
        for copy in leaving:
            copy.start()
        for b in range(8):
            arrived(out_held.at[b], out_sems.at[b])

        def leave(j):
            at = pl.ds(pl.multiple_of(512 * j, 512), 512)
            return pltpu.make_async_copy(mixed.at[:, at], mixed_ref.at[:, at], leave_sems.at[2 + j])

        def out(j, carry):
            weight = out_held[pl.ds(4 * j, 4)].reshape(512, width)
            mixed[:, pl.ds(pl.multiple_of(512 * j, 512), 512)] = dot_nt(low[...], weight).astype(BF16)
            leave(j).start()
            return carry

        lax.fori_loop(0, 2, out, 0)
        for copy in leaving + [leave(0), leave(1)]:
            copy.wait()

    block = (total, width)
    return call(
        kernel,
        (1,),
        [ANY, ANY, ANY, whole((total, 128)), whole(vecs.shape)] + [ANY] * (len(up) + len(first)),
        [ANY, ANY, ANY, whole((8, width))],
        [sds(block, F32), sds(block, BF16), sds(block, BF16), sds((8, width), F32)],
        [
            pltpu.VMEM((strips, 8, 128, strip), BF16), pltpu.VMEM((strips, total, strip), BF16),
            pltpu.VMEM((8, 128, width), BF16), pltpu.VMEM(block, F32), pltpu.VMEM(block, F32), pltpu.VMEM(block, BF16),
            pltpu.VMEM(block, BF16), DMA((strips, 8)), DMA((strips,)), DMA((8,)), DMA((2,)), DMA((4,)),
        ],
    )(meta, pre, grad_sum, unit_one, inverse_one, vecs, *up, *first)


def attend_back(meta, qkv, mixed, raised, inverse, grad_mixed, grads_one, grads_two, bias_up, batches, rows):
    total, width = grad_mixed.shape
    span = HEADS * HD
    steps = width // span

    def kernel(meta, q_ref, k_ref, v_ref, mixed_ref, g_ref, raised_ref, inv_ref, one_ref, two_ref, up_ref, out_ref, vec_ref, sums):
        batch, step = pl.program_id(0), pl.program_id(1)
        left = lax.broadcasted_iota(jnp.int32, (rows, 128), 1) < HD
        none = jnp.zeros((rows, 128), BF16)

        @pl.when((batch == 0) & (step == 0))
        def _():
            sums[...] = jnp.zeros_like(sums)

        for pair in range(HEADS // 2):
            cols = slice(128 * pair, 128 * (pair + 1))
            query, keyed, value = q_ref[0, :, cols] * jnp.asarray(HD**-0.5, BF16), k_ref[0, :, cols], v_ref[0, :, cols]
            grad = g_ref[:, cols].astype(F32) * inv_ref[:, cols]
            both = grad * mixed_ref[:, cols].astype(F32)
            grad = grad.astype(BF16)
            got = ([], [], [])
            for half in range(2):
                mine = left if half == 0 else jnp.logical_not(left)
                low = raised_ref[0, 2 * pair + half]
                inner = jnp.sum(jnp.where(mine, both, 0.0), -1, keepdims=True)
                slope = dot_nt(jnp.where(mine, grad, none), value) - inner
                scores = (low.astype(F32) * slope).astype(BF16)
                got[0].append(dot_nn(scores, keyed))
                got[1].append(dot_tn(scores, query))
                got[2].append(dot_tn(low, grad))
            for i in range(3):
                part = jnp.where(left, got[i][0], got[i][1])
                if i == 0:
                    part = part * (HD**-0.5)
                part = part.astype(BF16)
                out_ref[i, :, cols] = part
                if i != 1:
                    at = pl.ds(pl.multiple_of(step * span, span) + 128 * pair, 128)
                    sums[i : i + 1, at] += jnp.sum(part.astype(F32), 0, keepdims=True)

        @pl.when((batch == batches - 1) & (step == steps - 1))
        def _():
            vec_ref[...] = jnp.zeros_like(vec_ref)
            rows_of = (
                sums[0:1], sums[2:3], one_ref[2:3], one_ref[0:1], one_ref[1:2], two_ref[2:3], two_ref[0:1], two_ref[1:2]
            )
            table = jnp.concatenate(rows_of, 0).astype(BF16)
            for b in range(8):
                vec_ref[b, 0:8, 0:128] = table[:, 128 * b : 128 * (b + 1)]
                vec_ref[b, 8:9, 0:512] = up_ref[:, 512 * b : 512 * (b + 1)].astype(BF16)

    part = lambda w: spec((1, rows, span), lambda b, h, meta: (w, b, h))
    here = spec((rows, span), lambda b, h, meta: (b, h))
    return call(
        kernel,
        (batches, steps),
        [
            part(0), part(1), part(2), here, here, spec((1, HEADS, rows, rows), lambda b, h, meta: (b, h, 0, 0)), here,
            whole((8, width)), whole((8, width)), whole((1, 4 * width)),
        ],
        [spec((3, rows, span), lambda b, h, meta: (0, b, h)), whole((8, 16, width))],
        [sds((3, total, width), BF16), sds((8, 16, width), BF16)],
        [pltpu.VMEM((8, width), F32)],
    )(meta, qkv, qkv, qkv, mixed, grad_mixed, raised, inverse, grads_one, grads_two, bias_up)


def back_project(meta, grads, first, grad_resid):
    total, width = grad_resid.shape

    def kernel(meta, g_ref, resid_ref, *refs):
        parts, (out_ref, held, resid, made, sems, more, out_sems) = refs[: len(first)], refs[len(first) :]
        fetch(meta, parts, held, sems, 0, 384)
        incoming = pltpu.make_async_copy(resid_ref, resid, more)
        incoming.start()
        incoming.wait()

        def leave(j):
            at = pl.ds(pl.multiple_of(256 * j, 256), 256)
            return pltpu.make_async_copy(made.at[:, at], out_ref.at[:, at], out_sems.at[j])

        def body(j, carry):
            for b in range(2):
                arrived(held.at[2 * j + b], sems.at[2 * j + b])
            at = pl.ds(pl.multiple_of(256 * j, 256), 256)
            part = resid[:, at]
            for w in range(3):
                weight = held[pl.ds(2 * j, 2), 128 * w : 128 * (w + 1)].reshape(256, width)
                part = part + dot_nt(g_ref[w], weight)
            made[:, at] = part.astype(BF16)
            leave(j).start()
            return carry

        lax.fori_loop(0, 4, body, 0)
        for j in range(4):
            leave(j).wait()

    block = (total, width)
    return call(
        kernel,
        (1,),
        [whole((3, total, width)), ANY] + [ANY] * len(first),
        ANY,
        sds(block, BF16),
        [
            pltpu.VMEM((8, 384, width), BF16), pltpu.VMEM(block, F32), pltpu.VMEM(block, BF16), DMA((8,)), DMA(()),
            DMA((4,)),
        ],
    )(meta, grads, grad_resid, *first)


def ship(made, outs, sems, half, i):
    def copy(target):
        return pltpu.make_async_copy(made.at[half, i], target, sems.at[half, i])

    if isinstance(i, int):
        copy(outs[half].at[i] if i < 2 else outs[2 * i - 2 + half]).start()
        return

    @pl.when(i < 2)
    def _():
        copy(outs[half].at[jnp.minimum(i, 1)]).start()

    @pl.when(i == 2)
    def _():
        copy(outs[2 + half]).start()

    @pl.when(i == 3)
    def _():
        copy(outs[4 + half]).start()


def shipped(made, sems):
    for half in range(2):
        for i in range(4):
            arrived(made.at[half, i], sems.at[half, i])


def chip_of(half, i):
    return (i + 2) % 4 if half == 0 else (2 * i + 1) % 5


def six(rows, cols):
    return [sds((2, rows, cols), BF16)] * 2 + [sds((rows, cols), BF16)] * 4


def load_lefts(meta, own_ref, got_ref, lefts, sems, block, total):
    for chip in (2, 3, 1, 0):
        at = pl.ds(pl.multiple_of((meta[0] ^ (2 * chip)) * block, block), block)
        pltpu.make_async_copy(own_ref.at[:, at], lefts.at[chip, pl.ds(0, total)], sems.at[chip]).start()
        pltpu.make_async_copy(got_ref.at[chip], lefts.at[chip, pl.ds(total, total)], sems.at[chip]).start()


def load_right(own, got, target, sem, total):
    pltpu.make_async_copy(own, target.at[pl.ds(0, total)], sem).start()
    pltpu.make_async_copy(got, target.at[pl.ds(total, total)], sem).start()


def down_grad(meta, act, act_got, low, low_got):
    total, width = low.shape
    block, share = 512, width // 2

    def kernel(meta, left_ref, left_got, right_ref, right_got, *refs):
        outs, (lefts, rights, made, left_sems, right_sems, out_sems) = refs[:6], refs[6:]
        for half in range(2):
            at = pl.ds(share * half, share)
            load_right(right_ref.at[:, at], right_got.at[:, at], rights.at[half], right_sems.at[half], total)
            if half == 0:
                load_lefts(meta, left_ref, left_got, lefts, left_sems, block, total)
        for half in range(2):
            arrived(rights.at[half], right_sems.at[half])

            def body(i, carry):
                chip = chip_of(half, i)
                if half == 0:
                    arrived(lefts.at[chip], left_sems.at[chip])
                made[half, i] = dot_tn(lefts[chip], rights[half]).astype(BF16)
                ship(made, outs, out_sems, half, i)
                return carry

            lax.fori_loop(0, 4, body, 0)
        shipped(made, out_sems)

    outs = call(
        kernel,
        (1,),
        [ANY] * 4,
        [ANY] * 6,
        six(block, share),
        [
            pltpu.VMEM((4, 2 * total, block), BF16), pltpu.VMEM((2, 2 * total, share), BF16),
            pltpu.VMEM((2, 4, block, share), BF16), DMA((4,)), DMA((2,)), DMA((2, 4)),
        ],
    )(meta, act, act_got, low, low_got)
    return outs[:2], outs[2:4], outs[4:]


def load_columns(meta, own_ref, got_ref, target, sem, total):
    for chip in range(4):
        at = pl.ds(pl.multiple_of((meta[0] ^ (2 * chip)) * 128, 128), 128)
        cols = pl.ds(128 * chip, 128)
        pltpu.make_async_copy(own_ref.at[:, at], target.at[pl.ds(0, total), cols], sem).start()
        pltpu.make_async_copy(got_ref.at[chip], target.at[pl.ds(total, total), cols], sem).start()


ORDER = ((2, 3, 0, 1), (1, 3, 0, 2))


def up_grad(meta, hidden, hidden_got, pre, pre_got):
    total, width = hidden.shape
    wide = pre.shape[1]
    tile = 1024
    tiles = wide // tile // 2

    def kernel(meta, x_ref, x_got, pre_ref, pre_got, *refs):
        outs, (lefts, rights, made, left_sem, right_sems, out_sems) = refs[:6], refs[6:]
        for t in range(2 * tiles):
            at = pl.ds(tile * t, tile)
            load_right(pre_ref.at[:, at], pre_got.at[:, at], rights.at[t], right_sems.at[t], total)
            if t == 0:
                load_columns(meta, x_ref, x_got.at[1], lefts, left_sem, total)
        arrived(lefts, left_sem)
        for half in range(2):

            def body(t, carry):
                arrived(rights.at[half * tiles + t], right_sems.at[half * tiles + t])
                part = dot_tn(lefts[...], rights[half * tiles + t]).astype(BF16)
                at = pl.ds(pl.multiple_of(t * tile, tile), tile)
                for i, chip in enumerate(ORDER[half]):
                    made[half, i, :, at] = part[128 * chip : 128 * (chip + 1)]
                return carry

            lax.fori_loop(0, tiles, body, 0)
            for i in range(4):
                ship(made, outs, out_sems, half, i)
        shipped(made, out_sems)

    outs = call(
        kernel,
        (1,),
        [ANY] * 4,
        [ANY] * 6,
        six(128, wide // 2),
        [
            pltpu.VMEM((2 * total, 512), BF16), pltpu.VMEM((2 * tiles, 2 * total, tile), BF16),
            pltpu.VMEM((2, 4, 128, wide // 2), BF16), DMA(()), DMA((2 * tiles,)), DMA((2, 4)),
        ],
    )(meta, hidden, hidden_got, pre, pre_got)
    return outs[:2], outs[2:4], outs[4:]


def first_grad(meta, tokens, tokens_got, mixed, mixed_got, grads, grads_got, low, low_got, vec, vec_got):
    total, width = tokens.shape
    share = width // 2

    def kernel(meta, x_ref, x_got, m_ref, m_got, g_ref, g_got, low_ref, low_got, vec_ref, vec_got, *refs):
        outs = refs[:6], refs[6:12]
        lefts, rights, made_a, made_b, short, left_sems, right_sems, sems_a, sems_b, short_sems = refs[12:]
        for w in range(4):
            own, got = (g_ref.at[w], g_got.at[w]) if w < 3 else (low_ref, low_got)
            load_right(own, got, rights.at[w], right_sems.at[w], total)
            if w == 0:
                load_columns(meta, x_ref, x_got, lefts.at[0], left_sems.at[0], total)
                for chip in range(4):
                    at = meta[0] ^ (2 * chip)
                    pltpu.make_async_copy(vec_ref.at[at], short.at[chip, 0], short_sems.at[chip]).start()
                    pltpu.make_async_copy(vec_got.at[at], short.at[chip, 1], short_sems.at[chip]).start()
            if w == 2:
                load_columns(meta, m_ref, m_got.at[0], lefts.at[1], left_sems.at[1], total)
        arrived(lefts.at[0], left_sems.at[0])
        for group, (made, sems) in enumerate(((made_a, sems_a), (made_b, sems_b))):

            def body(k, carry):
                arrived(rights.at[2 * group + k], right_sems.at[2 * group + k])
                if group == 1:

                    @pl.when(k == 1)
                    def _():
                        arrived(lefts.at[1], left_sems.at[1])

                part = dot_tn(lefts[k * group], rights[2 * group + k]).astype(BF16)
                rows = pl.ds(pl.multiple_of(128 * k, 128), 128)
                for half in range(2):
                    for i, chip in enumerate(ORDER[half]):
                        made[half, i, rows] = part[128 * chip : 128 * (chip + 1), share * half : share * (half + 1)]
                return carry

            lax.fori_loop(0, 2, body, 0)
            if group == 1:
                for i, chip in enumerate(ORDER[0]):
                    arrived(short.at[chip], short_sems.at[chip])
                    both = short[chip, 0].astype(F32) + short[chip, 1].astype(F32)
                    made[0, i, 256:] = both[:, :share].astype(BF16)
                    made[1, i, 256:] = jnp.zeros((16, share), BF16)
            for half in range(2):
                for i in range(4):
                    ship(made, outs[group], sems, half, i)
        shipped(made_a, sems_a)
        shipped(made_b, sems_b)

    outs = call(
        kernel,
        (1,),
        [ANY] * 10,
        [ANY] * 12,
        six(256, share) + six(272, share),
        [
            pltpu.VMEM((2, 2 * total, 512), BF16), pltpu.VMEM((4, 2 * total, width), BF16),
            pltpu.VMEM((2, 4, 256, share), BF16), pltpu.VMEM((2, 4, 272, share), BF16),
            pltpu.VMEM((4, 2, 16, width), BF16), DMA((2,)), DMA((4,)), DMA((2, 4)), DMA((2, 4)), DMA((4,)),
        ],
    )(meta, tokens, tokens_got, mixed, mixed_got, grads, grads_got, low, low_got, vec, vec_got)
    return [(some[:2], some[2:4], some[4:]) for some in (outs[:6], outs[6:])]


def pack(weights, small):
    block, width = weights[0].shape
    high = block * len(weights) + 16

    def kernel(*refs):
        out_ref = refs[-1]
        for i in range(len(weights)):
            out_ref[block * i : block * (i + 1)] = refs[i][...]
        out_ref[block * len(weights) :] = jnp.zeros((16, width), BF16)
        start = 0
        for ref in refs[len(weights) : -1]:
            count = ref.shape[1]
            row, column = block * len(weights) + start // width, start % width
            out_ref[row : row + 1, column : column + count] = ref[...]
            start += count

    return pl.pallas_call(
        kernel,
        out_shape=jax.ShapeDtypeStruct((high, width), BF16),
        compiler_params=pltpu.CompilerParams(vmem_limit_bytes=VMEM),
        cost_estimate=pl.CostEstimate(flops=1024, bytes_accessed=1024, transcendentals=0),
    )(*weights, *[part.reshape(1, -1) for part in small])


def chosen(meta, pool, first):
    rows, width = pool.shape[1:]

    def kernel(meta, pool_ref, out_ref):
        out_ref[...] = pool_ref[...]

    return call(
        kernel,
        (2,),
        [spec((1, rows, width), lambda i, meta: (meta[first + i], 0, 0))],
        spec((1, rows, width), lambda i, meta: (i, 0, 0)),
        sds((2, rows, width), BF16),
        [],
    )(meta, pool)


CORE, ALONG_X, ALONG_Y = 1, 2, 4


def swap(value, mask):
    return lax.ppermute(value, "shard", [(i, i ^ mask) for i in range(8)])


def plus(*parts):
    total = parts[0].astype(F32)
    for part in parts[1:]:
        total = total + part.astype(F32)
    return total.astype(BF16)


class Order:
    def __init__(self, meta):
        self.meta = meta

    def place(self, *values):
        *values, self.meta = lax.optimization_barrier(values + (self.meta,))
        return values

    def then(self, value):
        self.meta, value = lax.optimization_barrier((self.meta, value))
        return value

    def run(self, function, *values):
        return self.then(function(*self.place(*values)))


def tie(*values):
    return lax.optimization_barrier(values)


def both_cores(*mine):
    return mine + tuple(swap(part, CORE) for part in mine)


def pairs(value, mask):
    return lax.ppermute(value, "rep", [(i, i ^ mask) for i in range(4)])


def turned(rest, got):
    return plus(rest[0], got[0][1]), plus(rest[1], got[1][1])


def passed(values):
    return swap(values[0], ALONG_X), swap(values[1], ALONG_Y)


def sent(values):
    return swap(values[0], ALONG_Y), swap(values[1], ALONG_X)


def summed(own, got, late):
    odd = lax.axis_index("rep") % 2 == 1
    first, second = plus(own[0], got[0][0], late[0]), plus(own[1], got[1][0], late[1])
    return jnp.where(odd, second, first), jnp.where(odd, first, second)


def merge(meta, own, got, late, rest, got_next):
    rows, cols = own[0].shape
    high, wide = rest[0].shape
    steps = 4

    def kernel(meta, own_a, own_b, got_a, got_b, late_a, late_b, rest_a, rest_b, next_a, next_b, *outs):
        kept_ref, given_ref, pass_a, pass_b = outs
        first = own_a[...].astype(F32) + got_a[0].astype(F32) + late_a[...].astype(F32)
        second = own_b[...].astype(F32) + got_b[0].astype(F32) + late_b[...].astype(F32)
        odd = meta[7] == 1
        kept_ref[...] = jnp.where(odd, second, first).astype(BF16)
        given_ref[...] = jnp.where(odd, first, second).astype(BF16)
        pass_a[...] = (rest_a[...].astype(F32) + next_a[0].astype(F32)).astype(BF16)
        pass_b[...] = (rest_b[...].astype(F32) + next_b[0].astype(F32)).astype(BF16)

    flat = spec((rows // steps, cols), lambda i, meta: (i, 0))
    mine = spec((1, rows // steps, cols), lambda i, meta: (0, i, 0))
    low = spec((high // steps, wide), lambda i, meta: (i, 0))
    other = spec((1, high // steps, wide), lambda i, meta: (1, i, 0))
    kept, given, *passing = call(
        kernel,
        (steps,),
        [flat, flat, mine, mine, flat, flat, low, low, other, other],
        [flat, flat, low, low],
        [sds((rows, cols), BF16)] * 2 + [sds((high, wide), BF16)] * 2,
        [],
    )(meta, *own, *got, *late, *rest, *got_next)
    return kept, given, tuple(passing)


def unfolded(mine, other):
    odd = lax.axis_index("rep") % 2 == 1
    return jnp.where(odd, other, mine).astype(F32), jnp.where(odd, mine, other).astype(F32)


def local_eight(
    inputs, lengths, dealing, w_query, w_key, w_value, w_out, b_query, b_value, b_out,
    ln1_gain, ln1_bias, w_up, b_up, w_down, b_down, ln2_gain, ln2_bias, cotangent,
):
    batches, rows, width = inputs.shape
    wide = w_up.shape[1]
    total = batches * rows
    group = batches * 4
    shard_index = lax.axis_index("shard")
    anchor = shard_index * group
    slots = anchor + lax.axis_index("rep") * batches + jnp.arange(batches, dtype=jnp.int32)
    local_dealing = lax.dynamic_slice_in_dim(dealing, anchor, group) - anchor
    sources = jnp.take(dealing, slots) - anchor
    places = jnp.arange(group, dtype=jnp.int32)
    wanted = jnp.sum(
        jnp.where(local_dealing[None, :] == (slots - anchor)[:, None], places[None, :], 0), 1
    )
    meta = jnp.concatenate([shard_index[None].astype(jnp.int32), jnp.take(lengths, slots), wanted, jnp.clip(sources, 0, group - 1), (lax.axis_index("rep") % 2)[None].astype(jnp.int32)])
    order = Order(meta)
    tokens = inputs.reshape(total, width)

    small = (b_query, b_value, b_out, ln1_gain, ln1_bias, b_down, ln2_gain, ln2_bias, b_up)
    own_first = pack((w_query, w_key, w_value, w_out), small)
    first_x, first_y = swap(own_first, ALONG_X), swap(own_first, ALONG_Y)
    first_x, first_y, to_both = order.then((first_x, first_y, w_up))
    first_far, up_x = swap(first_x, ALONG_Y), swap(to_both, ALONG_X)
    first_c = [swap(part, CORE) for part in (own_first, first_x, first_y)]
    first_far, up_x, to_x, to_y, *first_c = order.then((first_far, up_x, w_down, w_up, *first_c))
    first = (own_first, first_x, first_y, first_far, *first_c, swap(first_far, CORE))
    up_y, down_x = swap(to_y, ALONG_Y), swap(to_x, ALONG_X)
    up_c = [swap(part, CORE) for part in (w_up, up_x)]
    cot_pool = lax.all_gather(cotangent, "rep", axis=0, tiled=True)
    qkv, vecs, bias_up, tokens_give = order.then(project(order.meta, tokens, first))
    mixed, raised, inverse = order.then(attend(order.meta, qkv, batches, rows))
    up_y, down_x, tokens_give, to_y, *up_c = order.then((up_y, down_x, tokens_give, w_down, *up_c))
    up_far, down_y = swap(up_y, ALONG_X), swap(to_y, ALONG_Y)
    up_c.append(swap(up_y, CORE))
    tokens_got = swap(tokens_give, CORE)
    unit_one, inverse_one, hidden_low, both_give = order.then(mix_out(order.meta, mixed, tokens, first, vecs))
    to_top = order.then(down_x[:256])
    up_far, down_y, tokens_got, both_give, to_top, *up_c = order.then((up_far, down_y, tokens_got, both_give, to_top, *up_c))
    up = (w_up, up_x, up_y, up_far, *up_c, swap(up_far, CORE))
    down_top, down_end = swap(to_top, ALONG_Y), swap(down_y[256:], ALONG_X)
    up, *to_core = order.then((up, w_down, down_x, down_y))
    down_c = [swap(part, CORE) for part in to_core]
    act, slope, act_give = order.then(feed_up(order.meta, hidden_low, up, bias_up))
    down_top, down_end, act_give, both_give, *down_c = order.then((down_top, down_end, act_give, both_give, *down_c))
    down = (w_down, down_x, down_y, down_top, down_end) + tuple(down_c)
    down += tuple(swap(part, CORE) for part in (down_top, down_end))
    *down, act_give, both_give = order.then((*down, act_give, both_give))
    act_got, both_got = swap(act_give, CORE), swap(both_give, CORE)
    out, grad_sum, sum_low, grads_two, pre, grad_bias_up = order.then(
        feed_down(order.meta, act, slope, down, unit_one, cot_pool, vecs, batches, rows)
    )
    sum_got = swap(sum_low, CORE)
    out, act_got, sum_got, pre = order.then((out, act_got, sum_got, pre))
    pre_got = swap(pre, CORE)
    out_pool = lax.all_gather(out.reshape(batches, rows, width), "rep", axis=0, tiled=True)
    far_down, own_down, rest_down = order.then(down_grad(order.meta, act, act_got, sum_low, sum_got))
    pre_got, both_got, far_down = order.then((pre_got, both_got, far_down))
    got_down = sent(far_down)
    grad_resid, resid_low, grad_mixed, grads_one = order.then(
        back_up(order.meta, pre, up, first, grad_sum, unit_one, inverse_one, vecs)
    )
    far_up, own_up, rest_up = order.then(up_grad(order.meta, hidden_low, both_got, pre, pre_got))
    got_down, far_up, resid_low = order.then((got_down, far_up, resid_low))
    got_up = sent(far_up)
    late_down = passed(order.then(turned(rest_down, got_down)))
    grads, vec = order.then(
        attend_back(
            order.meta, qkv, mixed, raised, inverse, grad_mixed, grads_one, grads_two, grad_bias_up, batches, rows
        )
    )
    grad_input = order.then(back_project(order.meta, grads, first, grad_resid))
    got_up, late_down, resid_low, grads, vec = order.then((got_up, late_down, resid_low, grads, vec))
    resid_got, grads_got, vec_got = swap(resid_low, CORE), swap(grads, CORE), swap(vec, CORE)
    kept_down, given_down, pass_up = order.then(
        merge(order.meta, own_down, got_down, late_down, rest_up, got_up)
    )
    resid_got, grads_got, vec_got, pass_up, given_down = order.then((resid_got, grads_got, vec_got, pass_up, given_down))
    late_up, taken_down = passed(pass_up), pairs(given_down, 1)
    (far_a, own_a, rest_a), (far_b, own_b, rest_b) = order.then(
        first_grad(
            order.meta, tokens, tokens_got, mixed, both_got, grads, grads_got, resid_low, resid_got, vec, vec_got
        )
    )
    late_up, taken_down, far_a, out_pool = order.then((late_up, taken_down, far_a, out_pool))
    got_a = sent(far_a)
    far_b, half_down = order.then((far_b, plus(kept_down, taken_down)))
    got_b = sent(far_b)
    over_down = pairs(half_down, 2)
    kept_up, given_up = order.then(summed(own_up, got_up, late_up))
    got_a = order.then(got_a)
    late_a = passed(order.then(turned(rest_a, got_a)))
    taken_up = pairs(given_up, 1)
    layer_out = order.then(chosen(order.meta, out_pool, 5))
    got_b = order.then(got_b)
    late_b = passed(order.then(turned(rest_b, got_b)))
    late_a = order.then(late_a)
    kept_a, given_a = order.then(summed(own_a, got_a, late_a))
    taken_a = pairs(given_a, 1)
    over_down, taken_up = order.then((over_down, taken_up))
    total_down, half_up = order.then((plus(half_down, over_down), plus(kept_up, taken_up)))
    late_b = order.then(late_b)
    kept_b, given_b = order.then(summed(own_b, got_b, late_b))
    taken_b = pairs(given_b, 1)
    taken_a = order.then(taken_a)
    half_a = order.then(plus(kept_a, taken_a))
    over_a = pairs(half_a, 2)
    over_up = pairs(half_up, 2)
    taken_b = order.then(taken_b)
    half_b = order.then(plus(kept_b, taken_b))
    over_b = pairs(half_b, 2)
    total_down = order.then(total_down)
    other_down = pairs(total_down, 1)
    over_a = order.then(over_a)
    total_a = order.then(plus(half_a, over_a))
    other_a = pairs(total_a, 1)
    over_up, other_down = order.then((over_up, other_down))
    total_up = order.then(plus(half_up, over_up))
    other_up = pairs(total_up, 1)
    g_down = order.then(jnp.concatenate(unfolded(total_down, other_down), 1))
    over_b = order.then(over_b)
    total_b = order.then(plus(half_b, over_b))
    other_b = pairs(total_b, 1)
    other_a, other_up = order.then((other_a, other_up))
    g_up = order.then(jnp.concatenate(unfolded(total_up, other_up), 1))
    g_a = order.then(jnp.concatenate(unfolded(total_a, other_a), 1))
    left, right = unfolded(total_b, other_b)
    g_b = jnp.concatenate([left[:256], right[:256]], 1)
    line = lambda i: left[256 + i, :128]
    return (
        layer_out, grad_input.reshape(batches, rows, width),
        g_a[0:128], g_a[128:256], g_b[0:128], g_b[128:256],
        line(0), line(1), line(2), line(3), line(4),
        g_up, left[264, :512], g_down, line(5), line(6), line(7),
    )


def pick(pool, targets):
    return jnp.stack(
        [lax.dynamic_index_in_dim(pool, targets[i], 0, keepdims=False) for i in range(targets.shape[0])]
    )


def local_general(
    inputs, lengths, dealing, w_query, w_key, w_value, w_out, b_query, b_value, b_out,
    ln1_gain, ln1_bias, w_up, b_up, w_down, b_down, ln2_gain, ln2_bias, cotangent,
):
    batches, rows, width = inputs.shape
    shards = lax.axis_size("shard")
    replicas = lax.axis_size("rep")
    group = batches * replicas
    shard_index = lax.axis_index("shard")
    rep_index = lax.axis_index("rep")
    anchor = shard_index * group
    slots = anchor + rep_index * batches + jnp.arange(batches, dtype=jnp.int32)
    seq_lengths = jnp.take(lengths, slots)
    local_dealing = lax.dynamic_slice_in_dim(dealing, anchor, group) - anchor
    sources = jnp.take(dealing, slots) - anchor
    places = jnp.arange(group, dtype=jnp.int32)
    wanted = jnp.sum(
        jnp.where(local_dealing[None, :] == (slots - anchor)[:, None], places[None, :], 0), 1
    )

    def gather(block):
        return lax.all_gather(block, "shard", axis=0, tiled=True)

    block = w_query.shape[0]
    wide = w_up.shape[1]
    small = (b_query, b_value, b_out, ln1_gain, ln1_bias, b_down, ln2_gain, ln2_bias, b_up)
    vec = jnp.concatenate(small)
    first = jnp.concatenate([w_query, w_key, w_value, w_out], 0)
    all_vec = lax.all_gather(vec, "shard", axis=0, tiled=True).reshape(shards, -1)
    all_first = gather(first).reshape(shards, 4, block, width)
    cuts = [0]
    for part in small:
        cuts.append(cuts[-1] + part.shape[0])
    (bias_query, bias_value, bias_out, gain_one, shift_one, bias_down, gain_two, shift_two, bias_up) = [
        all_vec[:, cuts[i] : cuts[i + 1]].reshape(-1).astype(F32) for i in range(len(small))
    ]
    full_query, full_key, full_value, full_out = [
        all_first[:, i].reshape(width, width) for i in range(4)
    ]
    full_up = gather(w_up)
    full_down = gather(w_down)
    cot = pick(lax.all_gather(cotangent, "rep", axis=0, tiled=True), wanted)

    tokens = inputs.reshape(batches * rows, width)
    query = (matmul(tokens, full_query) + bias_query).astype(BF16)
    keyed = matmul(tokens, full_key).astype(BF16)
    value = (matmul(tokens, full_value) + bias_value).astype(BF16)
    heads = lambda a: a.reshape(batches, rows, H, HD).transpose(0, 2, 1, 3)
    flat = lambda a: a.transpose(0, 2, 1, 3).reshape(batches * rows, width)
    qh, kh, vh = heads(query), heads(keyed), heads(value)
    allowed = lax.broadcasted_iota(jnp.int32, (batches, 1, 1, rows), 3) < seq_lengths[:, None, None, None]
    scale = HD ** (-0.5)
    scores = jnp.einsum("bhqd,bhkd->bhqk", qh, kh, preferred_element_type=F32) * scale
    scores = jnp.where(allowed, scores, NEG)
    raised = jnp.exp(scores - jnp.max(scores, -1, keepdims=True))
    probs = raised / jnp.sum(raised, -1, keepdims=True)
    probs_low = probs.astype(BF16)
    mixed_low = flat(jnp.einsum("bhqk,bhkd->bhqd", probs_low, vh, preferred_element_type=F32).astype(BF16))
    hidden, unit_one, inverse_one = normalize(
        tokens.astype(F32) + matmul(mixed_low, full_out) + bias_out, gain_one, shift_one
    )
    hidden_low = hidden.astype(BF16)
    pre = matmul(hidden_low, full_up) + bias_up
    act, slope = gelu_both(pre)
    act_low = act.astype(BF16)
    summed = hidden + matmul(act_low, full_down) + bias_down
    normed, unit_two, inverse_two = normalize(summed, gain_two, shift_two)
    valid = (lax.broadcasted_iota(jnp.int32, (batches, rows, 1), 1) < seq_lengths[:, None, None]).reshape(-1, 1)
    out = jnp.where(valid, normed, 0.0).astype(BF16).reshape(batches, rows, width)
    layer_out = pick(lax.all_gather(out, "rep", axis=0, tiled=True), sources)

    grad_out = jnp.where(valid, cot.reshape(-1, width).astype(F32), 0.0)
    grad_gain_two = jnp.sum(grad_out * unit_two, 0)
    grad_shift_two = jnp.sum(grad_out, 0)
    grad_sum = norm_back(grad_out, unit_two, inverse_two, gain_two)
    grad_bias_down = jnp.sum(grad_sum, 0)
    grad_sum_low = grad_sum.astype(BF16)

    def reduced(part):
        return lax.psum_scatter(part, "shard", scatter_dimension=0, tiled=True)

    def over_rep(part):
        return lax.psum(part, "rep").astype(F32)

    g_down = reduced(left_trans(act_low, grad_sum_low).astype(BF16))
    grad_pre = (right_trans(grad_sum_low, full_down) * slope).astype(BF16)
    grad_bias_up = jnp.sum(grad_pre.astype(F32), 0)
    g_up = reduced(left_trans(hidden_low, grad_pre).astype(BF16))
    grad_hidden = grad_sum + right_trans(grad_pre, full_up)
    grad_gain_one = jnp.sum(grad_hidden * unit_one, 0)
    grad_shift_one = jnp.sum(grad_hidden, 0)
    grad_resid = norm_back(grad_hidden, unit_one, inverse_one, gain_one)
    grad_bias_out = jnp.sum(grad_resid, 0)
    grad_resid_low = grad_resid.astype(BF16)
    grad_w_out = left_trans(mixed_low, grad_resid_low).astype(BF16)
    grad_mixed = heads(right_trans(grad_resid_low, full_out).astype(BF16))
    grad_probs = jnp.einsum("bhqd,bhkd->bhqk", grad_mixed, vh, preferred_element_type=F32)
    inner = jnp.sum(probs * grad_probs, -1, keepdims=True)
    grad_scores = (probs * (grad_probs - inner) * scale).astype(BF16)
    query_low = flat(jnp.einsum("bhqk,bhkd->bhqd", grad_scores, kh, preferred_element_type=F32).astype(BF16))
    key_low = flat(jnp.einsum("bhqk,bhqd->bhkd", grad_scores, qh, preferred_element_type=F32).astype(BF16))
    value_low = flat(jnp.einsum("bhqk,bhqd->bhkd", probs_low, grad_mixed, preferred_element_type=F32).astype(BF16))
    grad_bias_query = jnp.sum(query_low.astype(F32), 0)
    grad_bias_value = jnp.sum(value_low.astype(F32), 0)
    blocks = [
        part.reshape(shards, block, width)
        for part in (
            left_trans(tokens, query_low).astype(BF16),
            left_trans(tokens, key_low).astype(BF16),
            left_trans(tokens, value_low).astype(BF16),
            grad_w_out,
        )
    ]
    g_first = reduced(jnp.concatenate(blocks, 1).reshape(shards * 4 * block, width))
    grad_tokens = (
        grad_resid
        + right_trans(query_low, full_query)
        + right_trans(key_low, full_key)
        + right_trans(value_low, full_value)
    )
    grad_input = grad_tokens.astype(BF16).reshape(batches, rows, width)
    vec_terms = (
        grad_bias_query, grad_bias_value, grad_bias_out, grad_gain_one, grad_shift_one,
        grad_bias_down, grad_gain_two, grad_shift_two, grad_bias_up,
    )
    g_vec = jnp.concatenate([part.reshape(shards, -1) for part in vec_terms], 1)
    g_vec = lax.psum(g_vec, ("shard", "rep"))
    g_vec = lax.dynamic_index_in_dim(g_vec, shard_index, 0, keepdims=False)
    (g_bquery, g_bvalue, g_bout, g_gain_one, g_shift_one, g_bdown, g_gain_two, g_shift_two, g_bup) = [
        g_vec[cuts[i] : cuts[i + 1]] for i in range(len(small))
    ]
    g_down = over_rep(g_down)
    g_up = over_rep(g_up)
    g_first = over_rep(g_first).reshape(4, block, width)
    return (
        layer_out, grad_input, g_first[0], g_first[1], g_first[2], g_first[3],
        g_bquery, g_bvalue, g_bout, g_gain_one, g_shift_one,
        g_up, g_bup, g_down, g_bdown, g_gain_two, g_shift_two,
    )


def solution(mesh):
    seqs = P(("shard", "rep"), None, None)
    mat = P("shard", None)
    vec = P("shard")
    in_specs = (
        seqs, P(), P(), mat, mat, mat, mat, vec, vec, vec, vec, vec, mat, vec, mat, vec, vec, vec, seqs,
    )
    out_specs = (
        seqs, seqs, mat, mat, mat, mat, vec, vec, vec, vec, vec, mat, vec, mat, vec, vec, vec,
    )
    shape = dict(mesh.shape)
    local = local_eight if shape["shard"] == 8 and shape["rep"] == 4 else local_general
    return jax.shard_map(local, mesh=mesh, in_specs=in_specs, out_specs=out_specs, check_vma=False)
```

```python
import math

import jax
import jax.numpy as jnp
from jax import lax
from jax.experimental import pallas as pl
from jax.experimental.pallas import tpu as pltpu
from jax.sharding import PartitionSpec as P

H = 16
HD = 64
EPS = 1e-05
NEG = -1e30
F32 = jnp.float32
BF16 = jnp.bfloat16


def matmul(left, right):
    return jnp.dot(left, right, preferred_element_type=F32)


def left_trans(left, right):
    return lax.dot_general(left, right, (((0,), (0,)), ((), ())), preferred_element_type=F32)


def right_trans(left, right):
    return lax.dot_general(left, right, (((1,), (1,)), ((), ())), preferred_element_type=F32)


def normalize(values, gain, shift):
    center = values - jnp.mean(values, -1, keepdims=True)
    inverse = lax.rsqrt(jnp.mean(center * center, -1, keepdims=True) + EPS)
    unit = center * inverse
    return (unit * gain + shift, unit, inverse)


def norm_back(grad, unit, inverse, gain):
    scaled = grad * gain
    return inverse * (
        scaled
        - jnp.mean(scaled, -1, keepdims=True)
        - unit * jnp.mean(scaled * unit, -1, keepdims=True)
    )


def gelu_both(pre):
    cumul = 0.5 * (1.0 + lax.erf(pre * 0.7071067811865476))
    density = jnp.exp(-0.5 * pre * pre) * 0.3989422804014327
    return (pre * cumul, cumul + pre * density)


VMEM = 56 * 1024 * 1024
TIGHT = ()
ANY = pl.BlockSpec(memory_space=pl.ANY)
DMA = pltpu.SemaphoreType.DMA


def spec(shape, index):
    return pl.BlockSpec(shape, index)


def whole(shape):
    zeros = (0,) * len(shape)
    return pl.BlockSpec(shape, lambda *_: zeros)


def sds(shape, dtype):
    return jax.ShapeDtypeStruct(shape, dtype)


def room(specs, shapes, scratch):
    total = 8 * 1024 * 1024
    for block, shape in zip(specs, shapes):
        if block.block_shape is not None:
            total += 2 * math.prod(block.block_shape) * shape.dtype.itemsize
    for item in scratch:
        if item.memory_space == pltpu.VMEM:
            total += math.prod(item.shape) * jnp.dtype(item.dtype).itemsize
    return total


def call(kernel, grid, in_specs, out_specs, out_shape, scratch):
    def run(*args):
        outs = out_shape if isinstance(out_shape, (list, tuple)) else [out_shape]
        specs = out_specs if isinstance(out_specs, (list, tuple)) else [out_specs]
        limit = VMEM
        if kernel.__qualname__.split(".")[0] in TIGHT:
            limit = room(list(in_specs) + list(specs), list(args[1:]) + list(outs), scratch)
        return pl.pallas_call(
            kernel,
            grid_spec=pltpu.PrefetchScalarGridSpec(
                num_scalar_prefetch=1,
                grid=grid,
                in_specs=in_specs,
                out_specs=out_specs,
                scratch_shapes=list(scratch),
            ),
            out_shape=out_shape,
            compiler_params=pltpu.CompilerParams(vmem_limit_bytes=limit),
            cost_estimate=pl.CostEstimate(flops=1024, bytes_accessed=1024, transcendentals=0),
        )(*args)

    return run


def dot_nn(a, b):
    return lax.dot_general(a, b, (((1,), (0,)), ((), ())), preferred_element_type=F32)


def dot_nt(a, b):
    return lax.dot_general(a, b, (((1,), (1,)), ((), ())), preferred_element_type=F32)


def dot_tn(a, b):
    return lax.dot_general(a, b, (((0,), (0,)), ((), ())), preferred_element_type=F32)


def fetch(meta, parts, target, sems, low, high, columns=None):
    cut = parts[3].shape[0]
    each = len(parts) // 2
    for core in range(2):
        for chip in range(4):
            at = meta[0] ^ (2 * chip + core)
            if chip < 3:
                pieces = [(parts[each * core + chip], low, high, 0)]
            else:
                pieces = []
                if low < cut:
                    pieces.append((parts[each * core + 3], low, min(high, cut), 0))
                if high > cut:
                    start = max(low, cut)
                    pieces.append((parts[each * core + 4], start - cut, high - cut, start - low))
            for ref, begin, end, offset in pieces:
                source = ref.at[pl.ds(begin, end - begin)]
                if columns is not None:
                    source = ref.at[pl.ds(begin, end - begin), columns]
                goal = target.at[at]
                if len(pieces) > 1:
                    goal = target.at[at, pl.ds(offset, end - begin)]
                pltpu.make_async_copy(source, goal, sems.at[at]).start()


def arrived(target, sem):
    pltpu.make_async_copy(target, target, sem).wait()


def hand_over(meta, source, target, sems, block):
    copies = []
    for chip in range(4):
        at = pl.ds(pl.multiple_of((meta[0] ^ (2 * chip + 1)) * block, block), block)
        copies.append(pltpu.make_async_copy(source.at[:, at], target.at[chip], sems.at[chip]))
        copies[-1].start()
    return copies


def project(meta, tokens, first):
    rows, width = tokens.shape
    tile = 512
    count = width // tile

    def kernel(meta, x_ref, *refs):
        parts, (out_ref, vec_ref, up_ref, give_ref, held, short, made, sems, short_sems, out_sems, give_sems) = refs[: len(first)], refs[len(first) :]
        for w in range(3):
            fetch(meta, parts, held.at[w], sems.at[w], 128 * w, 128 * (w + 1))
            if w == 0:
                fetch(meta, parts, short, short_sems, 512, 528)
        gifts = hand_over(meta, x_ref, give_ref, give_sems, 128)
        for b in range(8):
            arrived(short.at[b], short_sems.at[b])
        for b in range(8):
            two = short[b].astype(F32)
            for v in range(8):
                vec_ref[v : v + 1, 128 * b : 128 * (b + 1)] = two[0:1, 128 * v : 128 * (v + 1)]
            up_ref[0:1, 512 * b : 512 * (b + 1)] = two[1:2, :512]

        def body(i, carry):
            w, n = i // count, i % count

            @pl.when(n == 0)
            def _():
                for b in range(8):
                    arrived(held.at[w, b], sems.at[w, b])

            at = pl.ds(pl.multiple_of(n * tile, tile), tile)
            weight = held[w, :, :, at].reshape(width, tile)
            bias = jnp.where(w == 0, vec_ref[0:1, at], vec_ref[1:2, at])
            bias = jnp.where(w == 1, jnp.zeros_like(bias), bias)
            made[w, :, at] = (dot_nn(x_ref[...], weight) + bias).astype(BF16)

            @pl.when(n == count - 1)
            def _():
                pltpu.make_async_copy(made.at[w], out_ref.at[w], out_sems.at[w]).start()

            return carry

        lax.fori_loop(0, 3 * count, body, 0)
        for w in range(3):
            pltpu.make_async_copy(made.at[w], out_ref.at[w], out_sems.at[w]).wait()
        for copy in gifts:
            copy.wait()

    return call(
        kernel,
        (1,),
        [whole((rows, width))] + [ANY] * len(first),
        [ANY, whole((8, width)), whole((1, 4 * width)), ANY],
        [sds((3, rows, width), BF16), sds((8, width), F32), sds((1, 4 * width), F32), sds((4, rows, 128), BF16)],
        [
            pltpu.VMEM((3, 8, 128, width), BF16), pltpu.VMEM((8, 16, width), BF16),
            pltpu.VMEM((3, rows, width), BF16), DMA((3, 8)), DMA((8,)), DMA((3,)), DMA((4,)),
        ],
    )(meta, tokens, *first)


HEADS = 4


def attend(meta, qkv, batches, rows):
    total, width = qkv.shape[1:]
    span = HEADS * HD
    steps = width // span

    def kernel(meta, q_ref, k_ref, v_ref, mixed_ref, raised_ref, inverse_ref):
        length = meta[1 + pl.program_id(0)]
        allowed = lax.broadcasted_iota(jnp.int32, (1, rows), 1) < length
        shift = jnp.where(allowed, 0.0, NEG)
        left = lax.broadcasted_iota(jnp.int32, (rows, 128), 1) < HD
        one = jnp.ones((rows, 128), BF16)
        for pair in range(HEADS // 2):
            cols = slice(128 * pair, 128 * (pair + 1))
            query, keyed, value = q_ref[0, :, cols] * jnp.asarray(HD**-0.5, BF16), k_ref[0, :, cols], v_ref[0, :, cols]
            outs = []
            for half in range(2):
                mine = left if half == 0 else jnp.logical_not(left)
                scores = dot_nt(jnp.where(mine, query, jnp.zeros_like(query)), keyed) + shift
                raised = jnp.exp(scores - jnp.max(scores, -1, keepdims=True)).astype(BF16)
                raised_ref[0, 2 * pair + half] = raised
                outs.append(dot_nn(raised, jnp.where(mine, value, one)))
            inverse = 1.0 / pltpu.roll(jnp.where(left, outs[1], outs[0]), HD, 1)
            inverse_ref[:, cols] = inverse
            mixed_ref[:, cols] = (jnp.where(left, outs[0], outs[1]) * inverse).astype(BF16)

    part = lambda w: spec((1, rows, span), lambda b, h, meta: (w, b, h))
    here = spec((rows, span), lambda b, h, meta: (b, h))
    return call(
        kernel,
        (batches, steps),
        [part(0), part(1), part(2)],
        [here, spec((1, HEADS, rows, rows), lambda b, h, meta: (b, h, 0, 0)), here],
        [sds((total, width), BF16), sds((batches, H, rows, rows), BF16), sds((total, width), F32)],
        [],
    )(meta, qkv, qkv, qkv)


def mix_out(meta, mixed, tokens, first, vecs):
    total, width = mixed.shape
    tile = 128

    def kernel(meta, mixed_ref, tokens_ref, vec_ref, *refs):
        parts, (unit_ref, inv_ref, low_ref, give_ref, held, sems, give_sems) = refs[: len(first)], refs[len(first) :]
        fetch(meta, parts, held, sems, 384, 512)
        gifts = hand_over(meta, mixed_ref, give_ref.at[0], give_sems.at[0], 128)
        for b in range(8):
            arrived(held.at[b], sems.at[b])

        def body(i, carry):
            here = pl.ds(pl.multiple_of(i * tile, tile), tile)
            branch = dot_nn(mixed_ref[here], held[...].reshape(width, width)) + vec_ref[2:3]
            hidden, unit, inverse = normalize(tokens_ref[here].astype(F32) + branch, vec_ref[3:4], vec_ref[4:5])
            unit_ref[here] = unit
            inv_ref[here] = jnp.broadcast_to(inverse, (tile, 128))
            low_ref[here] = hidden.astype(BF16)
            return carry

        lax.fori_loop(0, total // tile, body, 0)
        gifts += hand_over(meta, low_ref, give_ref.at[1], give_sems.at[1], 128)
        for copy in gifts:
            copy.wait()

    block = (total, width)
    return call(
        kernel,
        (1,),
        [whole(block), whole(block), whole(vecs.shape)] + [ANY] * len(first),
        [whole(block), whole((total, 128)), whole(block), ANY],
        [sds(block, F32), sds((total, 128), F32), sds(block, BF16), sds((2, 4, total, 128), BF16)],
        [pltpu.VMEM((8, 128, width), BF16), DMA((8,)), DMA((2, 4))],
    )(meta, mixed, tokens, vecs, *first)


def feed_up(meta, low, up, bias):
    total, width = low.shape
    wide = up[0].shape[1]
    strip, tile = 512, 512
    strips, inner = wide // strip, strip // tile

    def kernel(meta, x_ref, bias_ref, *refs):
        parts, (act_ref, slope_ref, give_ref, held, act, slope, sems, out_sems, give_sems) = refs[: len(up)], refs[len(up) :]
        for t in range(strips):
            fetch(meta, parts, held.at[t], sems.at[t], 0, 128, pl.ds(strip * t, strip))

        def leave(i):
            at = pl.ds(pl.multiple_of(i * tile, tile), tile)
            return (
                pltpu.make_async_copy(act.at[i], act_ref.at[:, at], out_sems.at[0, i]),
                pltpu.make_async_copy(slope.at[i], slope_ref.at[:, at], out_sems.at[1, i]),
            )

        def body(i, carry):
            t, n = i // inner, i % inner

            @pl.when(n == 0)
            def _():
                for b in range(8):
                    arrived(held.at[t, b], sems.at[t, b])

            weight = held[t, :, :, pl.ds(pl.multiple_of(n * tile, tile), tile)].reshape(width, tile)
            pre = dot_nn(x_ref[...], weight) + bias_ref[:, pl.ds(pl.multiple_of(i * tile, tile), tile)]
            value, grad = gelu_both(pre)
            act[i] = value.astype(BF16)
            slope[i] = grad.astype(BF16)
            for copy in leave(i):
                copy.start()
            code = meta[0] ^ i

            @pl.when(code % 2 == 1)
            def _():
                pltpu.make_async_copy(act.at[i], give_ref.at[code // 2], give_sems.at[code // 2]).start()

            return carry

        lax.fori_loop(0, strips * inner, body, 0)
        for i in range(strips * inner):
            for copy in leave(i):
                copy.wait()
        for chip in range(4):
            arrived(give_ref.at[chip], give_sems.at[chip])

    out = sds((total, wide), BF16)
    tiles = wide // tile
    return call(
        kernel,
        (1,),
        [whole((total, width)), whole((1, wide))] + [ANY] * len(up),
        [ANY, ANY, ANY],
        [out, out, sds((4, total, tile), BF16)],
        [
            pltpu.VMEM((strips, 8, 128, strip), BF16), pltpu.VMEM((tiles, total, tile), BF16),
            pltpu.VMEM((tiles, total, tile), BF16), DMA((strips, 8)), DMA((2, tiles)), DMA((4,)),
        ],
    )(meta, low, bias, *up)


def feed_down(meta, act, slope, down, unit_one, cot_pool, vecs, batches, rows):
    total, wide = act.shape
    width = down[0].shape[1]
    chunk = 128

    def kernel(meta, act_ref, slope_ref, unit_ref, cot_ref, vec_ref, *refs):
        parts = refs[: len(down)]
        (
            out_ref, sum_ref, low_ref, grad_ref, pre_ref, bias_ref, out, grad_sums, low, early,
            held, left, right, total_ref, unit, cot, sems, left_sems, right_sems, out_sems, more,
        ) = refs[len(down) :]
        for b in range(8):
            pltpu.make_async_copy(act_ref.at[:, pl.ds(512 * b, 512)], left.at[b], left_sems.at[b]).start()
        fetch(meta, parts, held, sems, 0, 512)
        rest = [pltpu.make_async_copy(unit_ref, unit, more.at[0])] + [
            pltpu.make_async_copy(cot_ref.at[meta[3 + i]], cot.at[i], more.at[1 + i]) for i in range(batches)
        ]

        def add(b, carry):
            arrived(left.at[b], left_sems.at[b])
            arrived(held.at[b], sems.at[b])

            @pl.when(b == 4)
            def _():
                for copy in rest:
                    copy.start()
                for c in range(8):
                    at = pl.ds(512 * c, 512)
                    pltpu.make_async_copy(slope_ref.at[:, at], right.at[c], right_sems.at[c]).start()

            part = dot_nn(left[b], held[b])

            @pl.when(b == 0)
            def _():
                total_ref[...] = part

            @pl.when(b > 0)
            def _():
                total_ref[...] += part

            return carry

        lax.fori_loop(0, 8, add, 0)
        for copy in rest:
            copy.wait()
        grad_ref[...] = jnp.zeros_like(grad_ref)

        def body(i, carry):
            here = pl.ds(pl.multiple_of(i * chunk, chunk), chunk)
            batch = i // (rows // chunk)
            at = pl.multiple_of((i % (rows // chunk)) * chunk, chunk)
            summed = (unit[here] * vec_ref[3:4] + vec_ref[4:5]) + total_ref[here] + vec_ref[5:6]
            normed, unit_two, inverse = normalize(summed, vec_ref[6:7], vec_ref[7:8])
            place = at + lax.broadcasted_iota(jnp.int32, (chunk, 1), 0)
            valid = place < meta[1 + batch]
            out[here] = jnp.where(valid, normed, 0.0).astype(BF16)
            grad_out = jnp.where(valid, cot[batch, pl.ds(at, chunk)].astype(F32), 0.0)
            grad_sum = norm_back(grad_out, unit_two, inverse, vec_ref[6:7])
            grad_sums[here] = grad_sum
            low[here] = grad_sum.astype(BF16)
            grad_ref[0:1] += jnp.sum(grad_out * unit_two, 0, keepdims=True)
            grad_ref[1:2] += jnp.sum(grad_out, 0, keepdims=True)
            grad_ref[2:3] += jnp.sum(grad_sum, 0, keepdims=True)
            return carry

        lax.fori_loop(0, total // chunk, body, 0)
        leaving = [
            pltpu.make_async_copy(source, target, early.at[i])
            for i, (source, target) in enumerate(((low, low_ref), (out, out_ref), (grad_sums, sum_ref)))
        ]
        for copy in leaving:
            copy.start()

        def leave(b):
            at = pl.ds(pl.multiple_of(512 * b, 512), 512)
            return pltpu.make_async_copy(left.at[b], pre_ref.at[:, at], out_sems.at[b])

        def through(b, carry):
            arrived(right.at[b], right_sems.at[b])
            grad = (dot_nt(low[...], held[b]) * right[b].astype(F32)).astype(BF16)
            left[b] = grad
            leave(b).start()
            bias_ref[:, pl.ds(pl.multiple_of(512 * b, 512), 512)] = jnp.sum(grad.astype(F32), 0, keepdims=True)
            return carry

        lax.fori_loop(0, 8, through, 0)
        for b in range(8):
            leave(b).wait()
        for copy in leaving:
            copy.wait()

    block = (total, width)
    return call(
        kernel,
        (1,),
        [ANY, ANY, ANY, ANY, whole(vecs.shape)] + [ANY] * len(down),
        [ANY, ANY, ANY, whole((8, width)), ANY, whole((1, wide))],
        [
            sds(block, BF16), sds(block, F32), sds(block, BF16), sds((8, width), F32),
            sds((total, wide), BF16), sds((1, wide), F32),
        ],
        [
            pltpu.VMEM(block, BF16), pltpu.VMEM(block, F32), pltpu.VMEM(block, BF16), DMA((3,)),
            pltpu.VMEM((8, 512, width), BF16), pltpu.VMEM((8, total, 512), BF16), pltpu.VMEM((8, total, 512), BF16),
            pltpu.VMEM(block, F32), pltpu.VMEM(block, F32), pltpu.VMEM((batches, rows, width), BF16),
            DMA((8,)), DMA((8,)), DMA((8,)), DMA((8,)), DMA((1 + batches,)),
        ],
    )(meta, act, slope, unit_one, cot_pool, vecs, *down)


def back_up(meta, pre, up, first, grad_sum, unit_one, inverse_one, vecs):
    total, wide = pre.shape
    width = grad_sum.shape[1]
    chunk, strip = 128, 1024
    strips = wide // strip

    def kernel(meta, pre_ref, sum_ref, unit_ref, inv_ref, vec_ref, *refs):
        parts, others = refs[: len(up)], refs[len(up) : len(up) + len(first)]
        (
            resid_ref, low_ref, mixed_ref, grad_ref,
            held, pres, out_held, hidden, unit, low, mixed, sems, pre_sems, out_sems, more, leave_sems,
        ) = refs[len(up) + len(first) :]
        for t in range(strips):
            at = pl.ds(strip * t, strip)
            pltpu.make_async_copy(pre_ref.at[:, at], pres.at[t], pre_sems.at[t]).start()
            fetch(meta, parts, held.at[t], sems.at[t], 0, 128, at)
            if t == 0:
                incoming = pltpu.make_async_copy(sum_ref, hidden, more.at[0])
                incoming.start()
        other = pltpu.make_async_copy(unit_ref, unit, more.at[1])
        other.start()
        fetch(meta, others, out_held, out_sems, 384, 512)
        incoming.wait()

        def through(t, carry):
            arrived(pres.at[t], pre_sems.at[t])
            for b in range(8):
                arrived(held.at[t, b], sems.at[t, b])
            hidden[...] += dot_nt(pres[t], held[t].reshape(width, strip))
            return carry

        lax.fori_loop(0, strips, through, 0)
        other.wait()
        grad_ref[...] = jnp.zeros_like(grad_ref)

        def body(i, carry):
            here = pl.ds(pl.multiple_of(i * chunk, chunk), chunk)
            grad, unit_here = hidden[here], unit[here]
            grad_ref[0:1] += jnp.sum(grad * unit_here, 0, keepdims=True)
            grad_ref[1:2] += jnp.sum(grad, 0, keepdims=True)
            resid = norm_back(grad, unit_here, inv_ref[here, 0:1], vec_ref[3:4])
            grad_ref[2:3] += jnp.sum(resid, 0, keepdims=True)
            hidden[here] = resid
            low[here] = resid.astype(BF16)
            return carry

        lax.fori_loop(0, total // chunk, body, 0)
        leaving = [
            pltpu.make_async_copy(low, low_ref, leave_sems.at[0]), pltpu.make_async_copy(hidden, resid_ref, leave_sems.at[1])
        ]
        for copy in leaving:
            copy.start()
        for b in range(8):
            arrived(out_held.at[b], out_sems.at[b])

        def leave(j):
            at = pl.ds(pl.multiple_of(512 * j, 512), 512)
            return pltpu.make_async_copy(mixed.at[:, at], mixed_ref.at[:, at], leave_sems.at[2 + j])

        def out(j, carry):
            weight = out_held[pl.ds(4 * j, 4)].reshape(512, width)
            mixed[:, pl.ds(pl.multiple_of(512 * j, 512), 512)] = dot_nt(low[...], weight).astype(BF16)
            leave(j).start()
            return carry

        lax.fori_loop(0, 2, out, 0)
        for copy in leaving + [leave(0), leave(1)]:
            copy.wait()

    block = (total, width)
    return call(
        kernel,
        (1,),
        [ANY, ANY, ANY, whole((total, 128)), whole(vecs.shape)] + [ANY] * (len(up) + len(first)),
        [ANY, ANY, ANY, whole((8, width))],
        [sds(block, F32), sds(block, BF16), sds(block, BF16), sds((8, width), F32)],
        [
            pltpu.VMEM((strips, 8, 128, strip), BF16), pltpu.VMEM((strips, total, strip), BF16),
            pltpu.VMEM((8, 128, width), BF16), pltpu.VMEM(block, F32), pltpu.VMEM(block, F32), pltpu.VMEM(block, BF16),
            pltpu.VMEM(block, BF16), DMA((strips, 8)), DMA((strips,)), DMA((8,)), DMA((2,)), DMA((4,)),
        ],
    )(meta, pre, grad_sum, unit_one, inverse_one, vecs, *up, *first)


def attend_back(meta, qkv, mixed, raised, inverse, grad_mixed, grads_one, grads_two, bias_up, batches, rows):
    total, width = grad_mixed.shape
    span = HEADS * HD
    steps = width // span

    def kernel(meta, q_ref, k_ref, v_ref, mixed_ref, g_ref, raised_ref, inv_ref, one_ref, two_ref, up_ref, out_ref, vec_ref, sums):
        batch, step = pl.program_id(0), pl.program_id(1)
        left = lax.broadcasted_iota(jnp.int32, (rows, 128), 1) < HD
        none = jnp.zeros((rows, 128), BF16)

        @pl.when((batch == 0) & (step == 0))
        def _():
            sums[...] = jnp.zeros_like(sums)

        for pair in range(HEADS // 2):
            cols = slice(128 * pair, 128 * (pair + 1))
            query, keyed, value = q_ref[0, :, cols] * jnp.asarray(HD**-0.5, BF16), k_ref[0, :, cols], v_ref[0, :, cols]
            grad = g_ref[:, cols].astype(F32) * inv_ref[:, cols]
            both = grad * mixed_ref[:, cols].astype(F32)
            grad = grad.astype(BF16)
            got = ([], [], [])
            for half in range(2):
                mine = left if half == 0 else jnp.logical_not(left)
                low = raised_ref[0, 2 * pair + half]
                inner = jnp.sum(jnp.where(mine, both, 0.0), -1, keepdims=True)
                slope = dot_nt(jnp.where(mine, grad, none), value) - inner
                scores = (low.astype(F32) * slope).astype(BF16)
                got[0].append(dot_nn(scores, keyed))
                got[1].append(dot_tn(scores, query))
                got[2].append(dot_tn(low, grad))
            for i in range(3):
                part = jnp.where(left, got[i][0], got[i][1])
                if i == 0:
                    part = part * (HD**-0.5)
                part = part.astype(BF16)
                out_ref[i, :, cols] = part
                if i != 1:
                    at = pl.ds(pl.multiple_of(step * span, span) + 128 * pair, 128)
                    sums[i : i + 1, at] += jnp.sum(part.astype(F32), 0, keepdims=True)

        @pl.when((batch == batches - 1) & (step == steps - 1))
        def _():
            vec_ref[...] = jnp.zeros_like(vec_ref)
            rows_of = (
                sums[0:1], sums[2:3], one_ref[2:3], one_ref[0:1], one_ref[1:2], two_ref[2:3], two_ref[0:1], two_ref[1:2]
            )
            table = jnp.concatenate(rows_of, 0).astype(BF16)
            for b in range(8):
                vec_ref[b, 0:8, 0:128] = table[:, 128 * b : 128 * (b + 1)]
                vec_ref[b, 8:9, 0:512] = up_ref[:, 512 * b : 512 * (b + 1)].astype(BF16)

    part = lambda w: spec((1, rows, span), lambda b, h, meta: (w, b, h))
    here = spec((rows, span), lambda b, h, meta: (b, h))
    return call(
        kernel,
        (batches, steps),
        [
            part(0), part(1), part(2), here, here, spec((1, HEADS, rows, rows), lambda b, h, meta: (b, h, 0, 0)), here,
            whole((8, width)), whole((8, width)), whole((1, 4 * width)),
        ],
        [spec((3, rows, span), lambda b, h, meta: (0, b, h)), whole((8, 16, width))],
        [sds((3, total, width), BF16), sds((8, 16, width), BF16)],
        [pltpu.VMEM((8, width), F32)],
    )(meta, qkv, qkv, qkv, mixed, grad_mixed, raised, inverse, grads_one, grads_two, bias_up)


def back_project(meta, grads, first, grad_resid):
    total, width = grad_resid.shape

    def kernel(meta, g_ref, resid_ref, *refs):
        parts, (out_ref, held, resid, made, sems, more, out_sems) = refs[: len(first)], refs[len(first) :]
        fetch(meta, parts, held, sems, 0, 384)
        incoming = pltpu.make_async_copy(resid_ref, resid, more)
        incoming.start()
        incoming.wait()

        def leave(j):
            at = pl.ds(pl.multiple_of(256 * j, 256), 256)
            return pltpu.make_async_copy(made.at[:, at], out_ref.at[:, at], out_sems.at[j])

        def body(j, carry):
            for b in range(2):
                arrived(held.at[2 * j + b], sems.at[2 * j + b])
            at = pl.ds(pl.multiple_of(256 * j, 256), 256)
            part = resid[:, at]
            for w in range(3):
                weight = held[pl.ds(2 * j, 2), 128 * w : 128 * (w + 1)].reshape(256, width)
                part = part + dot_nt(g_ref[w], weight)
            made[:, at] = part.astype(BF16)
            leave(j).start()
            return carry

        lax.fori_loop(0, 4, body, 0)
        for j in range(4):
            leave(j).wait()

    block = (total, width)
    return call(
        kernel,
        (1,),
        [whole((3, total, width)), ANY] + [ANY] * len(first),
        ANY,
        sds(block, BF16),
        [
            pltpu.VMEM((8, 384, width), BF16), pltpu.VMEM(block, F32), pltpu.VMEM(block, BF16), DMA((8,)), DMA(()),
            DMA((4,)),
        ],
    )(meta, grads, grad_resid, *first)


def ship(made, outs, sems, half, i):
    def copy(target):
        return pltpu.make_async_copy(made.at[half, i], target, sems.at[half, i])

    if isinstance(i, int):
        copy(outs[half].at[i] if i < 2 else outs[2 * i - 2 + half]).start()
        return

    @pl.when(i < 2)
    def _():
        copy(outs[half].at[jnp.minimum(i, 1)]).start()

    @pl.when(i == 2)
    def _():
        copy(outs[2 + half]).start()

    @pl.when(i == 3)
    def _():
        copy(outs[4 + half]).start()


def shipped(made, sems):
    for half in range(2):
        for i in range(4):
            arrived(made.at[half, i], sems.at[half, i])


def chip_of(half, i):
    return (i + 2) % 4 if half == 0 else (2 * i + 1) % 5


def six(rows, cols):
    return [sds((2, rows, cols), BF16)] * 2 + [sds((rows, cols), BF16)] * 4


def load_lefts(meta, own_ref, got_ref, lefts, sems, block, total):
    for chip in (2, 3, 1, 0):
        at = pl.ds(pl.multiple_of((meta[0] ^ (2 * chip)) * block, block), block)
        pltpu.make_async_copy(own_ref.at[:, at], lefts.at[chip, pl.ds(0, total)], sems.at[chip]).start()
        pltpu.make_async_copy(got_ref.at[chip], lefts.at[chip, pl.ds(total, total)], sems.at[chip]).start()


def load_right(own, got, target, sem, total):
    pltpu.make_async_copy(own, target.at[pl.ds(0, total)], sem).start()
    pltpu.make_async_copy(got, target.at[pl.ds(total, total)], sem).start()


def down_grad(meta, act, act_got, low, low_got):
    total, width = low.shape
    block, share = 512, width // 2

    def kernel(meta, left_ref, left_got, right_ref, right_got, *refs):
        outs, (lefts, rights, made, left_sems, right_sems, out_sems) = refs[:6], refs[6:]
        for half in range(2):
            at = pl.ds(share * half, share)
            load_right(right_ref.at[:, at], right_got.at[:, at], rights.at[half], right_sems.at[half], total)
            if half == 0:
                load_lefts(meta, left_ref, left_got, lefts, left_sems, block, total)
        for half in range(2):
            arrived(rights.at[half], right_sems.at[half])

            def body(i, carry):
                chip = chip_of(half, i)
                if half == 0:
                    arrived(lefts.at[chip], left_sems.at[chip])
                made[half, i] = dot_tn(lefts[chip], rights[half]).astype(BF16)
                ship(made, outs, out_sems, half, i)
                return carry

            lax.fori_loop(0, 4, body, 0)
        shipped(made, out_sems)

    outs = call(
        kernel,
        (1,),
        [ANY] * 4,
        [ANY] * 6,
        six(block, share),
        [
            pltpu.VMEM((4, 2 * total, block), BF16), pltpu.VMEM((2, 2 * total, share), BF16),
            pltpu.VMEM((2, 4, block, share), BF16), DMA((4,)), DMA((2,)), DMA((2, 4)),
        ],
    )(meta, act, act_got, low, low_got)
    return outs[:2], outs[2:4], outs[4:]


def load_columns(meta, own_ref, got_ref, target, sem, total):
    for chip in range(4):
        at = pl.ds(pl.multiple_of((meta[0] ^ (2 * chip)) * 128, 128), 128)
        cols = pl.ds(128 * chip, 128)
        pltpu.make_async_copy(own_ref.at[:, at], target.at[pl.ds(0, total), cols], sem).start()
        pltpu.make_async_copy(got_ref.at[chip], target.at[pl.ds(total, total), cols], sem).start()


ORDER = ((2, 3, 0, 1), (1, 3, 0, 2))


def up_grad(meta, hidden, hidden_got, pre, pre_got):
    total, width = hidden.shape
    wide = pre.shape[1]
    tile = 1024
    tiles = wide // tile // 2

    def kernel(meta, x_ref, x_got, pre_ref, pre_got, *refs):
        outs, (lefts, rights, made, left_sem, right_sems, out_sems) = refs[:6], refs[6:]
        for t in range(2 * tiles):
            at = pl.ds(tile * t, tile)
            load_right(pre_ref.at[:, at], pre_got.at[:, at], rights.at[t], right_sems.at[t], total)
            if t == 0:
                load_columns(meta, x_ref, x_got.at[1], lefts, left_sem, total)
        arrived(lefts, left_sem)
        for half in range(2):

            def body(t, carry):
                arrived(rights.at[half * tiles + t], right_sems.at[half * tiles + t])
                part = dot_tn(lefts[...], rights[half * tiles + t]).astype(BF16)
                at = pl.ds(pl.multiple_of(t * tile, tile), tile)
                for i, chip in enumerate(ORDER[half]):
                    made[half, i, :, at] = part[128 * chip : 128 * (chip + 1)]
                return carry

            lax.fori_loop(0, tiles, body, 0)
            for i in range(4):
                ship(made, outs, out_sems, half, i)
        shipped(made, out_sems)

    outs = call(
        kernel,
        (1,),
        [ANY] * 4,
        [ANY] * 6,
        six(128, wide // 2),
        [
            pltpu.VMEM((2 * total, 512), BF16), pltpu.VMEM((2 * tiles, 2 * total, tile), BF16),
            pltpu.VMEM((2, 4, 128, wide // 2), BF16), DMA(()), DMA((2 * tiles,)), DMA((2, 4)),
        ],
    )(meta, hidden, hidden_got, pre, pre_got)
    return outs[:2], outs[2:4], outs[4:]


def first_grad(meta, tokens, tokens_got, mixed, mixed_got, grads, grads_got, low, low_got, vec, vec_got):
    total, width = tokens.shape
    share = width // 2

    def kernel(meta, x_ref, x_got, m_ref, m_got, g_ref, g_got, low_ref, low_got, vec_ref, vec_got, *refs):
        outs = refs[:6], refs[6:12]
        lefts, rights, made_a, made_b, short, left_sems, right_sems, sems_a, sems_b, short_sems = refs[12:]
        for w in range(4):
            own, got = (g_ref.at[w], g_got.at[w]) if w < 3 else (low_ref, low_got)
            load_right(own, got, rights.at[w], right_sems.at[w], total)
            if w == 0:
                load_columns(meta, x_ref, x_got, lefts.at[0], left_sems.at[0], total)
                for chip in range(4):
                    at = meta[0] ^ (2 * chip)
                    pltpu.make_async_copy(vec_ref.at[at], short.at[chip, 0], short_sems.at[chip]).start()
                    pltpu.make_async_copy(vec_got.at[at], short.at[chip, 1], short_sems.at[chip]).start()
            if w == 2:
                load_columns(meta, m_ref, m_got.at[0], lefts.at[1], left_sems.at[1], total)
        arrived(lefts.at[0], left_sems.at[0])
        for group, (made, sems) in enumerate(((made_a, sems_a), (made_b, sems_b))):

            def body(k, carry):
                arrived(rights.at[2 * group + k], right_sems.at[2 * group + k])
                if group == 1:

                    @pl.when(k == 1)
                    def _():
                        arrived(lefts.at[1], left_sems.at[1])

                part = dot_tn(lefts[k * group], rights[2 * group + k]).astype(BF16)
                rows = pl.ds(pl.multiple_of(128 * k, 128), 128)
                for half in range(2):
                    for i, chip in enumerate(ORDER[half]):
                        made[half, i, rows] = part[128 * chip : 128 * (chip + 1), share * half : share * (half + 1)]
                return carry

            lax.fori_loop(0, 2, body, 0)
            if group == 1:
                for i, chip in enumerate(ORDER[0]):
                    arrived(short.at[chip], short_sems.at[chip])
                    both = short[chip, 0].astype(F32) + short[chip, 1].astype(F32)
                    made[0, i, 256:] = both[:, :share].astype(BF16)
                    made[1, i, 256:] = jnp.zeros((16, share), BF16)
            for half in range(2):
                for i in range(4):
                    ship(made, outs[group], sems, half, i)
        shipped(made_a, sems_a)
        shipped(made_b, sems_b)

    outs = call(
        kernel,
        (1,),
        [ANY] * 10,
        [ANY] * 12,
        six(256, share) + six(272, share),
        [
            pltpu.VMEM((2, 2 * total, 512), BF16), pltpu.VMEM((4, 2 * total, width), BF16),
            pltpu.VMEM((2, 4, 256, share), BF16), pltpu.VMEM((2, 4, 272, share), BF16),
            pltpu.VMEM((4, 2, 16, width), BF16), DMA((2,)), DMA((4,)), DMA((2, 4)), DMA((2, 4)), DMA((4,)),
        ],
    )(meta, tokens, tokens_got, mixed, mixed_got, grads, grads_got, low, low_got, vec, vec_got)
    return [(some[:2], some[2:4], some[4:]) for some in (outs[:6], outs[6:])]


def pack(weights, small):
    block, width = weights[0].shape
    high = block * len(weights) + 16

    def kernel(*refs):
        out_ref = refs[-1]
        for i in range(len(weights)):
            out_ref[block * i : block * (i + 1)] = refs[i][...]
        out_ref[block * len(weights) :] = jnp.zeros((16, width), BF16)
        start = 0
        for ref in refs[len(weights) : -1]:
            count = ref.shape[1]
            row, column = block * len(weights) + start // width, start % width
            out_ref[row : row + 1, column : column + count] = ref[...]
            start += count

    return pl.pallas_call(
        kernel,
        out_shape=jax.ShapeDtypeStruct((high, width), BF16),
        compiler_params=pltpu.CompilerParams(vmem_limit_bytes=VMEM),
        cost_estimate=pl.CostEstimate(flops=1024, bytes_accessed=1024, transcendentals=0),
    )(*weights, *[part.reshape(1, -1) for part in small])


def chosen(meta, pool, first):
    rows, width = pool.shape[1:]

    def kernel(meta, pool_ref, out_ref):
        out_ref[...] = pool_ref[...]

    return call(
        kernel,
        (2,),
        [spec((1, rows, width), lambda i, meta: (meta[first + i], 0, 0))],
        spec((1, rows, width), lambda i, meta: (i, 0, 0)),
        sds((2, rows, width), BF16),
        [],
    )(meta, pool)


CORE, ALONG_X, ALONG_Y = 1, 2, 4


def swap(value, mask):
    return lax.ppermute(value, "shard", [(i, i ^ mask) for i in range(8)])


def plus(*parts):
    total = parts[0].astype(F32)
    for part in parts[1:]:
        total = total + part.astype(F32)
    return total.astype(BF16)


class Order:
    def __init__(self, meta):
        self.meta = meta

    def place(self, *values):
        *values, self.meta = lax.optimization_barrier(values + (self.meta,))
        return values

    def then(self, value):
        self.meta, value = lax.optimization_barrier((self.meta, value))
        return value

    def run(self, function, *values):
        return self.then(function(*self.place(*values)))


def tie(*values):
    return lax.optimization_barrier(values)


def both_cores(*mine):
    return mine + tuple(swap(part, CORE) for part in mine)


def pairs(value, mask):
    return lax.ppermute(value, "rep", [(i, i ^ mask) for i in range(4)])


def turned(rest, got):
    return plus(rest[0], got[0][1]), plus(rest[1], got[1][1])


def passed(values):
    return swap(values[0], ALONG_X), swap(values[1], ALONG_Y)


def sent(values):
    return swap(values[0], ALONG_Y), swap(values[1], ALONG_X)


def summed(own, got, late):
    odd = lax.axis_index("rep") % 2 == 1
    first, second = plus(own[0], got[0][0], late[0]), plus(own[1], got[1][0], late[1])
    return jnp.where(odd, second, first), jnp.where(odd, first, second)


def merge(meta, own, got, late, rest, got_next):
    rows, cols = own[0].shape
    high, wide = rest[0].shape
    steps = 2

    def kernel(meta, own_a, own_b, got_a, got_b, late_a, late_b, rest_a, rest_b, next_a, next_b, *outs):
        kept_ref, given_ref, pass_a, pass_b = outs
        first = own_a[...].astype(F32) + got_a[0].astype(F32) + late_a[...].astype(F32)
        second = own_b[...].astype(F32) + got_b[0].astype(F32) + late_b[...].astype(F32)
        odd = meta[7] == 1
        kept_ref[...] = jnp.where(odd, second, first).astype(BF16)
        given_ref[...] = jnp.where(odd, first, second).astype(BF16)
        pass_a[...] = (rest_a[...].astype(F32) + next_a[0].astype(F32)).astype(BF16)
        pass_b[...] = (rest_b[...].astype(F32) + next_b[0].astype(F32)).astype(BF16)

    flat = spec((rows // steps, cols), lambda i, meta: (i, 0))
    mine = spec((1, rows // steps, cols), lambda i, meta: (0, i, 0))
    low = spec((high // steps, wide), lambda i, meta: (i, 0))
    other = spec((1, high // steps, wide), lambda i, meta: (1, i, 0))
    kept, given, *passing = call(
        kernel,
        (steps,),
        [flat, flat, mine, mine, flat, flat, low, low, other, other],
        [flat, flat, low, low],
        [sds((rows, cols), BF16)] * 2 + [sds((high, wide), BF16)] * 2,
        [],
    )(meta, *own, *got, *late, *rest, *got_next)
    return kept, given, tuple(passing)


def unfolded(mine, other):
    odd = lax.axis_index("rep") % 2 == 1
    return jnp.where(odd, other, mine).astype(F32), jnp.where(odd, mine, other).astype(F32)


def local_eight(
    inputs, lengths, dealing, w_query, w_key, w_value, w_out, b_query, b_value, b_out,
    ln1_gain, ln1_bias, w_up, b_up, w_down, b_down, ln2_gain, ln2_bias, cotangent,
):
    batches, rows, width = inputs.shape
    wide = w_up.shape[1]
    total = batches * rows
    group = batches * 4
    shard_index = lax.axis_index("shard")
    anchor = shard_index * group
    slots = anchor + lax.axis_index("rep") * batches + jnp.arange(batches, dtype=jnp.int32)
    local_dealing = lax.dynamic_slice_in_dim(dealing, anchor, group) - anchor
    sources = jnp.take(dealing, slots) - anchor
    places = jnp.arange(group, dtype=jnp.int32)
    wanted = jnp.sum(
        jnp.where(local_dealing[None, :] == (slots - anchor)[:, None], places[None, :], 0), 1
    )
    meta = jnp.concatenate([shard_index[None].astype(jnp.int32), jnp.take(lengths, slots), wanted, jnp.clip(sources, 0, group - 1), (lax.axis_index("rep") % 2)[None].astype(jnp.int32)])
    order = Order(meta)
    tokens = inputs.reshape(total, width)

    small = (b_query, b_value, b_out, ln1_gain, ln1_bias, b_down, ln2_gain, ln2_bias, b_up)
    own_first = pack((w_query, w_key, w_value, w_out), small)
    first_x, first_y = swap(own_first, ALONG_X), swap(own_first, ALONG_Y)
    first_x, first_y, to_both = order.then((first_x, first_y, w_up))
    first_far, up_x = swap(first_x, ALONG_Y), swap(to_both, ALONG_X)
    first_c = [swap(part, CORE) for part in (own_first, first_x, first_y)]
    first_far, up_x, to_x, to_y, *first_c = order.then((first_far, up_x, w_down, w_up, *first_c))
    first = (own_first, first_x, first_y, first_far, *first_c, swap(first_far, CORE))
    up_y, down_x = swap(to_y, ALONG_Y), swap(to_x, ALONG_X)
    up_c = [swap(part, CORE) for part in (w_up, up_x)]
    cot_pool = lax.all_gather(cotangent, "rep", axis=0, tiled=True)
    qkv, vecs, bias_up, tokens_give = order.then(project(order.meta, tokens, first))
    mixed, raised, inverse = order.then(attend(order.meta, qkv, batches, rows))
    up_y, down_x, tokens_give, to_y, *up_c = order.then((up_y, down_x, tokens_give, w_down, *up_c))
    up_far, down_y = swap(up_y, ALONG_X), swap(to_y, ALONG_Y)
    up_c.append(swap(up_y, CORE))
    tokens_got = swap(tokens_give, CORE)
    unit_one, inverse_one, hidden_low, both_give = order.then(mix_out(order.meta, mixed, tokens, first, vecs))
    to_top = order.then(down_x[:256])
    up_far, down_y, tokens_got, both_give, to_top, *up_c = order.then((up_far, down_y, tokens_got, both_give, to_top, *up_c))
    up = (w_up, up_x, up_y, up_far, *up_c, swap(up_far, CORE))
    down_top, down_end = swap(to_top, ALONG_Y), swap(down_y[256:], ALONG_X)
    up, *to_core = order.then((up, w_down, down_x, down_y))
    down_c = [swap(part, CORE) for part in to_core]
    act, slope, act_give = order.then(feed_up(order.meta, hidden_low, up, bias_up))
    down_top, down_end, act_give, both_give, *down_c = order.then((down_top, down_end, act_give, both_give, *down_c))
    down = (w_down, down_x, down_y, down_top, down_end) + tuple(down_c)
    down += tuple(swap(part, CORE) for part in (down_top, down_end))
    *down, act_give, both_give = order.then((*down, act_give, both_give))
    act_got, both_got = swap(act_give, CORE), swap(both_give, CORE)
    out, grad_sum, sum_low, grads_two, pre, grad_bias_up = order.then(
        feed_down(order.meta, act, slope, down, unit_one, cot_pool, vecs, batches, rows)
    )
    sum_got = swap(sum_low, CORE)
    out, act_got, sum_got, pre = order.then((out, act_got, sum_got, pre))
    pre_got = swap(pre, CORE)
    out_pool = lax.all_gather(out.reshape(batches, rows, width), "rep", axis=0, tiled=True)
    far_down, own_down, rest_down = order.then(down_grad(order.meta, act, act_got, sum_low, sum_got))
    pre_got, both_got, far_down = order.then((pre_got, both_got, far_down))
    got_down = sent(far_down)
    grad_resid, resid_low, grad_mixed, grads_one = order.then(
        back_up(order.meta, pre, up, first, grad_sum, unit_one, inverse_one, vecs)
    )
    far_up, own_up, rest_up = order.then(up_grad(order.meta, hidden_low, both_got, pre, pre_got))
    got_down, far_up, resid_low = order.then((got_down, far_up, resid_low))
    got_up = sent(far_up)
    late_down = passed(order.then(turned(rest_down, got_down)))
    grads, vec = order.then(
        attend_back(
            order.meta, qkv, mixed, raised, inverse, grad_mixed, grads_one, grads_two, grad_bias_up, batches, rows
        )
    )
    grad_input = order.then(back_project(order.meta, grads, first, grad_resid))
    got_up, late_down, resid_low, grads, vec = order.then((got_up, late_down, resid_low, grads, vec))
    resid_got, grads_got, vec_got = swap(resid_low, CORE), swap(grads, CORE), swap(vec, CORE)
    kept_down, given_down, pass_up = order.then(
        merge(order.meta, own_down, got_down, late_down, rest_up, got_up)
    )
    resid_got, grads_got, vec_got, pass_up, given_down = order.then((resid_got, grads_got, vec_got, pass_up, given_down))
    late_up, taken_down = passed(pass_up), pairs(given_down, 1)
    (far_a, own_a, rest_a), (far_b, own_b, rest_b) = order.then(
        first_grad(
            order.meta, tokens, tokens_got, mixed, both_got, grads, grads_got, resid_low, resid_got, vec, vec_got
        )
    )
    late_up, taken_down, far_a, out_pool = order.then((late_up, taken_down, far_a, out_pool))
    got_a = sent(far_a)
    far_b, half_down = order.then((far_b, plus(kept_down, taken_down)))
    got_b = sent(far_b)
    over_down = pairs(half_down, 2)
    kept_up, given_up = order.then(summed(own_up, got_up, late_up))
    got_a = order.then(got_a)
    late_a = passed(order.then(turned(rest_a, got_a)))
    taken_up = pairs(given_up, 1)
    got_b = order.then(got_b)
    late_b = passed(order.then(turned(rest_b, got_b)))
    layer_out = order.then(chosen(order.meta, out_pool, 5))
    late_a = order.then(late_a)
    kept_a, given_a = order.then(summed(own_a, got_a, late_a))
    taken_a = pairs(given_a, 1)
    over_down, taken_up = order.then((over_down, taken_up))
    total_down, half_up = order.then((plus(half_down, over_down), plus(kept_up, taken_up)))
    late_b = order.then(late_b)
    kept_b, given_b = order.then(summed(own_b, got_b, late_b))
    taken_b = pairs(given_b, 1)
    taken_a = order.then(taken_a)
    half_a = order.then(plus(kept_a, taken_a))
    over_a = pairs(half_a, 2)
    over_up = pairs(half_up, 2)
    taken_b = order.then(taken_b)
    half_b = order.then(plus(kept_b, taken_b))
    over_b = pairs(half_b, 2)
    total_down = order.then(total_down)
    other_down = pairs(total_down, 1)
    over_a = order.then(over_a)
    total_a = order.then(plus(half_a, over_a))
    other_a = pairs(total_a, 1)
    over_up, other_down = order.then((over_up, other_down))
    total_up = order.then(plus(half_up, over_up))
    other_up = pairs(total_up, 1)
    g_down = order.then(jnp.concatenate(unfolded(total_down, other_down), 1))
    over_b = order.then(over_b)
    total_b = order.then(plus(half_b, over_b))
    other_b = pairs(total_b, 1)
    other_a, other_up = order.then((other_a, other_up))
    g_up = order.then(jnp.concatenate(unfolded(total_up, other_up), 1))
    g_a = order.then(jnp.concatenate(unfolded(total_a, other_a), 1))
    left, right = unfolded(total_b, other_b)
    g_b = jnp.concatenate([left[:256], right[:256]], 1)
    line = lambda i: left[256 + i, :128]
    return (
        layer_out, grad_input.reshape(batches, rows, width),
        g_a[0:128], g_a[128:256], g_b[0:128], g_b[128:256],
        line(0), line(1), line(2), line(3), line(4),
        g_up, left[264, :512], g_down, line(5), line(6), line(7),
    )


def pick(pool, targets):
    return jnp.stack(
        [lax.dynamic_index_in_dim(pool, targets[i], 0, keepdims=False) for i in range(targets.shape[0])]
    )


def local_general(
    inputs, lengths, dealing, w_query, w_key, w_value, w_out, b_query, b_value, b_out,
    ln1_gain, ln1_bias, w_up, b_up, w_down, b_down, ln2_gain, ln2_bias, cotangent,
):
    batches, rows, width = inputs.shape
    shards = lax.axis_size("shard")
    replicas = lax.axis_size("rep")
    group = batches * replicas
    shard_index = lax.axis_index("shard")
    rep_index = lax.axis_index("rep")
    anchor = shard_index * group
    slots = anchor + rep_index * batches + jnp.arange(batches, dtype=jnp.int32)
    seq_lengths = jnp.take(lengths, slots)
    local_dealing = lax.dynamic_slice_in_dim(dealing, anchor, group) - anchor
    sources = jnp.take(dealing, slots) - anchor
    places = jnp.arange(group, dtype=jnp.int32)
    wanted = jnp.sum(
        jnp.where(local_dealing[None, :] == (slots - anchor)[:, None], places[None, :], 0), 1
    )

    def gather(block):
        return lax.all_gather(block, "shard", axis=0, tiled=True)

    block = w_query.shape[0]
    wide = w_up.shape[1]
    small = (b_query, b_value, b_out, ln1_gain, ln1_bias, b_down, ln2_gain, ln2_bias, b_up)
    vec = jnp.concatenate(small)
    first = jnp.concatenate([w_query, w_key, w_value, w_out], 0)
    all_vec = lax.all_gather(vec, "shard", axis=0, tiled=True).reshape(shards, -1)
    all_first = gather(first).reshape(shards, 4, block, width)
    cuts = [0]
    for part in small:
        cuts.append(cuts[-1] + part.shape[0])
    (bias_query, bias_value, bias_out, gain_one, shift_one, bias_down, gain_two, shift_two, bias_up) = [
        all_vec[:, cuts[i] : cuts[i + 1]].reshape(-1).astype(F32) for i in range(len(small))
    ]
    full_query, full_key, full_value, full_out = [
        all_first[:, i].reshape(width, width) for i in range(4)
    ]
    full_up = gather(w_up)
    full_down = gather(w_down)
    cot = pick(lax.all_gather(cotangent, "rep", axis=0, tiled=True), wanted)

    tokens = inputs.reshape(batches * rows, width)
    query = (matmul(tokens, full_query) + bias_query).astype(BF16)
    keyed = matmul(tokens, full_key).astype(BF16)
    value = (matmul(tokens, full_value) + bias_value).astype(BF16)
    heads = lambda a: a.reshape(batches, rows, H, HD).transpose(0, 2, 1, 3)
    flat = lambda a: a.transpose(0, 2, 1, 3).reshape(batches * rows, width)
    qh, kh, vh = heads(query), heads(keyed), heads(value)
    allowed = lax.broadcasted_iota(jnp.int32, (batches, 1, 1, rows), 3) < seq_lengths[:, None, None, None]
    scale = HD ** (-0.5)
    scores = jnp.einsum("bhqd,bhkd->bhqk", qh, kh, preferred_element_type=F32) * scale
    scores = jnp.where(allowed, scores, NEG)
    raised = jnp.exp(scores - jnp.max(scores, -1, keepdims=True))
    probs = raised / jnp.sum(raised, -1, keepdims=True)
    probs_low = probs.astype(BF16)
    mixed_low = flat(jnp.einsum("bhqk,bhkd->bhqd", probs_low, vh, preferred_element_type=F32).astype(BF16))
    hidden, unit_one, inverse_one = normalize(
        tokens.astype(F32) + matmul(mixed_low, full_out) + bias_out, gain_one, shift_one
    )
    hidden_low = hidden.astype(BF16)
    pre = matmul(hidden_low, full_up) + bias_up
    act, slope = gelu_both(pre)
    act_low = act.astype(BF16)
    summed = hidden + matmul(act_low, full_down) + bias_down
    normed, unit_two, inverse_two = normalize(summed, gain_two, shift_two)
    valid = (lax.broadcasted_iota(jnp.int32, (batches, rows, 1), 1) < seq_lengths[:, None, None]).reshape(-1, 1)
    out = jnp.where(valid, normed, 0.0).astype(BF16).reshape(batches, rows, width)
    layer_out = pick(lax.all_gather(out, "rep", axis=0, tiled=True), sources)

    grad_out = jnp.where(valid, cot.reshape(-1, width).astype(F32), 0.0)
    grad_gain_two = jnp.sum(grad_out * unit_two, 0)
    grad_shift_two = jnp.sum(grad_out, 0)
    grad_sum = norm_back(grad_out, unit_two, inverse_two, gain_two)
    grad_bias_down = jnp.sum(grad_sum, 0)
    grad_sum_low = grad_sum.astype(BF16)

    def reduced(part):
        return lax.psum_scatter(part, "shard", scatter_dimension=0, tiled=True)

    def over_rep(part):
        return lax.psum(part, "rep").astype(F32)

    g_down = reduced(left_trans(act_low, grad_sum_low).astype(BF16))
    grad_pre = (right_trans(grad_sum_low, full_down) * slope).astype(BF16)
    grad_bias_up = jnp.sum(grad_pre.astype(F32), 0)
    g_up = reduced(left_trans(hidden_low, grad_pre).astype(BF16))
    grad_hidden = grad_sum + right_trans(grad_pre, full_up)
    grad_gain_one = jnp.sum(grad_hidden * unit_one, 0)
    grad_shift_one = jnp.sum(grad_hidden, 0)
    grad_resid = norm_back(grad_hidden, unit_one, inverse_one, gain_one)
    grad_bias_out = jnp.sum(grad_resid, 0)
    grad_resid_low = grad_resid.astype(BF16)
    grad_w_out = left_trans(mixed_low, grad_resid_low).astype(BF16)
    grad_mixed = heads(right_trans(grad_resid_low, full_out).astype(BF16))
    grad_probs = jnp.einsum("bhqd,bhkd->bhqk", grad_mixed, vh, preferred_element_type=F32)
    inner = jnp.sum(probs * grad_probs, -1, keepdims=True)
    grad_scores = (probs * (grad_probs - inner) * scale).astype(BF16)
    query_low = flat(jnp.einsum("bhqk,bhkd->bhqd", grad_scores, kh, preferred_element_type=F32).astype(BF16))
    key_low = flat(jnp.einsum("bhqk,bhqd->bhkd", grad_scores, qh, preferred_element_type=F32).astype(BF16))
    value_low = flat(jnp.einsum("bhqk,bhqd->bhkd", probs_low, grad_mixed, preferred_element_type=F32).astype(BF16))
    grad_bias_query = jnp.sum(query_low.astype(F32), 0)
    grad_bias_value = jnp.sum(value_low.astype(F32), 0)
    blocks = [
        part.reshape(shards, block, width)
        for part in (
            left_trans(tokens, query_low).astype(BF16),
            left_trans(tokens, key_low).astype(BF16),
            left_trans(tokens, value_low).astype(BF16),
            grad_w_out,
        )
    ]
    g_first = reduced(jnp.concatenate(blocks, 1).reshape(shards * 4 * block, width))
    grad_tokens = (
        grad_resid
        + right_trans(query_low, full_query)
        + right_trans(key_low, full_key)
        + right_trans(value_low, full_value)
    )
    grad_input = grad_tokens.astype(BF16).reshape(batches, rows, width)
    vec_terms = (
        grad_bias_query, grad_bias_value, grad_bias_out, grad_gain_one, grad_shift_one,
        grad_bias_down, grad_gain_two, grad_shift_two, grad_bias_up,
    )
    g_vec = jnp.concatenate([part.reshape(shards, -1) for part in vec_terms], 1)
    g_vec = lax.psum(g_vec, ("shard", "rep"))
    g_vec = lax.dynamic_index_in_dim(g_vec, shard_index, 0, keepdims=False)
    (g_bquery, g_bvalue, g_bout, g_gain_one, g_shift_one, g_bdown, g_gain_two, g_shift_two, g_bup) = [
        g_vec[cuts[i] : cuts[i + 1]] for i in range(len(small))
    ]
    g_down = over_rep(g_down)
    g_up = over_rep(g_up)
    g_first = over_rep(g_first).reshape(4, block, width)
    return (
        layer_out, grad_input, g_first[0], g_first[1], g_first[2], g_first[3],
        g_bquery, g_bvalue, g_bout, g_gain_one, g_shift_one,
        g_up, g_bup, g_down, g_bdown, g_gain_two, g_shift_two,
    )


def solution(mesh):
    seqs = P(("shard", "rep"), None, None)
    mat = P("shard", None)
    vec = P("shard")
    in_specs = (
        seqs, P(), P(), mat, mat, mat, mat, vec, vec, vec, vec, vec, mat, vec, mat, vec, vec, vec, seqs,
    )
    out_specs = (
        seqs, seqs, mat, mat, mat, mat, vec, vec, vec, vec, vec, mat, vec, mat, vec, vec, vec,
    )
    shape = dict(mesh.shape)
    local = local_eight if shape["shard"] == 8 and shape["rep"] == 4 else local_general
    return jax.shard_map(local, mesh=mesh, in_specs=in_specs, out_specs=out_specs, check_vma=False)
```
